128 devices in a mesh: row: 16 (over z, y_hi, core), col: 8 (over y_lo, x).
Axes of the slice: x: 4, y: 4 (y_hi: 2, y_lo: 2; y = y_hi * 2 + y_lo), z: 4, core: 2. Of those that a mesh axis runs over, the one named last changes fastest.
Arguments:
- queries: bfloat16 [3072, 3072], P('row', 'col'), may hold values from -24 to 24
- keys_tile: bfloat16 [3072, 3072], P('row', 'col'), may hold values from -4.5 to 4.5
- values_tile: bfloat16 [3072, 3072], P('row', 'col'), may hold values from -6 to 6
- out_weight: bfloat16 [3072, 6144], P('row', 'col'), may hold values from -0.75 to 0.75
- out_grad: bfloat16 [3072, 6144], P('row', 'col'), may hold values from -1.5 to 1.5
Outputs:
- mixed: bfloat16 [3072, 6144], P('row', 'col')
- query_grad: bfloat16 [3072, 3072], P('row', 'col')
- key_grad: bfloat16 [3072, 3072], P('row', 'col')
- value_grad: bfloat16 [3072, 3072], P('row', 'col')
- weight_grad: bfloat16 [3072, 6144], P('row', 'col')
The draws below stay inside these ranges and needn't reach their ends.
All inputs are finite; a program needn't handle non-finite values.
Results may differ from the reference program's by a relative error of at most 0.019.
Values may be sent and summed in bfloat16 or wider, within the bound.
A program may use at most 128 MiB of HBM per device.

```python
import jax
import jax.numpy as jnp
from jax import lax

D = 6144
HEADS = 24
HD = 128
TOKENS = 3072


def draw_pair(key):
    query_key = jax.random.fold_in(key, 101)
    key_key = jax.random.fold_in(key, 202)
    width = HEADS * HD
    keys_f = jnp.clip(jax.random.normal(key_key, (TOKENS, width), jnp.float32), -4.0, 4.0)
    queries_f = jnp.clip(2.0 * jax.random.normal(query_key, (TOKENS, width), jnp.float32), -8.0, 8.0)
    return (queries_f, keys_f)


def draw_queries(key, part):
    return draw_pair(key)[0].astype(jnp.bfloat16)


def draw_keys_tile(key, part):
    return draw_pair(key)[1].astype(jnp.bfloat16)


def block_levels(own_key, extent, pieces, least, top_value):
    gain, own = 1.0, jax.random.fold_in(own_key, 6)
    for position, parts in pieces:
        draws = jnp.exp(jax.random.uniform(jax.random.fold_in(own, position), (parts,), jnp.float32, least / len(pieces), top_value / len(pieces)))
        gain = gain * jnp.repeat(draws, extent[position] // parts).reshape([-1 if axis == position else 1 for axis in range(len(extent))])
    return gain


def centred(key, extent, deviation, limit, split=(), dtype=jnp.bfloat16):
    array = jax.random.normal(key, extent, jnp.float32) * deviation
    if len(split) > 0:
        array = block_levels(key, extent, split, -0.22, 0.18) * array
    return jnp.clip(array, min=-limit, max=limit).astype(dtype)


def setup_inputs(seed: int = 0) -> dict:
    key_of = jax.random.split(jax.random.key(seed), 6)
    queries = draw_queries(jax.random.fold_in(key_of[5], 71), 0)
    keys_tile = draw_keys_tile(jax.random.fold_in(key_of[5], 71), 0)
    values_tile = centred(key_of[2], (TOKENS, HEADS * HD), 1.0, 6.0, ((0, 16), (1, 8)))
    out_weight = centred(key_of[3], (HEADS * HD, D), (HD // 2) ** -0.5, 0.75, ((0, 16), (1, 8)))
    out_grad = centred(key_of[4], (TOKENS, D), 0.25, 1.5, ((0, 16), (1, 8)))
    return dict(queries=queries, keys_tile=keys_tile, values_tile=values_tile, out_weight=out_weight, out_grad=out_grad)


def head_forward(args):
    query_head, key_head, value_head = args
    scores = jnp.einsum("qd,kd->qk", query_head.astype(jnp.float32), key_head.astype(jnp.float32)) * (HD ** -0.5)
    top = jnp.max(scores, axis=1, keepdims=True)
    lse = top[:, 0] + jnp.log(jnp.sum(jnp.exp(scores - top), axis=1))
    probs = jnp.exp(scores - lse[:, None]).astype(jnp.bfloat16)
    attn = jnp.dot(probs, value_head, preferred_element_type=jnp.float32).astype(jnp.bfloat16)
    return attn, lse


def head_backward(args):
    query_head, key_head, value_head, grad_head, attn_head, lse = args
    delta = jnp.sum(grad_head.astype(jnp.float32) * attn_head.astype(jnp.float32), axis=1)
    scores = jnp.einsum("qd,kd->qk", query_head.astype(jnp.float32), key_head.astype(jnp.float32)) * (HD ** -0.5)
    probs = jnp.exp(scores - lse[:, None]).astype(jnp.bfloat16)
    dprob = jnp.einsum("qd,kd->qk", grad_head.astype(jnp.float32), value_head.astype(jnp.float32))
    dscore = (probs.astype(jnp.float32) * (dprob - delta[:, None]) * (HD ** -0.5)).astype(jnp.bfloat16)
    query_grad = jnp.dot(dscore, key_head, preferred_element_type=jnp.float32).astype(jnp.bfloat16)
    key_grad = jnp.dot(dscore.T, query_head, preferred_element_type=jnp.float32).astype(jnp.bfloat16)
    value_grad = jnp.dot(probs.T, grad_head, preferred_element_type=jnp.float32).astype(jnp.bfloat16)
    return query_grad, key_grad, value_grad


def split_heads(block):
    return block.reshape(block.shape[0], HEADS, HD).transpose(1, 0, 2)


def merge_heads(block):
    return block.transpose(1, 0, 2).reshape(block.shape[1], HEADS * HD)


def reference(queries, keys_tile, values_tile, out_weight, out_grad):
    query3 = split_heads(queries)
    key3 = split_heads(keys_tile)
    value3 = split_heads(values_tile)
    attn3, lse = lax.map(head_forward, (query3, key3, value3))
    attn = merge_heads(attn3)
    mixed = jnp.dot(attn, out_weight, preferred_element_type=jnp.float32).astype(jnp.bfloat16)
    d_attn = jnp.dot(out_grad, out_weight.T, preferred_element_type=jnp.float32).astype(jnp.bfloat16)
    weight_grad = jnp.dot(attn.T, out_grad, preferred_element_type=jnp.float32).astype(jnp.bfloat16)
    grad3 = split_heads(d_attn)
    query_g, key_g, value_g = lax.map(head_backward, (query3, key3, value3, grad3, attn3, lse))
    return mixed, merge_heads(query_g), merge_heads(key_g), merge_heads(value_g), weight_grad
```

```python
import jax
import jax.numpy as jnp
from jax import lax
from jax.experimental import pallas as pl
from jax.experimental.pallas import tpu as pltpu
from jax.sharding import PartitionSpec as P

HD = 128
NH = 3
TB = 192
ZT = 4 * TB
HC = NH * HD
DC = 768
PB = HC // 4
QT = 256
SCALE = HD ** (-0.5)
LOG2E = 1.4426950408889634
MESH = pl.DeviceIdType.MESH
F32 = jnp.float32
BF16 = jnp.bfloat16


def dot(a, b, ca, cb):
    return lax.dot_general(a, b, (((ca,), (cb,)), ((), ())), preferred_element_type=F32)


def kernel(
    q_ref, k_ref, v_ref, w_ref, g_ref,
    mixed_o, dq_o, dk_o, dv_o, wg_o,
    k_all, v_all, q_all, w_all, g_all, kt, vt,
    o_st, o_rc, lse_all, lse_c, wgt, attn_own, attn_all,
    d_st, d_rc, do_all, dp_all, delta,
    kacc, vacc, k_st, v_st, q_st, k_rc, v_rc, q_rc,
    m_st, m_rc, w_st, w_rc,
    sz, rz, sy, ry, sd, rd, sa, ra, sk, rk,
):
    row, col = lax.axis_index("row"), lax.axis_index("col")
    z, q = row // 4, row % 4
    yh, co = q // 2, q % 2
    own = jnp.where((col % 2 == yh) & (co == yh), 1, 0)

    def ypeer(j):
        a = yh if j < 2 else 1 - yh
        b = co if j % 2 == 0 else 1 - co
        return a * 2 + b

    def zpeer(d):
        return (z + d) % 4

    def send(src, dst, ss, rs, r, c):
        d = pltpu.make_async_remote_copy(
            src_ref=src, dst_ref=dst, send_sem=ss, recv_sem=rs, device_id=(r, c), device_id_type=MESH
        )
        d.start()
        return d

    def recv(dst, ss, rs):
        pltpu.make_async_remote_copy(
            src_ref=dst, dst_ref=dst, send_sem=ss, recv_sem=rs, device_id=(row, col), device_id_type=MESH
        ).wait_recv()

    def rows(i, n):
        return pl.ds(pl.multiple_of(i * n, n), n)

    barrier = pltpu.get_barrier_semaphore()

    def greet(r, c):
        pl.semaphore_signal(barrier, inc=1, device_id=(r, c), device_id_type=MESH)

    arow = z * 4 + (col % 2) * 2 + yh
    for d in (1, 2, 3):
        greet(zpeer(d) * 4 + q, col)
        greet(z * 4 + ypeer(d), col)
    for k in range(8):
        if k == 0:
            @pl.when(own == 0)
            def _():
                greet(arow, col)
        else:
            greet(arow, (col + k) % 8)
    for k in range(4):
        for m in range(2):
            tr, tc = z * 4 + co * 2 + (co + m) % 2, 2 * ((col // 2 + k) % 4) + yh
            if k == 0 and m == 0:
                @pl.when(own == 0)
                def _():
                    greet(tr, tc)
            else:
                greet(tr, tc)
    pl.semaphore_wait(barrier, 22 - 2 * own)

    sends = []

    def to_z(i, src, dst):
        for d in (1, 3, 2):
            sends.append(send(src, dst, sz.at[i, d - 1], rz.at[i, d - 1], zpeer(d) * 4 + q, col))

    def to_y(i, src, dst):
        for j in (2, 3, 1):
            sends.append(send(src, dst, sy.at[i, j - 1], ry.at[i, j - 1], z * 4 + ypeer(j), col))

    to_z(0, k_ref, k_all.at[rows(z, TB), :])
    to_y(0, q_ref, q_all.at[rows(q, TB), :])
    to_z(1, v_ref, v_all.at[rows(z, TB), :])
    to_y(1, g_ref, g_all.at[rows(q, TB), :])
    to_z(2, w_ref, w_all.at[rows(z, TB), :])
    k_all[rows(z, TB), :] = k_ref[...]
    v_all[rows(z, TB), :] = v_ref[...]
    w_all[rows(z, TB), :] = w_ref[...]
    q_all[rows(q, TB), :] = q_ref[...]
    g_all[rows(q, TB), :] = g_ref[...]
    lse_all[q] = jnp.zeros((8, ZT), F32)
    dp_all[q] = jnp.zeros((8, ZT), F32)

    for j in (1, 2, 3):
        recv(q_all.at[rows(ypeer(j), TB), :], sy.at[0, j - 1], ry.at[0, j - 1])
    for d in (1, 3, 2):
        recv(k_all.at[rows((z + 4 - d) % 4, TB), :], sz.at[0, d - 1], rz.at[0, d - 1])
    kt[...] = k_all[...].T
    for d in (1, 3, 2):
        recv(v_all.at[rows((z + 4 - d) % 4, TB), :], sz.at[1, d - 1], rz.at[1, d - 1])
    vt[...] = v_all[...].T

    def forward(i, carry):
        h, t = i // 3, i % 3
        hs, ts = rows(h, HD), rows(t, QT)
        s = dot(k_all[:, hs], q_all[ts, hs], 1, 1)
        top = jnp.max(s, axis=0, keepdims=True)
        p = jnp.exp2((s - top) * (SCALE * LOG2E))
        total = jnp.sum(p, axis=0, keepdims=True)
        o = dot(vt[hs, :], p.astype(BF16), 1, 0)
        o_st[hs, ts] = (o / total).astype(BF16)
        lse_all[q, pl.ds(h, 1), ts] = top * (SCALE * LOG2E) + jnp.log2(total)
        return carry

    lax.fori_loop(0, 9, forward, 0)

    for j in (2, 3, 1):
        p = ypeer(j)
        sends.append(send(lse_all.at[q], lse_all.at[q], sy.at[3, j - 1], ry.at[3, j - 1], z * 4 + p, col))
        sends.append(send(o_st.at[rows(p, PB), :], o_rc.at[q], sy.at[2, j - 1], ry.at[2, j - 1], z * 4 + p, col))
    o_rc[q] = o_st[rows(q, PB), :]

    for j in (1, 2, 3):
        recv(g_all.at[rows(ypeer(j), TB), :], sy.at[1, j - 1], ry.at[1, j - 1])
    for d in (1, 3, 2):
        recv(w_all.at[rows((z + 4 - d) % 4, TB), :], sz.at[2, d - 1], rz.at[2, d - 1])
    for k in range(4):
        zp = (col // 2 + k) % 4
        part = dot(w_all[rows(zp, TB), :], g_all[...], 1, 1).astype(BF16)
        d_st[2 * k] = part[:PB]
        d_st[2 * k + 1] = part[PB:]
        for m in range(2):
            half = (co + m) % 2
            tr, tc = z * 4 + co * 2 + half, 2 * zp + yh
            src = d_st.at[2 * k + half]
            if k == 0 and m == 0:
                @pl.when(own == 0)
                def _():
                    send(src, d_rc.at[col], sd.at[0], rd.at[col], tr, tc)

                @pl.when(own == 1)
                def _():
                    d_rc[col] = d_st[half]
            else:
                sends.append(send(src, d_rc.at[col], sd.at[2 * k + m], rd.at[col], tr, tc))

    for j in (1, 2, 3):
        p = ypeer(j)
        recv(lse_all.at[p], sy.at[3, j - 1], ry.at[3, j - 1])
        recv(o_rc.at[p], sy.at[2, j - 1], ry.at[2, j - 1])
    ls = [lse_all[j] for j in range(4)]
    top = jnp.maximum(jnp.maximum(ls[0], ls[1]), jnp.maximum(ls[2], ls[3]))
    lse = top + jnp.log2(sum(jnp.exp2(x - top) for x in ls))
    lse_c[...] = lse
    for j in range(4):
        wgt[j] = jnp.exp2(ls[j] - lse)
    for i in range(3):
        head = (3 * q + i) // 4
        part = slice(i * 32, (i + 1) * 32)
        attn_own[part, :] = sum(
            wgt[j, pl.ds(head, 1), :] * o_rc[j, part, :].astype(F32) for j in range(4)
        ).astype(BF16)
    slot = (col // 2) * 2 + co
    for k in (1, 2, 3, 4, 5, 6, 7):
        sends.append(send(attn_own, attn_all.at[rows(slot, PB), :], sa.at[k], ra.at[slot], arow, (col + k) % 8))

    @pl.when(own == 0)
    def _():
        send(attn_own, attn_all.at[rows(slot, PB), :], sa.at[0], ra.at[slot], arow, col)

    @pl.when(own == 1)
    def _():
        attn_all[rows(slot, PB), :] = attn_own[...]

    for k in range(8):
        src = (col + k) % 8
        if k == 0:
            @pl.when(own == 0)
            def _():
                recv(d_rc.at[src], sd.at[0], rd.at[src])
        else:
            recv(d_rc.at[src], sd.at[0], rd.at[src])
    for i in range(3):
        head = (3 * q + i) // 4
        part = slice(i * 32, (i + 1) * 32)
        do = sum(d_rc[k, part, :].astype(F32) for k in range(8)).astype(BF16)
        do_all[pl.ds(pl.multiple_of(q * PB + i * 32, 32), 32), :] = do
        dp_all[q, pl.ds(head, 1), :] += jnp.sum(
            do.astype(F32) * attn_own[part, :].astype(F32), axis=0, keepdims=True
        )
    for j in (2, 3, 1):
        r = z * 4 + ypeer(j)
        sends.append(send(dp_all.at[q], dp_all.at[q], sy.at[5, j - 1], ry.at[5, j - 1], r, col))
        sends.append(
            send(do_all.at[rows(q, PB), :], do_all.at[rows(q, PB), :], sy.at[4, j - 1], ry.at[4, j - 1], r, col)
        )

    for k in range(4):
        for m in range(2):
            src = 2 * ((col // 2 + k) % 4) + (co + m) % 2
            if k == 0 and m == 0:
                @pl.when(own == 0)
                def _():
                    recv(attn_all.at[rows(src, PB), :], sa.at[0], ra.at[src])
            else:
                recv(attn_all.at[rows(src, PB), :], sa.at[0], ra.at[src])

    def weight_part(i, carry):
        w_st[rows(i, TB), :] = dot(attn_all[rows(i, TB), :], g_all[...], 1, 0).astype(BF16)
        return carry

    lax.fori_loop(0, 4, weight_part, 0)
    for d in (1, 3, 2):
        sends.append(
            send(w_st.at[rows(zpeer(d), TB), :], w_rc.at[z], sz.at[3, d - 1], rz.at[3, d - 1], zpeer(d) * 4 + q, col)
        )
    w_rc[z] = w_st[rows(z, TB), :]

    def mixed_part(i, carry):
        m_st[rows(i, QT), :] = dot(attn_all[:, rows(i, QT)], w_all[...], 0, 0).astype(BF16)
        return carry

    lax.fori_loop(0, 3, mixed_part, 0)
    for j in (2, 3, 1):
        p = ypeer(j)
        sends.append(
            send(m_st.at[rows(p, TB), :], m_rc.at[q], sy.at[6, j - 1], ry.at[6, j - 1], z * 4 + p, col)
        )
    m_rc[q] = m_st[rows(q, TB), :]

    for j in (1, 2, 3):
        p = ypeer(j)
        recv(dp_all.at[p], sy.at[5, j - 1], ry.at[5, j - 1])
        recv(do_all.at[rows(p, PB), :], sy.at[4, j - 1], ry.at[4, j - 1])
    delta[...] = dp_all[0] + dp_all[1] + dp_all[2] + dp_all[3]

    def backward(h, carry):
        hs = rows(h, HD)
        kh = k_all[:, hs]
        vh = v_all[:, hs]
        for t in range(3):
            ts = slice(t * QT, (t + 1) * QT)
            qh = q_all[ts, hs]
            doh = do_all[hs, ts]
            s = dot(kh, qh, 1, 1)
            p = jnp.exp2(s * (SCALE * LOG2E) - lse_c[pl.ds(h, 1), ts]).astype(BF16)
            dprob = dot(vh, doh, 1, 0)
            ds = (p.astype(F32) * (dprob - delta[pl.ds(h, 1), ts]) * SCALE).astype(BF16)
            dvt = dot(p, doh, 1, 1)
            dkt = dot(ds, qh, 1, 0)
            if t == 0:
                vacc[...] = dvt
                kacc[...] = dkt
            else:
                vacc[...] += dvt
                kacc[...] += dkt
            q_st[ts, hs] = dot(kt[hs, :], ds, 1, 0).T.astype(BF16)
        v_st[:, hs] = vacc[...].astype(BF16)
        k_st[:, hs] = kacc[...].astype(BF16)
        for d in (1, 3, 2):
            r = zpeer(d) * 4 + q
            pr = rows(zpeer(d), TB)
            send(v_st.at[pr, hs], v_rc.at[z, :, hs], sk.at[0, h, d - 1], rk.at[0, h, d - 1], r, col)
            send(k_st.at[pr, hs], k_rc.at[z, :, hs], sk.at[1, h, d - 1], rk.at[1, h, d - 1], r, col)
        for j in (2, 3, 1):
            p = ypeer(j)
            send(
                q_st.at[rows(p, TB), hs], q_rc.at[q, :, hs], sk.at[2, h, j - 1], rk.at[2, h, j - 1], z * 4 + p, col
            )
        return carry

    lax.fori_loop(0, NH, backward, 0)
    v_rc[z] = v_st[rows(z, TB), :]
    k_rc[z] = k_st[rows(z, TB), :]
    q_rc[q] = q_st[rows(q, TB), :]

    for j in (1, 2, 3):
        recv(m_rc.at[ypeer(j)], sy.at[6, j - 1], ry.at[6, j - 1])
    mixed_o[...] = sum(m_rc[j].astype(F32) for j in range(4)).astype(BF16)
    for d in (1, 3, 2):
        recv(w_rc.at[(z + 4 - d) % 4], sz.at[3, d - 1], rz.at[3, d - 1])
    wg_o[...] = sum(w_rc[j].astype(F32) for j in range(4)).astype(BF16)
    for h in range(NH):
        hs = slice(h * HD, (h + 1) * HD)
        for j in (1, 2, 3):
            recv(q_rc.at[ypeer(j), :, hs], sk.at[2, h, j - 1], rk.at[2, h, j - 1])
        dq_o[:, hs] = sum(q_rc[j, :, hs].astype(F32) for j in range(4)).astype(BF16)
        for d in (1, 3, 2):
            src = (z + 4 - d) % 4
            recv(v_rc.at[src, :, hs], sk.at[0, h, d - 1], rk.at[0, h, d - 1])
            recv(k_rc.at[src, :, hs], sk.at[1, h, d - 1], rk.at[1, h, d - 1])
        dv_o[:, hs] = sum(v_rc[j, :, hs].astype(F32) for j in range(4)).astype(BF16)
        dk_o[:, hs] = sum(k_rc[j, :, hs].astype(F32) for j in range(4)).astype(BF16)

    def left(src, ss, rs):
        pltpu.make_async_remote_copy(
            src_ref=src, dst_ref=src, send_sem=ss, recv_sem=rs, device_id=(row, col), device_id_type=MESH
        ).wait_send()

    for d in sends:
        d.wait_send()

    @pl.when(own == 0)
    def _():
        left(d_st.at[0], sd.at[0], rd.at[0])
        left(attn_own, sa.at[0], ra.at[0])

    for h in range(NH):
        hs = slice(h * HD, (h + 1) * HD)
        for j in range(3):
            left(v_rc.at[0, :, hs], sk.at[0, h, j], rk.at[0, h, j])
            left(k_rc.at[0, :, hs], sk.at[1, h, j], rk.at[1, h, j])
            left(q_rc.at[0, :, hs], sk.at[2, h, j], rk.at[2, h, j])


def per_device(queries, keys_tile, values_tile, out_weight, out_grad):
    def vm(shape, dtype=BF16):
        return pltpu.VMEM(shape, dtype)

    dma = pltpu.SemaphoreType.DMA
    spec = pl.BlockSpec(memory_space=pltpu.VMEM)
    return pl.pallas_call(
        kernel,
        out_shape=(
            jax.ShapeDtypeStruct((TB, DC), BF16),
            jax.ShapeDtypeStruct((TB, HC), BF16),
            jax.ShapeDtypeStruct((TB, HC), BF16),
            jax.ShapeDtypeStruct((TB, HC), BF16),
            jax.ShapeDtypeStruct((TB, DC), BF16),
        ),
        in_specs=[spec] * 5,
        out_specs=(spec,) * 5,
        scratch_shapes=[
            vm((ZT, HC)), vm((ZT, HC)), vm((ZT, HC)), vm((ZT, DC)), vm((ZT, DC)), vm((HC, ZT)), vm((HC, ZT)),
            vm((HC, ZT)), vm((4, PB, ZT)), vm((4, 8, ZT), F32), vm((8, ZT), F32), vm((4, 8, ZT), F32),
            vm((PB, ZT)), vm((8 * PB, ZT)),
            vm((8, PB, ZT)), vm((8, PB, ZT)), vm((HC, ZT)), vm((4, 8, ZT), F32), vm((8, ZT), F32),
            vm((ZT, HD), F32), vm((ZT, HD), F32), vm((ZT, HC)), vm((ZT, HC)), vm((ZT, HC)),
            vm((4, TB, HC)), vm((4, TB, HC)), vm((4, TB, HC)),
            vm((ZT, DC)), vm((4, TB, DC)), vm((ZT, DC)), vm((4, TB, DC)),
            dma((4, 3)), dma((4, 3)), dma((7, 3)), dma((7, 3)), dma((8,)), dma((8,)), dma((8,)), dma((8,)),
            dma((3, 3, 3)), dma((3, 3, 3)),
        ],
        compiler_params=pltpu.CompilerParams(
            collective_id=0, has_side_effects=True, vmem_limit_bytes=60 * 1024 * 1024
        ),
    )(queries, keys_tile, values_tile, out_weight, out_grad)


def solution(mesh):
    spec = P("row", "col")
    return jax.shard_map(
        per_device, mesh=mesh, in_specs=(spec,) * 5, out_specs=(spec,) * 5, check_vma=False
    )
```

```python
import jax
import jax.numpy as jnp
from jax import lax
from jax.experimental import pallas as pl
from jax.experimental.pallas import tpu as pltpu
from jax.sharding import PartitionSpec as P

HD = 128
NH = 3
TB = 192
ZT = 4 * TB
HC = NH * HD
DC = 768
QT = 256
SCALE = HD ** (-0.5)
LOG2E = 1.4426950408889634
MESH = pl.DeviceIdType.MESH
F32 = jnp.float32
BF16 = jnp.bfloat16


def dot(a, b, ca, cb):
    return lax.dot_general(a, b, (((ca,), (cb,)), ((), ())), preferred_element_type=F32)


def kernel(
    q_ref, k_ref, v_ref, w_ref, g_ref,
    mixed_o, dq_o, dk_o, dv_o, wg_o,
    k_all, v_all, q_all, w_all, g_all, kt, vt,
    o_st, o_core, o_chip, o_rc, lse_own, lse_core, lse_chip, lse_far, lse_c, attn_all,
    d_st, d_rc, d_up, d_yl, do_all, dp_all, delta,
    kacc, vacc, k_st, v_st, q_st, k_rc, v_rc, q_core, q_up, q_rc,
    m_st, m_core, m_up, m_rc, w_st, w_rc,
    sz, rz, sy, ry, sd, rd, sa, ra, sb, rb, sk, rk,
):
    row, col = lax.axis_index("row"), lax.axis_index("col")
    z, q = row // 4, row % 4
    yh, co = q // 2, q % 2
    yl, x = col // 4, col % 4
    inner = x % 2 == yh
    outer = x % 2 != yh

    def ypeer(j):
        a = yh if j < 2 else 1 - yh
        b = co if j % 2 == 0 else 1 - co
        return a * 2 + b

    def zpeer(d):
        return (z + d) % 4

    def xpeer(d):
        return yl * 4 + (x + d) % 4

    other_yl = (1 - yl) * 4 + x

    def copy(src, dst, ss, rs, r, c):
        return pltpu.make_async_remote_copy(
            src_ref=src, dst_ref=dst, send_sem=ss, recv_sem=rs, device_id=(r, c), device_id_type=MESH
        )

    def send(src, dst, ss, rs, r, c):
        d = copy(src, dst, ss, rs, r, c)
        d.start()
        return d

    def recv(dst, ss, rs):
        copy(dst, dst, ss, rs, row, col).wait_recv()

    def left(src, ss, rs):
        copy(src, src, ss, rs, row, col).wait_send()

    def rows(i, n):
        return pl.ds(pl.multiple_of(i * n, n), n)

    barrier = pltpu.get_barrier_semaphore()

    def greet(r, c):
        pl.semaphore_signal(barrier, inc=1, device_id=(r, c), device_id_type=MESH)

    for d in (1, 2, 3):
        greet(zpeer(d) * 4 + q, col)
        greet(row, xpeer(d))
    greet(z * 4 + ypeer(1), col)
    greet(z * 4 + ypeer(2), col)
    greet(row, other_yl)
    pl.semaphore_wait(barrier, 9)

    core = z * 4 + ypeer(1)
    far = z * 4 + ypeer(2)
    sends = []

    def to_z(i, src, dst):
        for d in (1, 3, 2):
            sends.append(send(src, dst, sz.at[i, d - 1], rz.at[i, d - 1], zpeer(d) * 4 + q, col))

    def from_z(i, d, dst):
        recv(dst, sz.at[i, d - 1], rz.at[i, d - 1])

    def to_y(i, j, src, dst):
        sends.append(send(src, dst, sy.at[i, j - 1], ry.at[i, j - 1], far if j == 2 else core, col))

    def from_y(i, j, dst):
        recv(dst, sy.at[i, j - 1], ry.at[i, j - 1])

    to_y(1, 2, g_ref, g_all.at[rows(q, TB), :])
    to_z(2, w_ref, w_all.at[rows(z, TB), :])
    to_y(1, 1, g_ref, g_all.at[rows(q, TB), :])
    to_y(0, 2, q_ref, q_all.at[rows(q, TB), :])
    to_z(0, k_ref, k_all.at[rows(z, TB), :])
    to_y(0, 1, q_ref, q_all.at[rows(q, TB), :])
    to_z(1, v_ref, v_all.at[rows(z, TB), :])
    g_all[rows(q, TB), :] = g_ref[...]
    w_all[rows(z, TB), :] = w_ref[...]
    q_all[rows(q, TB), :] = q_ref[...]
    k_all[rows(z, TB), :] = k_ref[...]
    v_all[rows(z, TB), :] = v_ref[...]
    lse_own[...] = jnp.zeros_like(lse_own)
    dp_all[co] = jnp.zeros((8, ZT), F32)

    part_far = rows(ypeer(2), TB)
    from_y(1, 2, g_all.at[part_far, :])
    to_y(1, 3, g_all.at[part_far, :], g_all.at[part_far, :])
    from_y(0, 2, q_all.at[part_far, :])
    to_y(0, 3, q_all.at[part_far, :], q_all.at[part_far, :])
    for j in (1, 3):
        from_y(1, j, g_all.at[rows(ypeer(j), TB), :])

    slot_a, slot_b = 2 * yl + x // 2, 2 * (1 - yl) + x // 2
    for d in (0, 1, 3, 2):
        zp = (z + 4 - d) % 4
        if d > 0:
            from_z(2, d, w_all.at[rows(zp, TB), :])
        d_st[zp] = dot(w_all[rows(zp, TB), :], g_all[...], 1, 1).astype(BF16)
        tx = 2 * (zp % 2) + yh
        far_x = (x + 4 - tx) % 4
        piece = jnp.where(zp // 2 == yl, 0, 1)

        @pl.when(far_x != 0)
        def _():
            at = 2 * (far_x - 1) + piece
            send(d_st.at[zp], d_rc.at[at], sd.at[zp], rd.at[at], row, yl * 4 + tx)

    for j in (1, 3):
        from_y(0, j, q_all.at[rows(ypeer(j), TB), :])
    for d in (1, 3, 2):
        from_z(0, d, k_all.at[rows((z + 4 - d) % 4, TB), :])
    kt[...] = k_all[...].T
    for d in (1, 3, 2):
        from_z(1, d, v_all.at[rows((z + 4 - d) % 4, TB), :])
    vt[...] = v_all[...].T

    def forward(i, carry):
        h, t = i // 3, i % 3
        hs, ts = rows(h, HD), rows(t, QT)
        s = dot(k_all[:, hs], q_all[ts, hs], 1, 1)
        top = jnp.max(s, axis=0, keepdims=True)
        p = jnp.exp2((s - top) * (SCALE * LOG2E))
        total = jnp.sum(p, axis=0, keepdims=True)
        o = dot(vt[hs, :], p.astype(BF16), 1, 0)
        o_st[hs, ts] = (o / total).astype(BF16)
        lse_own[pl.ds(h, 1), ts] = top * (SCALE * LOG2E) + jnp.log2(total)
        return carry

    lax.fori_loop(0, 9, forward, 0)

    to_y(3, 1, lse_own, lse_core)
    to_y(2, 1, o_st.at[rows(1 - co, TB), :], o_core)

    @pl.when(inner)
    def _():
        for d in range(3):
            recv(d_rc.at[2 * d + 1], sd.at[0], rd.at[2 * d + 1])
        d_up[...] = (
            d_st[slot_b].astype(F32) + d_rc[1].astype(F32) + d_rc[3].astype(F32) + d_rc[5].astype(F32)
        ).astype(BF16)
        send(d_up, d_yl, sb.at[0], rb.at[0], row, other_yl)

    def both(a, b):
        top = jnp.maximum(a, b)
        lse = top + jnp.log2(jnp.exp2(a - top) + jnp.exp2(b - top))
        return lse, jnp.exp2(a - lse), jnp.exp2(b - lse)

    def head_rows(i):
        return (3 * co + i) // 2, slice(i * 64, (i + 1) * 64)

    from_y(3, 1, lse_core)
    lse1, wa, wb = both(lse_own[...], lse_core[...])
    lse_chip[...] = lse1
    to_y(3, 2, lse_chip, lse_far)
    delta[...] = wa
    lse_c[...] = wb
    from_y(2, 1, o_core)
    for i in range(3):
        head, part = head_rows(i)
        mine = o_st[pl.ds(pl.multiple_of(co * TB + i * 64, 64), 64), :].astype(F32)
        o_chip[part, :] = (
            delta[pl.ds(head, 1), :] * mine + lse_c[pl.ds(head, 1), :] * o_core[part, :].astype(F32)
        ).astype(BF16)

    @pl.when(outer)
    def _():
        send(o_chip, o_rc, sb.at[1], rb.at[1], far, col)

    half = rows(co, TB)

    @pl.when(inner)
    def _():
        for d in range(3):
            recv(d_rc.at[2 * d], sd.at[0], rd.at[2 * d])
        recv(d_yl, sb.at[0], rb.at[0])
        do_all[half, :] = (
            d_st[slot_a].astype(F32) + d_rc[0].astype(F32) + d_rc[2].astype(F32) + d_rc[4].astype(F32)
            + d_yl[...].astype(F32)
        ).astype(BF16)
        send(do_all.at[half, :], do_all.at[half, :], sb.at[2], rb.at[2], far, col)
        send(do_all.at[half, :], do_all.at[half, :], sb.at[3], rb.at[3], core, col)

    from_y(3, 2, lse_far)
    lse2, wa, wb = both(lse_chip[...], lse_far[...])
    lse_c[...] = lse2
    delta[...] = wa
    lse_core[...] = wb

    @pl.when(inner)
    def _():
        recv(o_rc, sb.at[1], rb.at[1])
        for i in range(3):
            head, part = head_rows(i)
            to = pl.ds(pl.multiple_of(slot_a * TB + i * 64, 64), 64)
            attn = (
                delta[pl.ds(head, 1), :] * o_chip[part, :].astype(F32)
                + lse_core[pl.ds(head, 1), :] * o_rc[part, :].astype(F32)
            ).astype(BF16)
            attn_all[to, :] = attn
            do = do_all[pl.ds(pl.multiple_of(co * TB + i * 64, 64), 64), :].astype(F32)
            dp_all[co, pl.ds(head, 1), :] += jnp.sum(do * attn.astype(F32), axis=0, keepdims=True)
        a, b = attn_all.at[rows(slot_a, TB), :], attn_all.at[rows(slot_b, TB), :]
        send(a, a, sa.at[0], ra.at[slot_a], row, other_yl)
        send(dp_all.at[co], dp_all.at[co], sb.at[4], rb.at[4], far, col)
        send(dp_all.at[co], dp_all.at[co], sb.at[5], rb.at[5], core, col)
        for d in (1, 3, 2):
            send(a, a, sa.at[d], ra.at[slot_a], row, xpeer(d))
        recv(b, sa.at[0], ra.at[slot_b])
        for d in (1, 3, 2):
            send(b, b, sa.at[3 + d], ra.at[slot_b], row, xpeer(d))

    @pl.when(outer)
    def _():
        recv(do_all.at[half, :], sb.at[2], rb.at[2])
        send(do_all.at[half, :], do_all.at[half, :], sb.at[3], rb.at[3], core, col)
        recv(dp_all.at[co], sb.at[4], rb.at[4])
        send(dp_all.at[co], dp_all.at[co], sb.at[5], rb.at[5], core, col)

    recv(do_all.at[rows(1 - co, TB), :], sb.at[3], rb.at[3])
    recv(dp_all.at[1 - co], sb.at[5], rb.at[5])
    delta[...] = dp_all[0] + dp_all[1]

    def backward(h, carry):
        hs = rows(h, HD)
        kh = k_all[:, hs]
        vh = v_all[:, hs]
        for t in range(3):
            ts = slice(t * QT, (t + 1) * QT)
            qh = q_all[ts, hs]
            doh = do_all[hs, ts]
            s = dot(kh, qh, 1, 1)
            p = jnp.exp2(s * (SCALE * LOG2E) - lse_c[pl.ds(h, 1), ts]).astype(BF16)
            dprob = dot(vh, doh, 1, 0)
            ds = (p.astype(F32) * (dprob - delta[pl.ds(h, 1), ts]) * SCALE).astype(BF16)
            dvt = dot(p, doh, 1, 1)
            dkt = dot(ds, qh, 1, 0)
            if t == 0:
                vacc[...] = dvt
                kacc[...] = dkt
            else:
                vacc[...] += dvt
                kacc[...] += dkt
            q_st[ts, hs] = dot(kt[hs, :], ds, 1, 0).T.astype(BF16)
        v_st[:, hs] = vacc[...].astype(BF16)
        k_st[:, hs] = kacc[...].astype(BF16)
        for d in (1, 3, 2):
            r = zpeer(d) * 4 + q
            pr = rows(zpeer(d), TB)
            send(v_st.at[pr, hs], v_rc.at[z, :, hs], sk.at[0, h, d - 1], rk.at[0, h, d - 1], r, col)
            send(k_st.at[pr, hs], k_rc.at[z, :, hs], sk.at[1, h, d - 1], rk.at[1, h, d - 1], r, col)
        return carry

    lax.fori_loop(0, NH, backward, 0)
    to_y(4, 3, q_st.at[rows(ypeer(3), TB), :], q_core.at[1])
    to_y(4, 1, q_st.at[rows(ypeer(1), TB), :], q_core.at[0])
    v_rc[z] = v_st[rows(z, TB), :]
    k_rc[z] = k_st[rows(z, TB), :]

    for i in range(4):
        at = rows(i, TB)

        @pl.when(outer | (slot_a != i))
        def _():
            @pl.when(outer | (slot_b != i))
            def _():
                recv(attn_all.at[at, :], sa.at[0], ra.at[i])

    def weight_part(i, carry):
        w_st[rows(i, TB), :] = dot(attn_all[rows(i, TB), :], g_all[...], 1, 0).astype(BF16)
        return carry

    lax.fori_loop(0, 4, weight_part, 0)
    for d in (1, 3, 2):
        sends.append(
            send(w_st.at[rows(zpeer(d), TB), :], w_rc.at[z], sz.at[3, d - 1], rz.at[3, d - 1], zpeer(d) * 4 + q, col)
        )

    def mixed_part(i, carry):
        m_st[rows(i, QT), :] = dot(attn_all[:, rows(i, QT)], w_all[...], 0, 0).astype(BF16)
        return carry

    lax.fori_loop(0, 3, mixed_part, 0)
    to_y(5, 3, m_st.at[rows(ypeer(3), TB), :], m_core.at[1])
    to_y(5, 1, m_st.at[rows(ypeer(1), TB), :], m_core.at[0])

    from_y(4, 3, q_core.at[1])
    q_up[...] = (q_st[part_far, :].astype(F32) + q_core[1].astype(F32)).astype(BF16)
    to_y(4, 2, q_up, q_rc)
    from_y(5, 3, m_core.at[1])
    m_up[...] = (m_st[part_far, :].astype(F32) + m_core[1].astype(F32)).astype(BF16)
    to_y(5, 2, m_up, m_rc)
    w_rc[z] = w_st[rows(z, TB), :]

    for h in range(NH):
        hs = slice(h * HD, (h + 1) * HD)
        for d in (1, 3, 2):
            src = (z + 4 - d) % 4
            recv(v_rc.at[src, :, hs], sk.at[0, h, d - 1], rk.at[0, h, d - 1])
            recv(k_rc.at[src, :, hs], sk.at[1, h, d - 1], rk.at[1, h, d - 1])
    dv_o[...] = sum(v_rc[j].astype(F32) for j in range(4)).astype(BF16)
    dk_o[...] = sum(k_rc[j].astype(F32) for j in range(4)).astype(BF16)
    from_y(4, 1, q_core.at[0])
    from_y(4, 2, q_rc)
    dq_o[...] = (q_st[rows(q, TB), :].astype(F32) + q_core[0].astype(F32) + q_rc[...].astype(F32)).astype(BF16)
    from_y(5, 1, m_core.at[0])
    from_y(5, 2, m_rc)
    mixed_o[...] = (m_st[rows(q, TB), :].astype(F32) + m_core[0].astype(F32) + m_rc[...].astype(F32)).astype(BF16)
    for d in (1, 3, 2):
        from_z(3, d, w_rc.at[(z + 4 - d) % 4])
    wg_o[...] = sum(w_rc[j].astype(F32) for j in range(4)).astype(BF16)

    for d in sends:
        d.wait_send()
    for i in range(4):
        @pl.when(x != 2 * (i % 2) + yh)
        def _():
            left(d_st.at[i], sd.at[i], rd.at[0])

    left(do_all.at[half, :], sb.at[3], rb.at[3])
    left(dp_all.at[0], sb.at[5], rb.at[5])

    @pl.when(inner)
    def _():
        left(d_up, sb.at[0], rb.at[0])
        left(do_all.at[half, :], sb.at[2], rb.at[2])
        left(dp_all.at[0], sb.at[4], rb.at[4])
        for i in range(7):
            left(attn_all.at[rows(0, TB), :], sa.at[i], ra.at[0])

    @pl.when(outer)
    def _():
        left(o_chip, sb.at[1], rb.at[1])

    for h in range(NH):
        hs = slice(h * HD, (h + 1) * HD)
        for j in range(3):
            left(v_rc.at[0, :, hs], sk.at[0, h, j], rk.at[0, h, j])
            left(k_rc.at[0, :, hs], sk.at[1, h, j], rk.at[1, h, j])


def per_device(queries, keys_tile, values_tile, out_weight, out_grad):
    def vm(shape, dtype=BF16):
        return pltpu.VMEM(shape, dtype)

    dma = pltpu.SemaphoreType.DMA
    spec = pl.BlockSpec(memory_space=pltpu.VMEM)
    return pl.pallas_call(
        kernel,
        out_shape=(
            jax.ShapeDtypeStruct((TB, DC), BF16),
            jax.ShapeDtypeStruct((TB, HC), BF16),
            jax.ShapeDtypeStruct((TB, HC), BF16),
            jax.ShapeDtypeStruct((TB, HC), BF16),
            jax.ShapeDtypeStruct((TB, DC), BF16),
        ),
        in_specs=[spec] * 5,
        out_specs=(spec,) * 5,
        scratch_shapes=[
            vm((ZT, HC)), vm((ZT, HC)), vm((ZT, HC)), vm((ZT, DC)), vm((ZT, DC)), vm((HC, ZT)), vm((HC, ZT)),
            vm((HC, ZT)), vm((TB, ZT)), vm((TB, ZT)), vm((TB, ZT)),
            vm((8, ZT), F32), vm((8, ZT), F32), vm((8, ZT), F32), vm((8, ZT), F32), vm((8, ZT), F32), vm((ZT, ZT)),
            vm((4, TB, ZT)), vm((6, TB, ZT)), vm((TB, ZT)), vm((TB, ZT)), vm((HC, ZT)), vm((2, 8, ZT), F32),
            vm((8, ZT), F32),
            vm((ZT, HD), F32), vm((ZT, HD), F32), vm((ZT, HC)), vm((ZT, HC)), vm((ZT, HC)),
            vm((4, TB, HC)), vm((4, TB, HC)), vm((2, TB, HC)), vm((TB, HC)), vm((TB, HC)),
            vm((ZT, DC)), vm((2, TB, DC)), vm((TB, DC)), vm((TB, DC)), vm((ZT, DC)), vm((4, TB, DC)),
            dma((4, 3)), dma((4, 3)), dma((6, 3)), dma((6, 3)), dma((4,)), dma((6,)), dma((7,)), dma((4,)),
            dma((6,)), dma((6,)), dma((2, 3, 3)), dma((2, 3, 3)),
        ],
        compiler_params=pltpu.CompilerParams(
            collective_id=0, has_side_effects=True, vmem_limit_bytes=60 * 1024 * 1024
        ),
    )(queries, keys_tile, values_tile, out_weight, out_grad)


def solution(mesh):
    spec = P("row", "col")
    return jax.shard_map(
        per_device, mesh=mesh, in_specs=(spec,) * 5, out_specs=(spec,) * 5, check_vma=False
    )
```

```python
import jax
import jax.numpy as jnp
from jax import lax
from jax.experimental import pallas as pl
from jax.experimental.pallas import tpu as pltpu
from jax.sharding import PartitionSpec as P

HD = 128
NH = 3
TB = 192
ZT = 4 * TB
HC = NH * HD
DC = 768
PB = HC // 4
QT = 256
SCALE = HD ** (-0.5)
LOG2E = 1.4426950408889634
MESH = pl.DeviceIdType.MESH
F32 = jnp.float32
BF16 = jnp.bfloat16


def dot(a, b, ca, cb):
    return lax.dot_general(a, b, (((ca,), (cb,)), ((), ())), preferred_element_type=F32)


def kernel(
    q_ref, k_ref, v_ref, w_ref, g_ref,
    mixed_o, dq_o, dk_o, dv_o, wg_o,
    k_all, v_all, q_all, w_all, g_all, kt, vt,
    o_st, o_core, o_up, o_far, lse_own, lse_core, lse_chip, lse_far, lse_c, w_own, w_core, w_chip, w_far,
    attn_own, attn_all, d_st, d_rc, do_all, dp_all, delta,
    kacc, vacc, k_st, v_st, q_st, k_r1, v_r1, k_r2, v_r2, q_core, q_up, q_rc,
    m_st, m_core, m_up, m_rc, w_st, w_r1, w_r2,
    sz, rz, sy, ry, sd, rd, sa, ra, sk, rk,
):
    row, col = lax.axis_index("row"), lax.axis_index("col")
    z, q = row // 4, row % 4
    yh, co = q // 2, q % 2
    own = (col % 2 == yh) & (co == yh)
    z_up, z_dn, z_op = (z + 1) % 4, (z + 3) % 4, (z + 2) % 4
    up, dn = z_up * 4 + q, z_dn * 4 + q

    def ypeer(j):
        a = yh if j < 2 else 1 - yh
        b = co if j % 2 == 0 else 1 - co
        return a * 2 + b

    core = z * 4 + ypeer(1)
    far = z * 4 + ypeer(2)

    def copy(src, dst, ss, rs, r, c):
        return pltpu.make_async_remote_copy(
            src_ref=src, dst_ref=dst, send_sem=ss, recv_sem=rs, device_id=(r, c), device_id_type=MESH
        )

    def send(src, dst, ss, rs, r, c):
        d = copy(src, dst, ss, rs, r, c)
        d.start()
        return d

    def recv(dst, ss, rs):
        copy(dst, dst, ss, rs, row, col).wait_recv()

    def left(src, ss, rs):
        copy(src, src, ss, rs, row, col).wait_send()

    def rows(i, n):
        return pl.ds(pl.multiple_of(i * n, n), n)

    barrier = pltpu.get_barrier_semaphore()

    def greet(r, c):
        pl.semaphore_signal(barrier, inc=1, device_id=(r, c), device_id_type=MESH)

    arow = z * 4 + (col % 2) * 2 + yh
    for r in (up, dn, core, far):
        greet(r, col)
    for k in range(8):
        if k == 0:
            @pl.when(jnp.logical_not(own))
            def _():
                greet(arow, col)
        else:
            greet(arow, (col + k) % 8)
    for k in range(4):
        for m in range(2):
            tr, tc = z * 4 + co * 2 + (co + m) % 2, 2 * ((col // 2 + k) % 4) + yh
            if k == 0 and m == 0:
                @pl.when(jnp.logical_not(own))
                def _():
                    greet(tr, tc)
            else:
                greet(tr, tc)
    pl.semaphore_wait(barrier, jnp.where(own, 18, 20))

    sends = []

    def lower(b):
        return rows(2 * b, PB)

    def upper(b):
        return rows(2 * b + 1, PB)

    def z_start(i, src, dst):
        to = dst.at[rows(z, TB), :]
        sends.append(send(src, to, sz.at[i, 0], rz.at[i, 0], up, col))
        sends.append(send(src, to, sz.at[i, 1], rz.at[i, 1], dn, col))

    def z_pass(i, dst):
        recv(dst.at[rows(z_dn, TB), :], sz.at[i, 0], rz.at[i, 0])
        a = dst.at[lower(z_dn), :]
        sends.append(send(a, a, sz.at[i, 2], rz.at[i, 2], up, col))
        recv(dst.at[rows(z_up, TB), :], sz.at[i, 1], rz.at[i, 1])
        b = dst.at[upper(z_up), :]
        sends.append(send(b, b, sz.at[i, 3], rz.at[i, 3], dn, col))

    def z_last(i, dst):
        recv(dst.at[lower(z_op), :], sz.at[i, 2], rz.at[i, 2])
        recv(dst.at[upper(z_op), :], sz.at[i, 3], rz.at[i, 3])

    def to_y(i, j, src, dst):
        sends.append(send(src, dst, sy.at[i, j - 1], ry.at[i, j - 1], far if j == 2 else core, col))

    def from_y(i, j, dst):
        recv(dst, sy.at[i, j - 1], ry.at[i, j - 1])

    z_start(0, k_ref, k_all)
    to_y(0, 2, q_ref, q_all.at[rows(q, TB), :])
    to_y(0, 1, q_ref, q_all.at[rows(q, TB), :])
    z_start(1, v_ref, v_all)
    to_y(1, 2, g_ref, g_all.at[rows(q, TB), :])
    to_y(1, 1, g_ref, g_all.at[rows(q, TB), :])
    k_all[rows(z, TB), :] = k_ref[...]
    v_all[rows(z, TB), :] = v_ref[...]
    q_all[rows(q, TB), :] = q_ref[...]
    g_all[rows(q, TB), :] = g_ref[...]
    w_all[rows(z, TB), :] = w_ref[...]
    lse_own[...] = jnp.zeros_like(lse_own)
    dp_all[q] = jnp.zeros((8, ZT), F32)

    part_far = rows(ypeer(2), TB)
    z_pass(0, k_all)
    from_y(0, 2, q_all.at[part_far, :])
    to_y(0, 3, q_all.at[part_far, :], q_all.at[part_far, :])
    z_pass(1, v_all)
    z_start(2, w_ref, w_all)
    for j in (1, 3):
        from_y(0, j, q_all.at[rows(ypeer(j), TB), :])
    z_last(0, k_all)
    kt[...] = k_all[...].T
    from_y(1, 2, g_all.at[part_far, :])
    to_y(1, 3, g_all.at[part_far, :], g_all.at[part_far, :])
    z_last(1, v_all)
    vt[...] = v_all[...].T

    def forward(i, carry):
        h, t = i // 3, i % 3
        hs, ts = rows(h, HD), rows(t, QT)
        s = dot(k_all[:, hs], q_all[ts, hs], 1, 1)
        top = jnp.max(s, axis=0, keepdims=True)
        p = jnp.exp2((s - top) * (SCALE * LOG2E))
        total = jnp.sum(p, axis=0, keepdims=True)
        o = dot(vt[hs, :], p.astype(BF16), 1, 0)
        o_st[hs, ts] = (o / total).astype(BF16)
        lse_own[pl.ds(h, 1), ts] = top * (SCALE * LOG2E) + jnp.log2(total)
        return carry

    def d_attn(n, zp):
        part = dot(w_all[rows(zp, TB), :], g_all[...], 1, 1).astype(BF16)
        d_st[2 * n] = part[:PB]
        d_st[2 * n + 1] = part[PB:]
        mine = own & (zp == col // 2)
        for m in (1, 0):
            half = (co + m) % 2
            tr, tc = z * 4 + co * 2 + half, 2 * zp + yh
            src = d_st.at[2 * n + half]
            if m == 1:
                sends.append(send(src, d_rc.at[col], sd.at[n, 1], rd.at[col], tr, tc))
            else:
                @pl.when(jnp.logical_not(mine))
                def _():
                    send(src, d_rc.at[col], sd.at[n, 0], rd.at[col], tr, tc)

                @pl.when(mine)
                def _():
                    d_rc[col] = d_st[2 * n + half]

    lax.fori_loop(0, 6, forward, 0)
    for j in (1, 3):
        from_y(1, j, g_all.at[rows(ypeer(j), TB), :])
    z_pass(2, w_all)
    d_attn(0, z)
    lax.fori_loop(6, 9, forward, 0)

    to_y(3, 1, lse_own, lse_core)
    to_y(2, 3, o_st.at[rows(ypeer(3), PB), :], o_core.at[1])
    to_y(2, 1, o_st.at[rows(ypeer(1), PB), :], o_core.at[0])
    d_attn(1, z_dn)
    d_attn(2, z_up)

    def both(a, b):
        top = jnp.maximum(a, b)
        lse = top + jnp.log2(jnp.exp2(a - top) + jnp.exp2(b - top))
        return lse, jnp.exp2(a - lse), jnp.exp2(b - lse)

    def pieces(owner):
        for i in range(3):
            yield (
                pl.ds((3 * owner + i) // 4, 1),
                slice(i * 32, (i + 1) * 32),
                pl.ds(pl.multiple_of(owner * PB + i * 32, 32), 32),
            )

    from_y(3, 1, lse_core)
    lse_chip[...], w_own[...], w_core[...] = both(lse_own[...], lse_core[...])
    to_y(3, 2, lse_chip, lse_far)
    from_y(2, 3, o_core.at[1])
    for head, part, src in pieces(ypeer(2)):
        o_up[part, :] = (
            w_own[head, :] * o_st[src, :].astype(F32) + w_core[head, :] * o_core[1, part, :].astype(F32)
        ).astype(BF16)
    to_y(2, 2, o_up, o_far)
    z_last(2, w_all)
    d_attn(3, z_op)
    from_y(2, 1, o_core.at[0])
    from_y(3, 2, lse_far)
    lse_c[...], w_chip[...], w_far[...] = both(lse_chip[...], lse_far[...])
    w_own[...] = w_own[...] * w_chip[...]
    w_core[...] = w_core[...] * w_chip[...]
    from_y(2, 2, o_far)
    for head, part, src in pieces(q):
        attn_own[part, :] = (
            w_own[head, :] * o_st[src, :].astype(F32)
            + w_core[head, :] * o_core[0, part, :].astype(F32)
            + w_far[head, :] * o_far[part, :].astype(F32)
        ).astype(BF16)

    slot = (col // 2) * 2 + co
    for k in (1, 7, 4, 2, 6, 3, 5):
        sends.append(send(attn_own, attn_all.at[rows(slot, PB), :], sa.at[k], ra.at[slot], arow, (col + k) % 8))

    @pl.when(jnp.logical_not(own))
    def _():
        send(attn_own, attn_all.at[rows(slot, PB), :], sa.at[0], ra.at[slot], arow, col)

    @pl.when(own)
    def _():
        attn_all[rows(slot, PB), :] = attn_own[...]

    for k in range(8):
        src = (col + k) % 8
        if k == 0:
            @pl.when(jnp.logical_not(own))
            def _():
                recv(d_rc.at[src], sd.at[0, 0], rd.at[src])
        else:
            recv(d_rc.at[src], sd.at[0, 0], rd.at[src])
    for head, part, dst in pieces(q):
        do = sum(d_rc[k, part, :].astype(F32) for k in range(8)).astype(BF16)
        do_all[dst, :] = do
        dp_all[q, head, :] += jnp.sum(do.astype(F32) * attn_own[part, :].astype(F32), axis=0, keepdims=True)

    def do_rows(j):
        return do_all.at[rows(ypeer(j), PB), :]

    for j in (2, 1):
        to_y(6, j, do_rows(0), do_rows(0))
        to_y(7, j, dp_all.at[q], dp_all.at[q])
    from_y(6, 2, do_rows(2))
    to_y(6, 3, do_rows(2), do_rows(2))
    from_y(7, 2, dp_all.at[ypeer(2)])
    to_y(7, 3, dp_all.at[ypeer(2)], dp_all.at[ypeer(2)])
    for j in (1, 3):
        from_y(6, j, do_rows(j))
        from_y(7, j, dp_all.at[ypeer(j)])
    delta[...] = dp_all[0] + dp_all[1] + dp_all[2] + dp_all[3]

    def backward(h, carry):
        hs = rows(h, HD)
        kh = k_all[:, hs]
        vh = v_all[:, hs]
        for t in range(3):
            ts = slice(t * QT, (t + 1) * QT)
            qh = q_all[ts, hs]
            doh = do_all[hs, ts]
            s = dot(kh, qh, 1, 1)
            p = jnp.exp2(s * (SCALE * LOG2E) - lse_c[pl.ds(h, 1), ts]).astype(BF16)
            dprob = dot(vh, doh, 1, 0)
            ds = (p.astype(F32) * (dprob - delta[pl.ds(h, 1), ts]) * SCALE).astype(BF16)
            dvt = dot(p, doh, 1, 1)
            dkt = dot(ds, qh, 1, 0)
            if t == 0:
                vacc[...] = dvt
                kacc[...] = dkt
            else:
                vacc[...] += dvt
                kacc[...] += dkt
            q_st[ts, hs] = dot(kt[hs, :], ds, 1, 0).T.astype(BF16)
        v_st[:, hs] = vacc[...].astype(BF16)
        k_st[:, hs] = kacc[...].astype(BF16)
        for i, (st, r1) in enumerate(((v_st, v_r1), (k_st, k_r1))):
            send(st.at[lower(z_op), hs], r1.at[0, :, hs], sk.at[i, h, 0], rk.at[i, h, 0], up, col)
            send(st.at[upper(z_op), hs], r1.at[1, :, hs], sk.at[i, h, 1], rk.at[i, h, 1], dn, col)
        return carry

    lax.fori_loop(0, NH, backward, 0)
    to_y(4, 3, q_st.at[rows(ypeer(3), TB), :], q_core.at[1])
    to_y(4, 1, q_st.at[rows(ypeer(1), TB), :], q_core.at[0])

    def z_add(i, st, r1, r2):
        a, b = lower(z_up), upper(z_dn)
        st[a, :] = (st[a, :].astype(F32) + r1[0].astype(F32)).astype(BF16)
        sends.append(send(st.at[rows(z_up, TB), :], r2.at[0], sz.at[i, 2], rz.at[i, 2], up, col))
        st[b, :] = (st[b, :].astype(F32) + r1[1].astype(F32)).astype(BF16)
        sends.append(send(st.at[rows(z_dn, TB), :], r2.at[1], sz.at[i, 3], rz.at[i, 3], dn, col))

    def z_sum(i, st, r2):
        recv(r2.at[0], sz.at[i, 2], rz.at[i, 2])
        recv(r2.at[1], sz.at[i, 3], rz.at[i, 3])
        return (st[rows(z, TB), :].astype(F32) + r2[0].astype(F32) + r2[1].astype(F32)).astype(BF16)

    def weight_part(b):
        for m in range(2):
            src = 2 * b + m

            @pl.when(jnp.logical_not(own & (src == slot)))
            def _():
                recv(attn_all.at[rows(src, PB), :], sa.at[0], ra.at[src])

        w_st[rows(b, TB), :] = dot(attn_all[rows(b, TB), :], g_all[...], 1, 0).astype(BF16)

    for i, (st, r1, r2) in enumerate(((v_st, v_r1, v_r2), (k_st, k_r1, k_r2))):
        for h in range(NH):
            hs = slice(h * HD, (h + 1) * HD)
            for j in range(2):
                recv(r1.at[j, :, hs], sk.at[i, h, j], rk.at[i, h, j])
        z_add(4 + i, st, r1, r2)
    weight_part(z_op)
    sends.append(send(w_st.at[lower(z_op), :], w_r1.at[0], sz.at[3, 0], rz.at[3, 0], up, col))
    sends.append(send(w_st.at[upper(z_op), :], w_r1.at[1], sz.at[3, 1], rz.at[3, 1], dn, col))
    from_y(4, 3, q_core.at[1])
    q_up[...] = (q_st[part_far, :].astype(F32) + q_core[1].astype(F32)).astype(BF16)
    to_y(4, 2, q_up, q_rc)
    weight_part(z_up)
    weight_part(z_dn)
    weight_part(z)

    def mixed_part(i, carry):
        m_st[rows(i, QT), :] = dot(attn_all[:, rows(i, QT)], w_all[...], 0, 0).astype(BF16)
        return carry

    lax.fori_loop(0, 3, mixed_part, 0)
    to_y(5, 3, m_st.at[rows(ypeer(3), TB), :], m_core.at[1])
    to_y(5, 1, m_st.at[rows(ypeer(1), TB), :], m_core.at[0])
    recv(w_r1.at[0], sz.at[3, 0], rz.at[3, 0])
    recv(w_r1.at[1], sz.at[3, 1], rz.at[3, 1])
    z_add(3, w_st, w_r1, w_r2)
    from_y(5, 3, m_core.at[1])
    m_up[...] = (m_st[part_far, :].astype(F32) + m_core[1].astype(F32)).astype(BF16)
    to_y(5, 2, m_up, m_rc)

    dv_o[...] = z_sum(4, v_st, v_r2)
    dk_o[...] = z_sum(5, k_st, k_r2)
    from_y(4, 1, q_core.at[0])
    from_y(4, 2, q_rc)
    dq_o[...] = (q_st[rows(q, TB), :].astype(F32) + q_core[0].astype(F32) + q_rc[...].astype(F32)).astype(BF16)
    from_y(5, 1, m_core.at[0])
    from_y(5, 2, m_rc)
    mixed_o[...] = (m_st[rows(q, TB), :].astype(F32) + m_core[0].astype(F32) + m_rc[...].astype(F32)).astype(BF16)
    wg_o[...] = z_sum(3, w_st, w_r2)

    for d in sends:
        d.wait_send()
    for n, zp in enumerate((z, z_dn, z_up, z_op)):
        @pl.when(jnp.logical_not(own & (zp == col // 2)))
        def _():
            left(d_st.at[2 * n], sd.at[n, 0], rd.at[0])

    @pl.when(jnp.logical_not(own))
    def _():
        left(attn_own, sa.at[0], ra.at[0])

    for h in range(NH):
        hs = slice(h * HD, (h + 1) * HD)
        for j in range(2):
            left(v_r1.at[0, :, hs], sk.at[0, h, j], rk.at[0, h, j])
            left(k_r1.at[0, :, hs], sk.at[1, h, j], rk.at[1, h, j])


def per_device(queries, keys_tile, values_tile, out_weight, out_grad):
    def vm(shape, dtype=BF16):
        return pltpu.VMEM(shape, dtype)

    dma = pltpu.SemaphoreType.DMA
    spec = pl.BlockSpec(memory_space=pltpu.VMEM)
    return pl.pallas_call(
        kernel,
        out_shape=(
            jax.ShapeDtypeStruct((TB, DC), BF16),
            jax.ShapeDtypeStruct((TB, HC), BF16),
            jax.ShapeDtypeStruct((TB, HC), BF16),
            jax.ShapeDtypeStruct((TB, HC), BF16),
            jax.ShapeDtypeStruct((TB, DC), BF16),
        ),
        in_specs=[spec] * 5,
        out_specs=(spec,) * 5,
        scratch_shapes=[
            vm((ZT, HC)), vm((ZT, HC)), vm((ZT, HC)), vm((ZT, DC)), vm((ZT, DC)), vm((HC, ZT)), vm((HC, ZT)),
            vm((HC, ZT)), vm((2, PB, ZT)), vm((PB, ZT)), vm((PB, ZT)),
            *[vm((8, ZT), F32) for _ in range(9)],
            vm((PB, ZT)), vm((8 * PB, ZT)), vm((8, PB, ZT)), vm((8, PB, ZT)), vm((HC, ZT)), vm((4, 8, ZT), F32),
            vm((8, ZT), F32),
            vm((ZT, HD), F32), vm((ZT, HD), F32), vm((ZT, HC)), vm((ZT, HC)), vm((ZT, HC)),
            vm((2, PB, HC)), vm((2, PB, HC)), vm((2, TB, HC)), vm((2, TB, HC)),
            vm((2, TB, HC)), vm((TB, HC)), vm((TB, HC)),
            vm((ZT, DC)), vm((2, TB, DC)), vm((TB, DC)), vm((TB, DC)),
            vm((ZT, DC)), vm((2, PB, DC)), vm((2, TB, DC)),
            dma((6, 4)), dma((6, 4)), dma((8, 3)), dma((8, 3)), dma((4, 2)), dma((8,)), dma((8,)), dma((8,)),
            dma((2, 3, 2)), dma((2, 3, 2)),
        ],
        compiler_params=pltpu.CompilerParams(
            collective_id=0, has_side_effects=True, vmem_limit_bytes=60 * 1024 * 1024
        ),
    )(queries, keys_tile, values_tile, out_weight, out_grad)


def solution(mesh):
    spec = P("row", "col")
    return jax.shard_map(
        per_device, mesh=mesh, in_specs=(spec,) * 5, out_specs=(spec,) * 5, check_vma=False
    )
```

```python
import jax
import jax.numpy as jnp
from jax import lax
from jax.experimental import pallas as pl
from jax.experimental.pallas import tpu as pltpu
from jax.sharding import PartitionSpec as P

HD = 128
NH = 3
TB = 192
ZT = 4 * TB
HC = NH * HD
DC = 768
PB = HC // 4
QT = 256
SCALE = HD ** (-0.5)
LOG2E = 1.4426950408889634
MESH = pl.DeviceIdType.MESH
F32 = jnp.float32
BF16 = jnp.bfloat16


def dot(a, b, ca, cb):
    return lax.dot_general(a, b, (((ca,), (cb,)), ((), ())), preferred_element_type=F32)


def kernel(
    q_ref, k_ref, v_ref, w_ref, g_ref,
    mixed_o, dq_o, dk_o, dv_o, wg_o,
    k_all, v_all, q_all, w_all, g_all, kt, vt,
    o_st, o_core, o_chip, o_far, lse_own, lse_core, lse_chip, lse_far, lse_c, w_own, w_core, w_chip, w_far,
    attn_all, d_st, d_r1, d_sum, d_rc, d_up, d_yl, do_all, dp_all, delta,
    kacc, vacc, k_st, v_st, q_st, k_r1, v_r1, k_r2, v_r2, q_core, q_up, q_rc,
    m_st, m_core, m_up, m_rc, w_st, w_r1, w_r2,
    sz, rz, sy, ry, sd, rx, sl, rd, sa, ra, rh, sb, rb, sk, rk,
):
    row, col = lax.axis_index("row"), lax.axis_index("col")
    z, q = row // 4, row % 4
    yh, co = q // 2, q % 2
    yl, x = col // 4, col % 4
    inner = x % 2 == yh
    outer = x % 2 != yh
    x_up, x_dn, other_yl = yl * 4 + (x + 1) % 4, yl * 4 + (x + 3) % 4, (1 - yl) * 4 + x
    z_up, z_dn, z_op = (z + 1) % 4, (z + 3) % 4, (z + 2) % 4
    up, dn = z_up * 4 + q, z_dn * 4 + q

    def ypeer(j):
        a = yh if j < 2 else 1 - yh
        b = co if j % 2 == 0 else 1 - co
        return a * 2 + b

    core = z * 4 + ypeer(1)
    far = z * 4 + ypeer(2)

    def copy(src, dst, ss, rs, r, c):
        return pltpu.make_async_remote_copy(
            src_ref=src, dst_ref=dst, send_sem=ss, recv_sem=rs, device_id=(r, c), device_id_type=MESH
        )

    def send(src, dst, ss, rs, r, c):
        d = copy(src, dst, ss, rs, r, c)
        d.start()
        return d

    def recv(dst, ss, rs):
        copy(dst, dst, ss, rs, row, col).wait_recv()

    def left(src, ss, rs):
        copy(src, src, ss, rs, row, col).wait_send()

    def rows(i, n):
        return pl.ds(pl.multiple_of(i * n, n), n)

    barrier = pltpu.get_barrier_semaphore()

    def greet(r, c):
        pl.semaphore_signal(barrier, inc=1, device_id=(r, c), device_id_type=MESH)

    for r in (up, dn, core, far):
        greet(r, col)
    for c in (x_up, x_dn, other_yl):
        greet(row, c)
    pl.semaphore_wait(barrier, 7)

    sends = []

    def lower(b):
        return rows(2 * b, PB)

    def upper(b):
        return rows(2 * b + 1, PB)

    def z_start(i, src, dst):
        to = dst.at[rows(z, TB), :]
        sends.append(send(src, to, sz.at[i, 0], rz.at[i, 0], up, col))
        sends.append(send(src, to, sz.at[i, 1], rz.at[i, 1], dn, col))

    def z_pass(i, dst):
        recv(dst.at[rows(z_dn, TB), :], sz.at[i, 0], rz.at[i, 0])
        a = dst.at[lower(z_dn), :]
        sends.append(send(a, a, sz.at[i, 2], rz.at[i, 2], up, col))
        recv(dst.at[rows(z_up, TB), :], sz.at[i, 1], rz.at[i, 1])
        b = dst.at[upper(z_up), :]
        sends.append(send(b, b, sz.at[i, 3], rz.at[i, 3], dn, col))

    def z_last(i, dst):
        recv(dst.at[lower(z_op), :], sz.at[i, 2], rz.at[i, 2])
        recv(dst.at[upper(z_op), :], sz.at[i, 3], rz.at[i, 3])

    def to_y(i, j, src, dst):
        sends.append(send(src, dst, sy.at[i, j - 1], ry.at[i, j - 1], far if j == 2 else core, col))

    def from_y(i, j, dst):
        recv(dst, sy.at[i, j - 1], ry.at[i, j - 1])

    z_start(0, k_ref, k_all)
    to_y(0, 2, q_ref, q_all.at[rows(q, TB), :])
    to_y(0, 1, q_ref, q_all.at[rows(q, TB), :])
    z_start(1, v_ref, v_all)
    to_y(1, 2, g_ref, g_all.at[rows(q, TB), :])
    to_y(1, 1, g_ref, g_all.at[rows(q, TB), :])
    k_all[rows(z, TB), :] = k_ref[...]
    v_all[rows(z, TB), :] = v_ref[...]
    q_all[rows(q, TB), :] = q_ref[...]
    g_all[rows(q, TB), :] = g_ref[...]
    w_all[rows(z, TB), :] = w_ref[...]
    lse_own[...] = jnp.zeros_like(lse_own)
    dp_all[co] = jnp.zeros((8, ZT), F32)

    part_far = rows(ypeer(2), TB)
    z_pass(0, k_all)
    from_y(0, 2, q_all.at[part_far, :])
    to_y(0, 3, q_all.at[part_far, :], q_all.at[part_far, :])
    z_pass(1, v_all)
    z_start(2, w_ref, w_all)
    for j in (1, 3):
        from_y(0, j, q_all.at[rows(ypeer(j), TB), :])
    z_last(0, k_all)
    kt[...] = k_all[...].T
    from_y(1, 2, g_all.at[part_far, :])
    to_y(1, 3, g_all.at[part_far, :], g_all.at[part_far, :])
    z_last(1, v_all)
    vt[...] = v_all[...].T

    def forward(i, carry):
        h, t = i // 3, i % 3
        hs, ts = rows(h, HD), rows(t, QT)
        s = dot(k_all[:, hs], q_all[ts, hs], 1, 1)
        top = jnp.max(s, axis=0, keepdims=True)
        p = jnp.exp2((s - top) * (SCALE * LOG2E))
        total = jnp.sum(p, axis=0, keepdims=True)
        o = dot(vt[hs, :], p.astype(BF16), 1, 0)
        o_st[hs, ts] = (o / total).astype(BF16)
        lse_own[pl.ds(h, 1), ts] = top * (SCALE * LOG2E) + jnp.log2(total)
        return carry

    def slot_of(c, other):
        return 2 * (1 - yl if other else yl) + c % 4 // 2

    slot_a, slot_b = slot_of(x, False), slot_of(x, True)

    def d_attn(n, zp):
        d_st[zp] = dot(w_all[rows(zp, TB), :], g_all[...], 1, 1).astype(BF16)
        tx = 2 * (zp % 2) + yh
        piece = jnp.where(zp // 2 == yl, 0, 1)

        @pl.when(inner & (tx != x))
        def _():
            send(d_st.at[zp, :PB], d_r1.at[piece], sd.at[n, 0], rx.at[piece], row, x_up)
            send(d_st.at[zp, PB:], d_r1.at[2 + piece], sd.at[n, 1], rx.at[2 + piece], row, x_dn)

        @pl.when(outer & (tx == (x + 1) % 4))
        def _():
            send(d_st.at[zp, PB:], d_rc.at[piece, PB:], sd.at[n, 0], rd.at[2 * piece + 1], row, x_up)

        @pl.when(outer & (tx == (x + 3) % 4))
        def _():
            send(d_st.at[zp, :PB], d_rc.at[2 + piece, :PB], sd.at[n, 0], rd.at[4 + 2 * piece], row, x_dn)

    lax.fori_loop(0, 6, forward, 0)
    for j in (1, 3):
        from_y(1, j, g_all.at[rows(ypeer(j), TB), :])
    z_pass(2, w_all)
    d_attn(0, z)
    lax.fori_loop(6, 9, forward, 0)

    to_y(3, 1, lse_own, lse_core)
    to_y(2, 1, o_st.at[rows(1 - co, TB), :], o_core)
    d_attn(1, z_dn)
    d_attn(2, z_up)

    def both(a, b):
        top = jnp.maximum(a, b)
        lse = top + jnp.log2(jnp.exp2(a - top) + jnp.exp2(b - top))
        return lse, jnp.exp2(a - lse), jnp.exp2(b - lse)

    def pieces():
        for i in range(3):
            yield (
                pl.ds((3 * co + i) // 2, 1),
                slice(i * 64, (i + 1) * 64),
                pl.ds(pl.multiple_of(co * TB + i * 64, 64), 64),
                pl.ds(pl.multiple_of(slot_a * TB + i * 64, 64), 64),
            )

    from_y(3, 1, lse_core)
    lse_chip[...], w_own[...], w_core[...] = both(lse_own[...], lse_core[...])
    to_y(3, 2, lse_chip, lse_far)
    from_y(2, 1, o_core)
    for head, part, src, to in pieces():
        o_chip[part, :] = (
            w_own[head, :] * o_st[src, :].astype(F32) + w_core[head, :] * o_core[part, :].astype(F32)
        ).astype(BF16)

    @pl.when(outer)
    def _():
        send(o_chip, o_far, sb.at[1], rb.at[1], far, col)

    z_last(2, w_all)
    d_attn(3, z_op)
    from_y(3, 2, lse_far)
    lse_c[...], w_chip[...], w_far[...] = both(lse_chip[...], lse_far[...])
    half = rows(co, TB)

    def half_of(b, i):
        return rows(2 * b + i, PB)

    @pl.when(inner)
    def _():
        recv(o_far, sb.at[1], rb.at[1])
        for head, part, src, to in pieces():
            attn_all[to, :] = (
                w_chip[head, :] * o_chip[part, :].astype(F32) + w_far[head, :] * o_far[part, :].astype(F32)
            ).astype(BF16)
        a, b = attn_all.at[rows(slot_a, TB), :], attn_all.at[rows(slot_b, TB), :]
        send(a, a, sa.at[0], ra.at[slot_a], row, other_yl)
        send(a, a, sa.at[1], ra.at[slot_a], row, x_up)
        send(a, a, sa.at[2], ra.at[slot_a], row, x_dn)
        for i in (2, 3, 6, 7):
            recv(d_rc.at[i // 4 * 2 + 1, i % 2 * PB : (i % 2 + 1) * PB], sd.at[0, 0], rd.at[i])
        d_up[...] = (d_st[slot_b].astype(F32) + d_rc[1].astype(F32) + d_rc[3].astype(F32)).astype(BF16)
        send(d_up, d_yl, sb.at[0], rb.at[0], row, other_yl)
        recv(b, sa.at[0], ra.at[slot_b])
        send(b, b, sa.at[3], ra.at[slot_b], row, x_up)
        send(b, b, sa.at[4], ra.at[slot_b], row, x_dn)
        for i in (0, 1, 4, 5):
            recv(d_rc.at[i // 4 * 2, i % 2 * PB : (i % 2 + 1) * PB], sd.at[0, 0], rd.at[i])
        recv(d_yl, sb.at[0], rb.at[0])
        do_all[half, :] = (
            d_st[slot_a].astype(F32) + d_rc[0].astype(F32) + d_rc[2].astype(F32) + d_yl[...].astype(F32)
        ).astype(BF16)
        send(do_all.at[half, :], do_all.at[half, :], sb.at[2], rb.at[2], far, col)
        send(do_all.at[half, :], do_all.at[half, :], sb.at[3], rb.at[3], core, col)
        for head, part, src, to in pieces():
            dp_all[co, head, :] += jnp.sum(
                do_all[src, :].astype(F32) * attn_all[to, :].astype(F32), axis=0, keepdims=True
            )
        send(dp_all.at[co], dp_all.at[co], sb.at[4], rb.at[4], far, col)
        send(dp_all.at[co], dp_all.at[co], sb.at[5], rb.at[5], core, col)

    @pl.when(outer)
    def _():
        for p in (1, 0):
            s_up, s_dn = slot_of(x + 1, p == 1), slot_of(x + 3, p == 1)
            recv(d_r1.at[p], sd.at[0, 0], rx.at[p])
            d_sum[p] = (d_st[s_up, :PB].astype(F32) + d_r1[p].astype(F32)).astype(BF16)
            send(d_sum.at[p], d_rc.at[p, :PB], sl.at[p], rd.at[2 * p], row, x_up)
            recv(d_r1.at[2 + p], sd.at[0, 0], rx.at[2 + p])
            d_sum[2 + p] = (d_st[s_dn, PB:].astype(F32) + d_r1[2 + p].astype(F32)).astype(BF16)
            send(d_sum.at[2 + p], d_rc.at[2 + p, PB:], sl.at[2 + p], rd.at[4 + 2 * p + 1], row, x_dn)
        for p in range(2):
            s_up, s_dn = slot_of(x + 1, p == 1), slot_of(x + 3, p == 1)
            recv(attn_all.at[rows(s_dn, TB), :], sa.at[0], ra.at[s_dn])
            a = attn_all.at[half_of(s_dn, 0), :]
            send(a, a, sa.at[p], rh.at[2 * s_dn], row, x_up)
            recv(attn_all.at[rows(s_up, TB), :], sa.at[0], ra.at[s_up])
            b = attn_all.at[half_of(s_up, 1), :]
            send(b, b, sa.at[2 + p], rh.at[2 * s_up + 1], row, x_dn)
        recv(do_all.at[half, :], sb.at[2], rb.at[2])
        send(do_all.at[half, :], do_all.at[half, :], sb.at[3], rb.at[3], core, col)
        recv(dp_all.at[co], sb.at[4], rb.at[4])
        send(dp_all.at[co], dp_all.at[co], sb.at[5], rb.at[5], core, col)

    recv(do_all.at[rows(1 - co, TB), :], sb.at[3], rb.at[3])
    recv(dp_all.at[1 - co], sb.at[5], rb.at[5])
    delta[...] = dp_all[0] + dp_all[1]

    def backward(h, carry):
        hs = rows(h, HD)
        kh = k_all[:, hs]
        vh = v_all[:, hs]
        for t in range(3):
            ts = slice(t * QT, (t + 1) * QT)
            qh = q_all[ts, hs]
            doh = do_all[hs, ts]
            s = dot(kh, qh, 1, 1)
            p = jnp.exp2(s * (SCALE * LOG2E) - lse_c[pl.ds(h, 1), ts]).astype(BF16)
            dprob = dot(vh, doh, 1, 0)
            ds = (p.astype(F32) * (dprob - delta[pl.ds(h, 1), ts]) * SCALE).astype(BF16)
            dvt = dot(p, doh, 1, 1)
            dkt = dot(ds, qh, 1, 0)
            if t == 0:
                vacc[...] = dvt
                kacc[...] = dkt
            else:
                vacc[...] += dvt
                kacc[...] += dkt
            q_st[ts, hs] = dot(kt[hs, :], ds, 1, 0).T.astype(BF16)
        v_st[:, hs] = vacc[...].astype(BF16)
        k_st[:, hs] = kacc[...].astype(BF16)
        for i, (st, r1) in enumerate(((v_st, v_r1), (k_st, k_r1))):
            send(st.at[lower(z_op), hs], r1.at[0, :, hs], sk.at[i, h, 0], rk.at[i, h, 0], up, col)
            send(st.at[upper(z_op), hs], r1.at[1, :, hs], sk.at[i, h, 1], rk.at[i, h, 1], dn, col)
        return carry

    lax.fori_loop(0, NH, backward, 0)
    to_y(4, 3, q_st.at[rows(ypeer(3), TB), :], q_core.at[1])
    to_y(4, 1, q_st.at[rows(ypeer(1), TB), :], q_core.at[0])

    def z_add(i, st, r1, r2):
        a, b = lower(z_up), upper(z_dn)
        st[a, :] = (st[a, :].astype(F32) + r1[0].astype(F32)).astype(BF16)
        sends.append(send(st.at[rows(z_up, TB), :], r2.at[0], sz.at[i, 2], rz.at[i, 2], up, col))
        st[b, :] = (st[b, :].astype(F32) + r1[1].astype(F32)).astype(BF16)
        sends.append(send(st.at[rows(z_dn, TB), :], r2.at[1], sz.at[i, 3], rz.at[i, 3], dn, col))

    def z_sum(i, st, r2):
        recv(r2.at[0], sz.at[i, 2], rz.at[i, 2])
        recv(r2.at[1], sz.at[i, 3], rz.at[i, 3])
        return (st[rows(z, TB), :].astype(F32) + r2[0].astype(F32) + r2[1].astype(F32)).astype(BF16)

    def weight_part(b):
        w_st[rows(b, TB), :] = dot(attn_all[rows(b, TB), :], g_all[...], 1, 0).astype(BF16)

    for i, (st, r1, r2) in enumerate(((v_st, v_r1, v_r2), (k_st, k_r1, k_r2))):
        for h in range(NH):
            hs = slice(h * HD, (h + 1) * HD)
            for j in range(2):
                recv(r1.at[j, :, hs], sk.at[i, h, j], rk.at[i, h, j])
        z_add(4 + i, st, r1, r2)

    @pl.when(inner)
    def _():
        for p in range(2):
            b = slot_of(x + 2, p == 1)
            for i in range(2):
                recv(attn_all.at[half_of(b, i), :], sa.at[0], rh.at[2 * b + i])

    weight_part(z_op)
    sends.append(send(w_st.at[lower(z_op), :], w_r1.at[0], sz.at[3, 0], rz.at[3, 0], up, col))
    sends.append(send(w_st.at[upper(z_op), :], w_r1.at[1], sz.at[3, 1], rz.at[3, 1], dn, col))
    from_y(4, 3, q_core.at[1])
    q_up[...] = (q_st[part_far, :].astype(F32) + q_core[1].astype(F32)).astype(BF16)
    to_y(4, 2, q_up, q_rc)
    weight_part(z_up)
    weight_part(z_dn)
    weight_part(z)

    def mixed_part(i, carry):
        m_st[rows(i, QT), :] = dot(attn_all[:, rows(i, QT)], w_all[...], 0, 0).astype(BF16)
        return carry

    lax.fori_loop(0, 3, mixed_part, 0)
    to_y(5, 3, m_st.at[rows(ypeer(3), TB), :], m_core.at[1])
    to_y(5, 1, m_st.at[rows(ypeer(1), TB), :], m_core.at[0])
    recv(w_r1.at[0], sz.at[3, 0], rz.at[3, 0])
    recv(w_r1.at[1], sz.at[3, 1], rz.at[3, 1])
    z_add(3, w_st, w_r1, w_r2)
    from_y(5, 3, m_core.at[1])
    m_up[...] = (m_st[part_far, :].astype(F32) + m_core[1].astype(F32)).astype(BF16)
    to_y(5, 2, m_up, m_rc)

    dv_o[...] = z_sum(4, v_st, v_r2)
    dk_o[...] = z_sum(5, k_st, k_r2)
    from_y(4, 1, q_core.at[0])
    from_y(4, 2, q_rc)
    dq_o[...] = (q_st[rows(q, TB), :].astype(F32) + q_core[0].astype(F32) + q_rc[...].astype(F32)).astype(BF16)
    from_y(5, 1, m_core.at[0])
    from_y(5, 2, m_rc)
    mixed_o[...] = (m_st[rows(q, TB), :].astype(F32) + m_core[0].astype(F32) + m_rc[...].astype(F32)).astype(BF16)
    wg_o[...] = z_sum(3, w_st, w_r2)

    for d in sends:
        d.wait_send()
    left(do_all.at[half, :], sb.at[3], rb.at[3])
    left(dp_all.at[0], sb.at[5], rb.at[5])

    @pl.when(inner)
    def _():
        for n, zp in enumerate((z, z_dn, z_up, z_op)):
            @pl.when(2 * (zp % 2) + yh != x)
            def _():
                left(d_st.at[0, :PB], sd.at[n, 0], rx.at[0])
                left(d_st.at[0, :PB], sd.at[n, 1], rx.at[0])

        for i in range(5):
            left(attn_all.at[rows(0, TB), :], sa.at[i], ra.at[0])
        left(d_up, sb.at[0], rb.at[0])
        left(do_all.at[half, :], sb.at[2], rb.at[2])
        left(dp_all.at[0], sb.at[4], rb.at[4])

    @pl.when(outer)
    def _():
        for n in range(4):
            left(d_st.at[0, :PB], sd.at[n, 0], rx.at[0])
            left(d_sum.at[n], sl.at[n], rx.at[0])
            left(attn_all.at[half_of(0, 0), :], sa.at[n], ra.at[0])
        left(o_chip, sb.at[1], rb.at[1])

    for h in range(NH):
        hs = slice(h * HD, (h + 1) * HD)
        for j in range(2):
            left(v_r1.at[0, :, hs], sk.at[0, h, j], rk.at[0, h, j])
            left(k_r1.at[0, :, hs], sk.at[1, h, j], rk.at[1, h, j])


def per_device(queries, keys_tile, values_tile, out_weight, out_grad):
    def vm(shape, dtype=BF16):
        return pltpu.VMEM(shape, dtype)

    dma = pltpu.SemaphoreType.DMA
    spec = pl.BlockSpec(memory_space=pltpu.VMEM)
    return pl.pallas_call(
        kernel,
        out_shape=(
            jax.ShapeDtypeStruct((TB, DC), BF16),
            jax.ShapeDtypeStruct((TB, HC), BF16),
            jax.ShapeDtypeStruct((TB, HC), BF16),
            jax.ShapeDtypeStruct((TB, HC), BF16),
            jax.ShapeDtypeStruct((TB, DC), BF16),
        ),
        in_specs=[spec] * 5,
        out_specs=(spec,) * 5,
        scratch_shapes=[
            vm((ZT, HC)), vm((ZT, HC)), vm((ZT, HC)), vm((ZT, DC)), vm((ZT, DC)), vm((HC, ZT)), vm((HC, ZT)),
            vm((HC, ZT)), vm((TB, ZT)), vm((TB, ZT)), vm((TB, ZT)),
            *[vm((8, ZT), F32) for _ in range(9)],
            vm((ZT, ZT)), vm((4, TB, ZT)), vm((4, PB, ZT)), vm((4, PB, ZT)), vm((4, TB, ZT)), vm((TB, ZT)),
            vm((TB, ZT)), vm((HC, ZT)), vm((2, 8, ZT), F32), vm((8, ZT), F32),
            vm((ZT, HD), F32), vm((ZT, HD), F32), vm((ZT, HC)), vm((ZT, HC)), vm((ZT, HC)),
            vm((2, PB, HC)), vm((2, PB, HC)), vm((2, TB, HC)), vm((2, TB, HC)),
            vm((2, TB, HC)), vm((TB, HC)), vm((TB, HC)),
            vm((ZT, DC)), vm((2, TB, DC)), vm((TB, DC)), vm((TB, DC)),
            vm((ZT, DC)), vm((2, PB, DC)), vm((2, TB, DC)),
            dma((6, 4)), dma((6, 4)), dma((6, 3)), dma((6, 3)), dma((4, 2)), dma((4,)), dma((4,)), dma((8,)),
            dma((5,)), dma((4,)), dma((8,)), dma((6,)), dma((6,)), dma((2, 3, 2)), dma((2, 3, 2)),
        ],
        compiler_params=pltpu.CompilerParams(
            collective_id=0, has_side_effects=True, vmem_limit_bytes=60 * 1024 * 1024
        ),
    )(queries, keys_tile, values_tile, out_weight, out_grad)


def solution(mesh):
    spec = P("row", "col")
    return jax.shard_map(
        per_device, mesh=mesh, in_specs=(spec,) * 5, out_specs=(spec,) * 5, check_vma=False
    )
```

```python
import jax
import jax.numpy as jnp
from jax import lax
from jax.experimental import pallas as pl
from jax.experimental.pallas import tpu as pltpu
from jax.sharding import PartitionSpec as P

HD = 128
NH = 3
TB = 192
ZT = 4 * TB
HC = NH * HD
DC = 768
PB = HC // 4
QT = 256
SCALE = HD ** (-0.5)
LOG2E = 1.4426950408889634
MESH = pl.DeviceIdType.MESH
F32 = jnp.float32
BF16 = jnp.bfloat16


def dot(a, b, ca, cb):
    return lax.dot_general(a, b, (((ca,), (cb,)), ((), ())), preferred_element_type=F32)


def kernel(
    q_ref, k_ref, v_ref, w_ref, g_ref,
    mixed_o, dq_o, dk_o, dv_o, wg_o,
    k_all, v_all, q_all, w_all, g_all, kt, vt,
    o_st, o_core, o_chip, o_far, lse_own, lse_core, lse_chip, lse_far, lse_c, w_own, w_core, w_chip, w_far,
    attn_all, d_st, d_r1, d_sum, d_rc, d_up, d_yl, do_all, dp_all, delta,
    kacc, vacc, k_st, v_st, q_st, k_r1, v_r1, k_r2, v_r2, q_core, q_up, q_rc,
    m_st, m_core, m_up, m_rc, w_st, w_r1, w_r2,
    sz, rz, sy, ry, sd, rx, sl, rd, sa, ra, rh, sb, rb, sk, rk, sq, rq, p_all,
):
    row, col = lax.axis_index("row"), lax.axis_index("col")
    z, q = row // 4, row % 4
    yh, co = q // 2, q % 2
    yl, x = col // 4, col % 4
    inner = x % 2 == yh
    outer = x % 2 != yh
    x_up, x_dn, other_yl = yl * 4 + (x + 1) % 4, yl * 4 + (x + 3) % 4, (1 - yl) * 4 + x
    z_up, z_dn, z_op = (z + 1) % 4, (z + 3) % 4, (z + 2) % 4
    up, dn = z_up * 4 + q, z_dn * 4 + q

    def ypeer(j):
        a = yh if j < 2 else 1 - yh
        b = co if j % 2 == 0 else 1 - co
        return a * 2 + b

    core = z * 4 + ypeer(1)
    far = z * 4 + ypeer(2)

    def copy(src, dst, ss, rs, r, c):
        return pltpu.make_async_remote_copy(
            src_ref=src, dst_ref=dst, send_sem=ss, recv_sem=rs, device_id=(r, c), device_id_type=MESH
        )

    def send(src, dst, ss, rs, r, c):
        d = copy(src, dst, ss, rs, r, c)
        d.start()
        return d

    def recv(dst, ss, rs):
        copy(dst, dst, ss, rs, row, col).wait_recv()

    def left(src, ss, rs):
        copy(src, src, ss, rs, row, col).wait_send()

    def rows(i, n):
        return pl.ds(pl.multiple_of(i * n, n), n)

    barrier = pltpu.get_barrier_semaphore()

    def greet(r, c):
        pl.semaphore_signal(barrier, inc=1, device_id=(r, c), device_id_type=MESH)

    for r in (up, dn, core, far):
        greet(r, col)
    for c in (x_up, x_dn, other_yl):
        greet(row, c)
    pl.semaphore_wait(barrier, 7)

    sends = []

    def lower(b):
        return rows(2 * b, PB)

    def upper(b):
        return rows(2 * b + 1, PB)

    def z_start(i, src, dst):
        to = dst.at[rows(z, TB), :]
        sends.append(send(src, to, sz.at[i, 0], rz.at[i, 0], up, col))
        sends.append(send(src, to, sz.at[i, 1], rz.at[i, 1], dn, col))

    def z_pass(i, dst):
        recv(dst.at[rows(z_dn, TB), :], sz.at[i, 0], rz.at[i, 0])
        a = dst.at[lower(z_dn), :]
        sends.append(send(a, a, sz.at[i, 2], rz.at[i, 2], up, col))
        recv(dst.at[rows(z_up, TB), :], sz.at[i, 1], rz.at[i, 1])
        b = dst.at[upper(z_up), :]
        sends.append(send(b, b, sz.at[i, 3], rz.at[i, 3], dn, col))

    def z_last(i, dst):
        recv(dst.at[lower(z_op), :], sz.at[i, 2], rz.at[i, 2])
        recv(dst.at[upper(z_op), :], sz.at[i, 3], rz.at[i, 3])

    def to_y(i, j, src, dst):
        sends.append(send(src, dst, sy.at[i, j - 1], ry.at[i, j - 1], far if j == 2 else core, col))

    def from_y(i, j, dst):
        recv(dst, sy.at[i, j - 1], ry.at[i, j - 1])

    z_start(0, k_ref, k_all)
    to_y(0, 2, q_ref, q_all.at[rows(q, TB), :])
    to_y(0, 1, q_ref, q_all.at[rows(q, TB), :])
    z_start(1, v_ref, v_all)
    to_y(1, 2, g_ref, g_all.at[rows(q, TB), :])
    to_y(1, 1, g_ref, g_all.at[rows(q, TB), :])
    k_all[rows(z, TB), :] = k_ref[...]
    v_all[rows(z, TB), :] = v_ref[...]
    q_all[rows(q, TB), :] = q_ref[...]
    g_all[rows(q, TB), :] = g_ref[...]
    w_all[rows(z, TB), :] = w_ref[...]
    lse_own[...] = jnp.zeros_like(lse_own)
    dp_all[co] = jnp.zeros((8, ZT), F32)

    part_far = rows(ypeer(2), TB)
    z_pass(0, k_all)
    from_y(0, 2, q_all.at[part_far, :])
    to_y(0, 3, q_all.at[part_far, :], q_all.at[part_far, :])
    z_pass(1, v_all)
    z_start(2, w_ref, w_all)
    for j in (1, 3):
        from_y(0, j, q_all.at[rows(ypeer(j), TB), :])
    z_last(0, k_all)
    kt[...] = k_all[...].T
    from_y(1, 2, g_all.at[part_far, :])
    to_y(1, 3, g_all.at[part_far, :], g_all.at[part_far, :])
    z_last(1, v_all)
    vt[...] = v_all[...].T

    def forward(i, carry):
        h, t = i // 3, i % 3
        hs, ts = rows(h, HD), rows(t, QT)
        s = dot(k_all[:, hs], q_all[ts, hs], 1, 1)
        top = jnp.max(s, axis=0, keepdims=True)
        p = jnp.exp2((s - top) * (SCALE * LOG2E))
        total = jnp.sum(p, axis=0, keepdims=True)
        o = dot(vt[hs, :], p.astype(BF16), 1, 0)
        o_st[hs, ts] = (o / total).astype(BF16)
        lse_own[pl.ds(h, 1), ts] = top * (SCALE * LOG2E) + jnp.log2(total)
        return carry

    def slot_of(c, other):
        return 2 * (1 - yl if other else yl) + c % 4 // 2

    slot_a, slot_b = slot_of(x, False), slot_of(x, True)

    def d_attn(n, zp):
        d_st[zp] = dot(w_all[rows(zp, TB), :], g_all[...], 1, 1).astype(BF16)
        tx = 2 * (zp % 2) + yh
        piece = jnp.where(zp // 2 == yl, 0, 1)

        @pl.when(inner & (tx != x))
        def _():
            send(d_st.at[zp, :PB], d_r1.at[piece], sd.at[n, 0], rx.at[piece], row, x_up)
            send(d_st.at[zp, PB:], d_r1.at[2 + piece], sd.at[n, 1], rx.at[2 + piece], row, x_dn)

        @pl.when(outer & (tx == (x + 1) % 4))
        def _():
            send(d_st.at[zp, PB:], d_rc.at[piece, PB:], sd.at[n, 0], rd.at[2 * piece + 1], row, x_up)

        @pl.when(outer & (tx == (x + 3) % 4))
        def _():
            send(d_st.at[zp, :PB], d_rc.at[2 + piece, :PB], sd.at[n, 0], rd.at[4 + 2 * piece], row, x_dn)

    lax.fori_loop(0, 6, forward, 0)
    for j in (1, 3):
        from_y(1, j, g_all.at[rows(ypeer(j), TB), :])
    z_pass(2, w_all)
    d_attn(0, z)
    lax.fori_loop(6, 9, forward, 0)

    to_y(3, 1, lse_own, lse_core)
    to_y(2, 1, o_st.at[rows(1 - co, TB), :], o_core)
    d_attn(1, z_dn)
    d_attn(2, z_up)

    def both(a, b):
        top = jnp.maximum(a, b)
        lse = top + jnp.log2(jnp.exp2(a - top) + jnp.exp2(b - top))
        return lse, jnp.exp2(a - lse), jnp.exp2(b - lse)

    def pieces():
        for i in range(3):
            yield (
                pl.ds((3 * co + i) // 2, 1),
                slice(i * 64, (i + 1) * 64),
                pl.ds(pl.multiple_of(co * TB + i * 64, 64), 64),
                pl.ds(pl.multiple_of(slot_a * TB + i * 64, 64), 64),
            )

    from_y(3, 1, lse_core)
    lse_chip[...], w_own[...], w_core[...] = both(lse_own[...], lse_core[...])
    to_y(3, 2, lse_chip, lse_far)
    from_y(2, 1, o_core)
    for head, part, src, to in pieces():
        o_chip[part, :] = (
            w_own[head, :] * o_st[src, :].astype(F32) + w_core[head, :] * o_core[part, :].astype(F32)
        ).astype(BF16)

    @pl.when(outer)
    def _():
        send(o_chip, o_far, sb.at[1], rb.at[1], far, col)

    z_last(2, w_all)
    d_attn(3, z_op)
    from_y(3, 2, lse_far)
    lse_c[...], w_chip[...], w_far[...] = both(lse_chip[...], lse_far[...])
    half = rows(co, TB)

    def again(i, carry):
        h, t = i // 3, i % 3
        hs, ts = rows(h, HD), rows(t, QT)
        s = dot(k_all[:, hs], q_all[ts, hs], 1, 1)
        p_all[rows(h, ZT), ts] = jnp.exp2(s * (SCALE * LOG2E) - lse_c[pl.ds(h, 1), ts]).astype(BF16)
        return carry

    def half_of(b, i):
        return rows(2 * b + i, PB)

    @pl.when(inner)
    def _():
        lax.fori_loop(0, 9, again, 0)
        recv(o_far, sb.at[1], rb.at[1])
        for head, part, src, to in pieces():
            attn_all[to, :] = (
                w_chip[head, :] * o_chip[part, :].astype(F32) + w_far[head, :] * o_far[part, :].astype(F32)
            ).astype(BF16)
        a, b = attn_all.at[rows(slot_a, TB), :], attn_all.at[rows(slot_b, TB), :]
        send(a, a, sa.at[0], ra.at[slot_a], row, other_yl)
        send(a, a, sa.at[1], ra.at[slot_a], row, x_up)
        send(a, a, sa.at[2], ra.at[slot_a], row, x_dn)
        for i in (2, 3, 6, 7):
            recv(d_rc.at[i // 4 * 2 + 1, i % 2 * PB : (i % 2 + 1) * PB], sd.at[0, 0], rd.at[i])
        d_up[...] = (d_st[slot_b].astype(F32) + d_rc[1].astype(F32) + d_rc[3].astype(F32)).astype(BF16)
        send(d_up, d_yl, sb.at[0], rb.at[0], row, other_yl)
        recv(b, sa.at[0], ra.at[slot_b])
        send(b, b, sa.at[3], ra.at[slot_b], row, x_up)
        send(b, b, sa.at[4], ra.at[slot_b], row, x_dn)
        for i in (0, 1, 4, 5):
            recv(d_rc.at[i // 4 * 2, i % 2 * PB : (i % 2 + 1) * PB], sd.at[0, 0], rd.at[i])
        recv(d_yl, sb.at[0], rb.at[0])
        do_all[half, :] = (
            d_st[slot_a].astype(F32) + d_rc[0].astype(F32) + d_rc[2].astype(F32) + d_yl[...].astype(F32)
        ).astype(BF16)
        send(do_all.at[half, :], do_all.at[half, :], sb.at[2], rb.at[2], far, col)
        send(do_all.at[half, :], do_all.at[half, :], sb.at[3], rb.at[3], core, col)
        for head, part, src, to in pieces():
            dp_all[co, head, :] += jnp.sum(
                do_all[src, :].astype(F32) * attn_all[to, :].astype(F32), axis=0, keepdims=True
            )
        send(dp_all.at[co], dp_all.at[co], sb.at[4], rb.at[4], far, col)
        send(dp_all.at[co], dp_all.at[co], sb.at[5], rb.at[5], core, col)

    @pl.when(outer)
    def _():
        for p in (1, 0):
            s_up, s_dn = slot_of(x + 1, p == 1), slot_of(x + 3, p == 1)
            recv(d_r1.at[p], sd.at[0, 0], rx.at[p])
            d_sum[p] = (d_st[s_up, :PB].astype(F32) + d_r1[p].astype(F32)).astype(BF16)
            send(d_sum.at[p], d_rc.at[p, :PB], sl.at[p], rd.at[2 * p], row, x_up)
            recv(d_r1.at[2 + p], sd.at[0, 0], rx.at[2 + p])
            d_sum[2 + p] = (d_st[s_dn, PB:].astype(F32) + d_r1[2 + p].astype(F32)).astype(BF16)
            send(d_sum.at[2 + p], d_rc.at[2 + p, PB:], sl.at[2 + p], rd.at[4 + 2 * p + 1], row, x_dn)
        lax.fori_loop(0, 9, again, 0)
        for p in range(2):
            s_up, s_dn = slot_of(x + 1, p == 1), slot_of(x + 3, p == 1)
            recv(attn_all.at[rows(s_dn, TB), :], sa.at[0], ra.at[s_dn])
            a = attn_all.at[half_of(s_dn, 0), :]
            send(a, a, sa.at[p], rh.at[2 * s_dn], row, x_up)
            recv(attn_all.at[rows(s_up, TB), :], sa.at[0], ra.at[s_up])
            b = attn_all.at[half_of(s_up, 1), :]
            send(b, b, sa.at[2 + p], rh.at[2 * s_up + 1], row, x_dn)

    def z_add(st, r1, r2, hs, ss, rs):
        recv(r1.at[0, :, hs], ss(0), rs(0))
        a, b = lower(z_up), upper(z_dn)
        st[a, hs] = (st[a, hs].astype(F32) + r1[0, :, hs].astype(F32)).astype(BF16)
        send(st.at[rows(z_up, TB), hs], r2.at[0, :, hs], ss(2), rs(2), up, col)
        recv(r1.at[1, :, hs], ss(1), rs(1))
        st[b, hs] = (st[b, hs].astype(F32) + r1[1, :, hs].astype(F32)).astype(BF16)
        send(st.at[rows(z_dn, TB), hs], r2.at[1, :, hs], ss(3), rs(3), dn, col)

    def z_sum(st, r2, hs, ss, rs):
        recv(r2.at[0, :, hs], ss(2), rs(2))
        recv(r2.at[1, :, hs], ss(3), rs(3))
        return (
            st[rows(z, TB), hs].astype(F32) + r2[0, :, hs].astype(F32) + r2[1, :, hs].astype(F32)
        ).astype(BF16)

    def z_left(st, r1, r2, hs, ss, rs):
        for j in range(2):
            left(r1.at[0, :, hs], ss(j), rs(j))
            left(r2.at[0, :, hs], ss(2 + j), rs(2 + j))

    every = slice(None)

    def w_sems(sem):
        return lambda j: sem.at[3, j]

    def weight_part(b):
        w_st[rows(b, TB), :] = dot(attn_all[rows(b, TB), :], g_all[...], 1, 0).astype(BF16)

    @pl.when(inner)
    def _():
        for p in range(2):
            b = slot_of(x + 2, p == 1)
            for i in range(2):
                recv(attn_all.at[half_of(b, i), :], sa.at[0], rh.at[2 * b + i])

    weight_part(z_op)
    send(w_st.at[lower(z_op), :], w_r1.at[0], sz.at[3, 0], rz.at[3, 0], up, col)
    send(w_st.at[upper(z_op), :], w_r1.at[1], sz.at[3, 1], rz.at[3, 1], dn, col)
    weight_part(z_up)
    weight_part(z_dn)

    @pl.when(outer)
    def _():
        recv(do_all.at[half, :], sb.at[2], rb.at[2])
        send(do_all.at[half, :], do_all.at[half, :], sb.at[3], rb.at[3], core, col)
        recv(dp_all.at[co], sb.at[4], rb.at[4])
        send(dp_all.at[co], dp_all.at[co], sb.at[5], rb.at[5], core, col)

    def mixed_part(i, carry):
        m_st[rows(i, QT), :] = dot(attn_all[:, rows(i, QT)], w_all[...], 0, 0).astype(BF16)
        return carry

    lax.fori_loop(0, 3, mixed_part, 0)
    to_y(5, 3, m_st.at[rows(ypeer(3), TB), :], m_core.at[1])
    to_y(5, 1, m_st.at[rows(ypeer(1), TB), :], m_core.at[0])
    weight_part(z)

    recv(do_all.at[rows(1 - co, TB), :], sb.at[3], rb.at[3])
    recv(dp_all.at[1 - co], sb.at[5], rb.at[5])
    delta[...] = dp_all[0] + dp_all[1]

    def k_sems(sem, i, h):
        return lambda j: sem.at[i, h, j]

    def head_next(h):
        hs = rows(h, HD)
        recv(q_core.at[1, :, hs], sq.at[h, 2], rq.at[h, 2])
        q_up[:, hs] = (q_st[part_far, hs].astype(F32) + q_core[1, :, hs].astype(F32)).astype(BF16)
        send(q_up.at[:, hs], q_rc.at[:, hs], sq.at[h, 1], rq.at[h, 1], far, col)
        z_add(v_st, v_r1, v_r2, hs, k_sems(sk, 0, h), k_sems(rk, 0, h))
        z_add(k_st, k_r1, k_r2, hs, k_sems(sk, 1, h), k_sems(rk, 1, h))

    def backward(h, carry):
        hs = rows(h, HD)
        kh = k_all[:, hs]
        vh = v_all[:, hs]
        for t in range(3):
            ts = slice(t * QT, (t + 1) * QT)
            qh = q_all[ts, hs]
            doh = do_all[hs, ts]
            p = p_all[rows(h, ZT), ts]
            dprob = dot(vh, doh, 1, 0)
            ds = (p.astype(F32) * (dprob - delta[pl.ds(h, 1), ts]) * SCALE).astype(BF16)
            dvt = dot(p, doh, 1, 1)
            dkt = dot(ds, qh, 1, 0)
            if t == 0:
                vacc[...] = dvt
                kacc[...] = dkt
            else:
                vacc[...] += dvt
                kacc[...] += dkt
            q_st[ts, hs] = dot(kt[hs, :], ds, 1, 0).T.astype(BF16)
        v_st[:, hs] = vacc[...].astype(BF16)
        k_st[:, hs] = kacc[...].astype(BF16)
        for i, (st, r1) in enumerate(((v_st, v_r1), (k_st, k_r1))):
            send(st.at[lower(z_op), hs], r1.at[0, :, hs], sk.at[i, h, 0], rk.at[i, h, 0], up, col)
            send(st.at[upper(z_op), hs], r1.at[1, :, hs], sk.at[i, h, 1], rk.at[i, h, 1], dn, col)
        send(q_st.at[rows(ypeer(3), TB), hs], q_core.at[1, :, hs], sq.at[h, 2], rq.at[h, 2], core, col)
        send(q_st.at[rows(ypeer(1), TB), hs], q_core.at[0, :, hs], sq.at[h, 0], rq.at[h, 0], core, col)

        @pl.when(h == 0)
        def _():
            recv(m_core.at[1], sy.at[5, 2], ry.at[5, 2])
            m_up[...] = (m_st[part_far, :].astype(F32) + m_core[1].astype(F32)).astype(BF16)
            send(m_up, m_rc, sy.at[5, 1], ry.at[5, 1], far, col)
            z_add(w_st, w_r1, w_r2, every, w_sems(sz), w_sems(rz))

        @pl.when(h > 0)
        def _():
            head_next(h - 1)

        return carry

    lax.fori_loop(0, NH, backward, 0)
    head_next(NH - 1)

    from_y(5, 1, m_core.at[0])
    from_y(5, 2, m_rc)
    mixed_o[...] = (m_st[rows(q, TB), :].astype(F32) + m_core[0].astype(F32) + m_rc[...].astype(F32)).astype(BF16)
    wg_o[...] = z_sum(w_st, w_r2, every, w_sems(sz), w_sems(rz))
    for h in range(NH):
        hs = slice(h * HD, (h + 1) * HD)
        recv(q_core.at[0, :, hs], sq.at[h, 0], rq.at[h, 0])
        recv(q_rc.at[:, hs], sq.at[h, 1], rq.at[h, 1])
        dq_o[:, hs] = (
            q_st[rows(q, TB), hs].astype(F32) + q_core[0, :, hs].astype(F32) + q_rc[:, hs].astype(F32)
        ).astype(BF16)
        dv_o[:, hs] = z_sum(v_st, v_r2, hs, k_sems(sk, 0, h), k_sems(rk, 0, h))
        dk_o[:, hs] = z_sum(k_st, k_r2, hs, k_sems(sk, 1, h), k_sems(rk, 1, h))

    for d in sends:
        d.wait_send()
    left(do_all.at[half, :], sb.at[3], rb.at[3])
    left(dp_all.at[0], sb.at[5], rb.at[5])

    @pl.when(inner)
    def _():
        for n, zp in enumerate((z, z_dn, z_up, z_op)):
            @pl.when(2 * (zp % 2) + yh != x)
            def _():
                left(d_st.at[0, :PB], sd.at[n, 0], rx.at[0])
                left(d_st.at[0, :PB], sd.at[n, 1], rx.at[0])

        for i in range(5):
            left(attn_all.at[rows(0, TB), :], sa.at[i], ra.at[0])
        left(d_up, sb.at[0], rb.at[0])
        left(do_all.at[half, :], sb.at[2], rb.at[2])
        left(dp_all.at[0], sb.at[4], rb.at[4])

    @pl.when(outer)
    def _():
        for n in range(4):
            left(d_st.at[0, :PB], sd.at[n, 0], rx.at[0])
            left(d_sum.at[n], sl.at[n], rx.at[0])
            left(attn_all.at[half_of(0, 0), :], sa.at[n], ra.at[0])
        left(o_chip, sb.at[1], rb.at[1])

    left(m_up, sy.at[5, 1], ry.at[5, 1])
    z_left(w_st, w_r1, w_r2, every, w_sems(sz), w_sems(rz))
    for h in range(NH):
        hs = slice(h * HD, (h + 1) * HD)
        for j in range(3):
            left(q_rc.at[:, hs], sq.at[h, j], rq.at[h, j])
        z_left(v_st, v_r1, v_r2, hs, k_sems(sk, 0, h), k_sems(rk, 0, h))
        z_left(k_st, k_r1, k_r2, hs, k_sems(sk, 1, h), k_sems(rk, 1, h))


def per_device(queries, keys_tile, values_tile, out_weight, out_grad):
    def vm(shape, dtype=BF16):
        return pltpu.VMEM(shape, dtype)

    dma = pltpu.SemaphoreType.DMA
    spec = pl.BlockSpec(memory_space=pltpu.VMEM)
    return pl.pallas_call(
        kernel,
        out_shape=(
            jax.ShapeDtypeStruct((TB, DC), BF16),
            jax.ShapeDtypeStruct((TB, HC), BF16),
            jax.ShapeDtypeStruct((TB, HC), BF16),
            jax.ShapeDtypeStruct((TB, HC), BF16),
            jax.ShapeDtypeStruct((TB, DC), BF16),
        ),
        in_specs=[spec] * 5,
        out_specs=(spec,) * 5,
        scratch_shapes=[
            vm((ZT, HC)), vm((ZT, HC)), vm((ZT, HC)), vm((ZT, DC)), vm((ZT, DC)), vm((HC, ZT)), vm((HC, ZT)),
            vm((HC, ZT)), vm((TB, ZT)), vm((TB, ZT)), vm((TB, ZT)),
            *[vm((8, ZT), F32) for _ in range(9)],
            vm((ZT, ZT)), vm((4, TB, ZT)), vm((4, PB, ZT)), vm((4, PB, ZT)), vm((4, TB, ZT)), vm((TB, ZT)),
            vm((TB, ZT)), vm((HC, ZT)), vm((2, 8, ZT), F32), vm((8, ZT), F32),
            vm((ZT, HD), F32), vm((ZT, HD), F32), vm((ZT, HC)), vm((ZT, HC)), vm((ZT, HC)),
            vm((2, PB, HC)), vm((2, PB, HC)), vm((2, TB, HC)), vm((2, TB, HC)),
            vm((2, TB, HC)), vm((TB, HC)), vm((TB, HC)),
            vm((ZT, DC)), vm((2, TB, DC)), vm((TB, DC)), vm((TB, DC)),
            vm((ZT, DC)), vm((2, PB, DC)), vm((2, TB, DC)),
            dma((6, 4)), dma((6, 4)), dma((6, 3)), dma((6, 3)), dma((4, 2)), dma((4,)), dma((4,)), dma((8,)),
            dma((5,)), dma((4,)), dma((8,)), dma((6,)), dma((6,)), dma((2, 3, 4)), dma((2, 3, 4)),
            dma((3, 3)), dma((3, 3)), vm((NH * ZT, ZT)),
        ],
        compiler_params=pltpu.CompilerParams(
            collective_id=0, has_side_effects=True, vmem_limit_bytes=60 * 1024 * 1024
        ),
    )(queries, keys_tile, values_tile, out_weight, out_grad)


def solution(mesh):
    spec = P("row", "col")
    return jax.shard_map(
        per_device, mesh=mesh, in_specs=(spec,) * 5, out_specs=(spec,) * 5, check_vma=False
    )
```

```python
import jax
import jax.numpy as jnp
from jax import lax
from jax.experimental import pallas as pl
from jax.experimental.pallas import tpu as pltpu
from jax.sharding import PartitionSpec as P

HD = 128
NH = 3
TB = 192
ZT = 4 * TB
HC = NH * HD
DC = 768
PB = HC // 4
QT = 256
SCALE = HD ** (-0.5)
LOG2E = 1.4426950408889634
MESH = pl.DeviceIdType.MESH
F32 = jnp.float32
BF16 = jnp.bfloat16


def dot(a, b, ca, cb):
    return lax.dot_general(a, b, (((ca,), (cb,)), ((), ())), preferred_element_type=F32)


def kernel(
    q_ref, k_ref, v_ref, w_ref, g_ref,
    mixed_o, dq_o, dk_o, dv_o, wg_o,
    k_all, v_all, q_all, w_all, g_all, kt, vt,
    o_st, o_core, o_chip, o_far, lse_own, lse_core, lse_chip, lse_far, lse_c, w_own, w_core, w_chip, w_far,
    attn_all, d_st, d_r1, d_sum, d_rc, d_up, d_yl, do_all, dp_all, delta,
    kacc, vacc, k_st, v_st, q_st, k_r1, v_r1, k_r2, v_r2, q_core, q_up, q_rc,
    m_st, m_core, m_up, m_rc, w_st, w_rc,
    sz, rz, sy, ry, sd, rx, sl, rd, sa, ra, rh, sb, rb, sk, rk, sq, rq, sw, rw, p_all,
):
    row, col = lax.axis_index("row"), lax.axis_index("col")
    z, q = row // 4, row % 4
    yh, co = q // 2, q % 2
    yl, x = col // 4, col % 4
    inner = x % 2 == yh
    outer = x % 2 != yh
    x_up, x_dn, other_yl = yl * 4 + (x + 1) % 4, yl * 4 + (x + 3) % 4, (1 - yl) * 4 + x
    z_up, z_dn, z_op = (z + 1) % 4, (z + 3) % 4, (z + 2) % 4
    up, dn = z_up * 4 + q, z_dn * 4 + q

    def ypeer(j):
        a = yh if j < 2 else 1 - yh
        b = co if j % 2 == 0 else 1 - co
        return a * 2 + b

    core = z * 4 + ypeer(1)
    far = z * 4 + ypeer(2)

    def copy(src, dst, ss, rs, r, c):
        return pltpu.make_async_remote_copy(
            src_ref=src, dst_ref=dst, send_sem=ss, recv_sem=rs, device_id=(r, c), device_id_type=MESH
        )

    def send(src, dst, ss, rs, r, c):
        d = copy(src, dst, ss, rs, r, c)
        d.start()
        return d

    def recv(dst, ss, rs):
        copy(dst, dst, ss, rs, row, col).wait_recv()

    def left(src, ss, rs):
        copy(src, src, ss, rs, row, col).wait_send()

    def rows(i, n):
        return pl.ds(pl.multiple_of(i * n, n), n)

    barrier = pltpu.get_barrier_semaphore()

    def greet(r, c):
        pl.semaphore_signal(barrier, inc=1, device_id=(r, c), device_id_type=MESH)

    for r in (up, dn, z_op * 4 + q, core, far):
        greet(r, col)
    for c in (x_up, x_dn, other_yl):
        greet(row, c)
    pl.semaphore_wait(barrier, 8)

    sends = []

    def lower(b):
        return rows(2 * b, PB)

    def upper(b):
        return rows(2 * b + 1, PB)

    def z_start(i, src, dst):
        to = dst.at[rows(z, TB), :]
        sends.append(send(src, to, sz.at[i, 0], rz.at[i, 0], up, col))
        sends.append(send(src, to, sz.at[i, 1], rz.at[i, 1], dn, col))

    def z_pass(i, dst):
        recv(dst.at[rows(z_dn, TB), :], sz.at[i, 0], rz.at[i, 0])
        a = dst.at[lower(z_dn), :]
        sends.append(send(a, a, sz.at[i, 2], rz.at[i, 2], up, col))
        recv(dst.at[rows(z_up, TB), :], sz.at[i, 1], rz.at[i, 1])
        b = dst.at[upper(z_up), :]
        sends.append(send(b, b, sz.at[i, 3], rz.at[i, 3], dn, col))

    def z_last(i, dst):
        recv(dst.at[lower(z_op), :], sz.at[i, 2], rz.at[i, 2])
        recv(dst.at[upper(z_op), :], sz.at[i, 3], rz.at[i, 3])

    def to_y(i, j, src, dst):
        sends.append(send(src, dst, sy.at[i, j - 1], ry.at[i, j - 1], far if j == 2 else core, col))

    def from_y(i, j, dst):
        recv(dst, sy.at[i, j - 1], ry.at[i, j - 1])

    z_start(0, k_ref, k_all)
    to_y(0, 2, q_ref, q_all.at[rows(q, TB), :])
    to_y(0, 1, q_ref, q_all.at[rows(q, TB), :])
    z_start(1, v_ref, v_all)
    to_y(1, 2, g_ref, g_all.at[rows(q, TB), :])
    to_y(1, 1, g_ref, g_all.at[rows(q, TB), :])
    k_all[rows(z, TB), :] = k_ref[...]
    v_all[rows(z, TB), :] = v_ref[...]
    q_all[rows(q, TB), :] = q_ref[...]
    g_all[rows(q, TB), :] = g_ref[...]
    w_all[rows(z, TB), :] = w_ref[...]
    lse_own[...] = jnp.zeros_like(lse_own)
    dp_all[co] = jnp.zeros((8, ZT), F32)

    part_far = rows(ypeer(2), TB)
    z_pass(0, k_all)
    from_y(0, 2, q_all.at[part_far, :])
    to_y(0, 3, q_all.at[part_far, :], q_all.at[part_far, :])
    z_pass(1, v_all)
    z_start(2, w_ref, w_all)
    for j in (1, 3):
        from_y(0, j, q_all.at[rows(ypeer(j), TB), :])
    z_last(0, k_all)
    kt[...] = k_all[...].T
    from_y(1, 2, g_all.at[part_far, :])
    to_y(1, 3, g_all.at[part_far, :], g_all.at[part_far, :])
    z_last(1, v_all)
    vt[...] = v_all[...].T

    def forward(h, carry):
        hs = rows(h, HD)
        kh, vh = k_all[:, hs], vt[hs, :]
        for t in range(3):
            ts = slice(t * QT, (t + 1) * QT)
            s = dot(kh, q_all[ts, hs], 1, 1)
            top = jnp.max(s, axis=0, keepdims=True)
            p = jnp.exp2((s - top) * (SCALE * LOG2E))
            total = jnp.sum(p, axis=0, keepdims=True)
            o = dot(vh, p.astype(BF16), 1, 0)
            o_st[hs, ts] = (o / total).astype(BF16)
            lse_own[pl.ds(h, 1), ts] = top * (SCALE * LOG2E) + jnp.log2(total)
        return carry

    def slot_of(c, other):
        return 2 * (1 - yl if other else yl) + c % 4 // 2

    slot_a, slot_b = slot_of(x, False), slot_of(x, True)

    def d_attn(n, zp):
        d_st[zp] = dot(w_all[rows(zp, TB), :], g_all[...], 1, 1).astype(BF16)
        tx = 2 * (zp % 2) + yh
        piece = jnp.where(zp // 2 == yl, 0, 1)

        @pl.when(inner & (tx != x))
        def _():
            send(d_st.at[zp, :PB], d_r1.at[piece], sd.at[n, 0], rx.at[piece], row, x_up)
            send(d_st.at[zp, PB:], d_r1.at[2 + piece], sd.at[n, 1], rx.at[2 + piece], row, x_dn)

        @pl.when(outer & (tx == (x + 1) % 4))
        def _():
            send(d_st.at[zp, PB:], d_rc.at[piece, PB:], sd.at[n, 0], rd.at[2 * piece + 1], row, x_up)

        @pl.when(outer & (tx == (x + 3) % 4))
        def _():
            send(d_st.at[zp, :PB], d_rc.at[2 + piece, :PB], sd.at[n, 0], rd.at[4 + 2 * piece], row, x_dn)

    lax.fori_loop(0, 2, forward, 0)
    for j in (1, 3):
        from_y(1, j, g_all.at[rows(ypeer(j), TB), :])
    z_pass(2, w_all)
    d_attn(0, z)
    lax.fori_loop(2, 3, forward, 0)

    to_y(3, 1, lse_own, lse_core)
    to_y(2, 1, o_st.at[rows(1 - co, TB), :], o_core)
    d_attn(1, z_dn)
    d_attn(2, z_up)

    def both(a, b):
        top = jnp.maximum(a, b)
        lse = top + jnp.log2(jnp.exp2(a - top) + jnp.exp2(b - top))
        return lse, jnp.exp2(a - lse), jnp.exp2(b - lse)

    def pieces():
        for i in range(3):
            yield (
                pl.ds((3 * co + i) // 2, 1),
                slice(i * 64, (i + 1) * 64),
                pl.ds(pl.multiple_of(co * TB + i * 64, 64), 64),
                pl.ds(pl.multiple_of(slot_a * TB + i * 64, 64), 64),
            )

    from_y(3, 1, lse_core)
    lse_chip[...], w_own[...], w_core[...] = both(lse_own[...], lse_core[...])
    to_y(3, 2, lse_chip, lse_far)
    from_y(2, 1, o_core)
    for head, part, src, to in pieces():
        o_chip[part, :] = (
            w_own[head, :] * o_st[src, :].astype(F32) + w_core[head, :] * o_core[part, :].astype(F32)
        ).astype(BF16)

    @pl.when(outer)
    def _():
        send(o_chip, o_far, sb.at[1], rb.at[1], far, col)

    z_last(2, w_all)
    d_attn(3, z_op)
    from_y(3, 2, lse_far)
    lse_c[...], w_chip[...], w_far[...] = both(lse_chip[...], lse_far[...])
    half = rows(co, TB)

    def again(h, carry):
        hs = rows(h, HD)
        kh = k_all[:, hs]
        for t in range(3):
            ts = slice(t * QT, (t + 1) * QT)
            s = dot(kh, q_all[ts, hs], 1, 1)
            p_all[rows(h, ZT), ts] = jnp.exp2(s * (SCALE * LOG2E) - lse_c[pl.ds(h, 1), ts]).astype(BF16)
        return carry

    def block(b, i):
        return attn_all.at[rows(2 * b + i, PB), :]

    def weight_part(b):
        w_st[rows(b, TB), :] = dot(attn_all[rows(b, TB), :], g_all[...], 1, 0).astype(BF16)

        @pl.when(b != z)
        def _():
            send(w_st.at[rows(b, TB), :], w_rc.at[z], sw.at[b], rw.at[z], b * 4 + q, col)

    @pl.when(inner)
    def _():
        lax.fori_loop(0, NH, again, 0)
        recv(o_far, sb.at[1], rb.at[1])
        for head, part, src, to in pieces():
            attn_all[to, :] = (
                w_chip[head, :] * o_chip[part, :].astype(F32) + w_far[head, :] * o_far[part, :].astype(F32)
            ).astype(BF16)
        def pass_on(b, i, n, to):
            send(block(b, i), block(b, i), sa.at[n], ra.at[2 * b + i], row, to)

        pass_on(slot_a, 0, 0, other_yl)
        pass_on(slot_a, 0, 2, x_up)
        pass_on(slot_a, 1, 4, x_dn)
        pass_on(slot_a, 1, 1, other_yl)
        pass_on(slot_a, 1, 3, x_up)
        pass_on(slot_a, 0, 5, x_dn)
        weight_part(slot_a)
        for i in (2, 3, 6, 7):
            recv(d_rc.at[i // 4 * 2 + 1, i % 2 * PB : (i % 2 + 1) * PB], sd.at[0, 0], rd.at[i])
        d_up[...] = (d_st[slot_b].astype(F32) + d_rc[1].astype(F32) + d_rc[3].astype(F32)).astype(BF16)
        send(d_up, d_yl, sb.at[0], rb.at[0], row, other_yl)
        recv(block(slot_b, 0), sa.at[0], ra.at[2 * slot_b])
        pass_on(slot_b, 0, 6, x_up)
        recv(block(slot_b, 1), sa.at[0], ra.at[2 * slot_b + 1])
        pass_on(slot_b, 1, 7, x_dn)
        pass_on(slot_b, 1, 8, x_up)
        pass_on(slot_b, 0, 9, x_dn)
        weight_part(slot_b)
        for i in (0, 1, 4, 5):
            recv(d_rc.at[i // 4 * 2, i % 2 * PB : (i % 2 + 1) * PB], sd.at[0, 0], rd.at[i])
        recv(d_yl, sb.at[0], rb.at[0])
        do_all[half, :] = (
            d_st[slot_a].astype(F32) + d_rc[0].astype(F32) + d_rc[2].astype(F32) + d_yl[...].astype(F32)
        ).astype(BF16)
        send(do_all.at[half, :], do_all.at[half, :], sb.at[2], rb.at[2], far, col)
        send(do_all.at[half, :], do_all.at[half, :], sb.at[3], rb.at[3], core, col)
        for head, part, src, to in pieces():
            dp_all[co, head, :] += jnp.sum(
                do_all[src, :].astype(F32) * attn_all[to, :].astype(F32), axis=0, keepdims=True
            )
        send(dp_all.at[co], dp_all.at[co], sb.at[4], rb.at[4], far, col)
        send(dp_all.at[co], dp_all.at[co], sb.at[5], rb.at[5], core, col)

    @pl.when(outer)
    def _():
        for p in (1, 0):
            s_up, s_dn = slot_of(x + 1, p == 1), slot_of(x + 3, p == 1)
            recv(d_r1.at[p], sd.at[0, 0], rx.at[p])
            d_sum[p] = (d_st[s_up, :PB].astype(F32) + d_r1[p].astype(F32)).astype(BF16)
            send(d_sum.at[p], d_rc.at[p, :PB], sl.at[p], rd.at[2 * p], row, x_up)
            recv(d_r1.at[2 + p], sd.at[0, 0], rx.at[2 + p])
            d_sum[2 + p] = (d_st[s_dn, PB:].astype(F32) + d_r1[2 + p].astype(F32)).astype(BF16)
            send(d_sum.at[2 + p], d_rc.at[2 + p, PB:], sl.at[2 + p], rd.at[4 + 2 * p + 1], row, x_dn)
        lax.fori_loop(0, NH, again, 0)
        for p in range(2):
            s_up, s_dn = slot_of(x + 1, p == 1), slot_of(x + 3, p == 1)
            recv(block(s_dn, 0), sa.at[0], ra.at[2 * s_dn])
            send(block(s_dn, 0), block(s_dn, 0), sa.at[p], rh.at[2 * s_dn], row, x_up)
            recv(block(s_up, 1), sa.at[0], ra.at[2 * s_up + 1])
            send(block(s_up, 1), block(s_up, 1), sa.at[2 + p], rh.at[2 * s_up + 1], row, x_dn)
            recv(block(s_dn, 1), sa.at[0], ra.at[2 * s_dn + 1])
            weight_part(s_dn)
            recv(block(s_up, 0), sa.at[0], ra.at[2 * s_up])
            weight_part(s_up)

    def z_add(st, r1, r2, hs, ss, rs):
        recv(r1.at[0, :, hs], ss(0), rs(0))
        a, b = lower(z_up), upper(z_dn)
        st[a, hs] = (st[a, hs].astype(F32) + r1[0, :, hs].astype(F32)).astype(BF16)
        send(st.at[rows(z_up, TB), hs], r2.at[0, :, hs], ss(2), rs(2), up, col)
        recv(r1.at[1, :, hs], ss(1), rs(1))
        st[b, hs] = (st[b, hs].astype(F32) + r1[1, :, hs].astype(F32)).astype(BF16)
        send(st.at[rows(z_dn, TB), hs], r2.at[1, :, hs], ss(3), rs(3), dn, col)

    def z_sum(st, r2, hs, ss, rs):
        recv(r2.at[0, :, hs], ss(2), rs(2))
        recv(r2.at[1, :, hs], ss(3), rs(3))
        return (
            st[rows(z, TB), hs].astype(F32) + r2[0, :, hs].astype(F32) + r2[1, :, hs].astype(F32)
        ).astype(BF16)

    def z_left(st, r1, r2, hs, ss, rs):
        for j in range(2):
            left(r1.at[0, :, hs], ss(j), rs(j))
            left(r2.at[0, :, hs], ss(2 + j), rs(2 + j))

    @pl.when(inner)
    def _():
        for p in range(2):
            b = slot_of(x + 2, p == 1)
            for i in range(2):
                recv(block(b, i), sa.at[0], rh.at[2 * b + i])
            weight_part(b)

    @pl.when(outer)
    def _():
        recv(do_all.at[half, :], sb.at[2], rb.at[2])
        send(do_all.at[half, :], do_all.at[half, :], sb.at[3], rb.at[3], core, col)
        recv(dp_all.at[co], sb.at[4], rb.at[4])
        send(dp_all.at[co], dp_all.at[co], sb.at[5], rb.at[5], core, col)

    def mixed_part(i, carry):
        m_st[rows(i, QT), :] = dot(attn_all[:, rows(i, QT)], w_all[...], 0, 0).astype(BF16)
        return carry

    lax.fori_loop(0, 3, mixed_part, 0)
    to_y(5, 3, m_st.at[rows(ypeer(3), TB), :], m_core.at[1])
    to_y(5, 1, m_st.at[rows(ypeer(1), TB), :], m_core.at[0])

    recv(do_all.at[rows(1 - co, TB), :], sb.at[3], rb.at[3])
    recv(dp_all.at[1 - co], sb.at[5], rb.at[5])
    delta[...] = dp_all[0] + dp_all[1]

    def k_sems(sem, i, h):
        return lambda j: sem.at[i, h, j]

    def head_next(h):
        hs = rows(h, HD)
        recv(q_core.at[1, :, hs], sq.at[h, 2], rq.at[h, 2])
        q_up[:, hs] = (q_st[part_far, hs].astype(F32) + q_core[1, :, hs].astype(F32)).astype(BF16)
        send(q_up.at[:, hs], q_rc.at[:, hs], sq.at[h, 1], rq.at[h, 1], far, col)
        z_add(v_st, v_r1, v_r2, hs, k_sems(sk, 0, h), k_sems(rk, 0, h))
        z_add(k_st, k_r1, k_r2, hs, k_sems(sk, 1, h), k_sems(rk, 1, h))

    def backward(h, carry):
        hs = rows(h, HD)
        kh = k_all[:, hs]
        vh = v_all[:, hs]
        for t in range(3):
            ts = slice(t * QT, (t + 1) * QT)
            qh = q_all[ts, hs]
            doh = do_all[hs, ts]
            p = p_all[rows(h, ZT), ts]
            dprob = dot(vh, doh, 1, 0)
            ds = (p.astype(F32) * (dprob - delta[pl.ds(h, 1), ts]) * SCALE).astype(BF16)
            dvt = dot(p, doh, 1, 1)
            dkt = dot(ds, qh, 1, 0)
            if t == 0:
                vacc[...] = dvt
                kacc[...] = dkt
            else:
                vacc[...] += dvt
                kacc[...] += dkt
            q_st[ts, hs] = dot(kt[hs, :], ds, 1, 0).T.astype(BF16)
        v_st[:, hs] = vacc[...].astype(BF16)
        k_st[:, hs] = kacc[...].astype(BF16)
        for i, (st, r1) in enumerate(((v_st, v_r1), (k_st, k_r1))):
            send(st.at[lower(z_op), hs], r1.at[0, :, hs], sk.at[i, h, 0], rk.at[i, h, 0], up, col)
            send(st.at[upper(z_op), hs], r1.at[1, :, hs], sk.at[i, h, 1], rk.at[i, h, 1], dn, col)
        send(q_st.at[rows(ypeer(3), TB), hs], q_core.at[1, :, hs], sq.at[h, 2], rq.at[h, 2], core, col)
        send(q_st.at[rows(ypeer(1), TB), hs], q_core.at[0, :, hs], sq.at[h, 0], rq.at[h, 0], core, col)

        @pl.when(h == 0)
        def _():
            recv(m_core.at[1], sy.at[5, 2], ry.at[5, 2])
            m_up[...] = (m_st[part_far, :].astype(F32) + m_core[1].astype(F32)).astype(BF16)
            send(m_up, m_rc, sy.at[5, 1], ry.at[5, 1], far, col)

        @pl.when(h > 0)
        def _():
            head_next(h - 1)

        return carry

    lax.fori_loop(0, NH, backward, 0)
    head_next(NH - 1)

    from_y(5, 1, m_core.at[0])
    from_y(5, 2, m_rc)
    mixed_o[...] = (m_st[rows(q, TB), :].astype(F32) + m_core[0].astype(F32) + m_rc[...].astype(F32)).astype(BF16)
    total = w_st[rows(z, TB), :].astype(F32)
    for d in (1, 3, 2):
        src = (z + d) % 4
        recv(w_rc.at[src], sw.at[0], rw.at[src])
        total += w_rc[src].astype(F32)
    wg_o[...] = total.astype(BF16)
    for h in range(NH):
        hs = slice(h * HD, (h + 1) * HD)
        recv(q_core.at[0, :, hs], sq.at[h, 0], rq.at[h, 0])
        recv(q_rc.at[:, hs], sq.at[h, 1], rq.at[h, 1])
        dq_o[:, hs] = (
            q_st[rows(q, TB), hs].astype(F32) + q_core[0, :, hs].astype(F32) + q_rc[:, hs].astype(F32)
        ).astype(BF16)
        dv_o[:, hs] = z_sum(v_st, v_r2, hs, k_sems(sk, 0, h), k_sems(rk, 0, h))
        dk_o[:, hs] = z_sum(k_st, k_r2, hs, k_sems(sk, 1, h), k_sems(rk, 1, h))

    for d in sends:
        d.wait_send()
    left(do_all.at[half, :], sb.at[3], rb.at[3])
    left(dp_all.at[0], sb.at[5], rb.at[5])

    @pl.when(inner)
    def _():
        for n, zp in enumerate((z, z_dn, z_up, z_op)):
            @pl.when(2 * (zp % 2) + yh != x)
            def _():
                left(d_st.at[0, :PB], sd.at[n, 0], rx.at[0])
                left(d_st.at[0, :PB], sd.at[n, 1], rx.at[0])

        for i in range(10):
            left(block(0, 0), sa.at[i], ra.at[0])
        left(d_up, sb.at[0], rb.at[0])
        left(do_all.at[half, :], sb.at[2], rb.at[2])
        left(dp_all.at[0], sb.at[4], rb.at[4])

    @pl.when(outer)
    def _():
        for n in range(4):
            left(d_st.at[0, :PB], sd.at[n, 0], rx.at[0])
            left(d_sum.at[n], sl.at[n], rx.at[0])
            left(block(0, 0), sa.at[n], ra.at[0])
        left(o_chip, sb.at[1], rb.at[1])

    left(m_up, sy.at[5, 1], ry.at[5, 1])
    for b in range(4):
        @pl.when(z != b)
        def _():
            left(w_rc.at[0], sw.at[b], rw.at[0])

    for h in range(NH):
        hs = slice(h * HD, (h + 1) * HD)
        for j in range(3):
            left(q_rc.at[:, hs], sq.at[h, j], rq.at[h, j])
        z_left(v_st, v_r1, v_r2, hs, k_sems(sk, 0, h), k_sems(rk, 0, h))
        z_left(k_st, k_r1, k_r2, hs, k_sems(sk, 1, h), k_sems(rk, 1, h))


def per_device(queries, keys_tile, values_tile, out_weight, out_grad):
    def vm(shape, dtype=BF16):
        return pltpu.VMEM(shape, dtype)

    dma = pltpu.SemaphoreType.DMA
    spec = pl.BlockSpec(memory_space=pltpu.VMEM)
    return pl.pallas_call(
        kernel,
        out_shape=(
            jax.ShapeDtypeStruct((TB, DC), BF16),
            jax.ShapeDtypeStruct((TB, HC), BF16),
            jax.ShapeDtypeStruct((TB, HC), BF16),
            jax.ShapeDtypeStruct((TB, HC), BF16),
            jax.ShapeDtypeStruct((TB, DC), BF16),
        ),
        in_specs=[spec] * 5,
        out_specs=(spec,) * 5,
        scratch_shapes=[
            vm((ZT, HC)), vm((ZT, HC)), vm((ZT, HC)), vm((ZT, DC)), vm((ZT, DC)), vm((HC, ZT)), vm((HC, ZT)),
            vm((HC, ZT)), vm((TB, ZT)), vm((TB, ZT)), vm((TB, ZT)),
            *[vm((8, ZT), F32) for _ in range(9)],
            vm((ZT, ZT)), vm((4, TB, ZT)), vm((4, PB, ZT)), vm((4, PB, ZT)), vm((4, TB, ZT)), vm((TB, ZT)),
            vm((TB, ZT)), vm((HC, ZT)), vm((2, 8, ZT), F32), vm((8, ZT), F32),
            vm((ZT, HD), F32), vm((ZT, HD), F32), vm((ZT, HC)), vm((ZT, HC)), vm((ZT, HC)),
            vm((2, PB, HC)), vm((2, PB, HC)), vm((2, TB, HC)), vm((2, TB, HC)),
            vm((2, TB, HC)), vm((TB, HC)), vm((TB, HC)),
            vm((ZT, DC)), vm((2, TB, DC)), vm((TB, DC)), vm((TB, DC)),
            vm((ZT, DC)), vm((4, TB, DC)),
            dma((6, 4)), dma((6, 4)), dma((6, 3)), dma((6, 3)), dma((4, 2)), dma((4,)), dma((4,)), dma((8,)),
            dma((10,)), dma((8,)), dma((8,)), dma((6,)), dma((6,)), dma((2, 3, 4)), dma((2, 3, 4)),
            dma((3, 3)), dma((3, 3)), dma((4,)), dma((4,)), vm((NH * ZT, ZT)),
        ],
        compiler_params=pltpu.CompilerParams(
            collective_id=0, has_side_effects=True, vmem_limit_bytes=60 * 1024 * 1024
        ),
    )(queries, keys_tile, values_tile, out_weight, out_grad)


def solution(mesh):
    spec = P("row", "col")
    return jax.shard_map(
        per_device, mesh=mesh, in_specs=(spec,) * 5, out_specs=(spec,) * 5, check_vma=False
    )
```

```python
import jax
import jax.numpy as jnp
from jax import lax
from jax.experimental import pallas as pl
from jax.experimental.pallas import tpu as pltpu
from jax.sharding import PartitionSpec as P

HD = 128
NH = 3
TB = 192
ZT = 4 * TB
HC = NH * HD
DC = 768
PB = HC // 4
QT = 256
SCALE = HD ** (-0.5)
LOG2E = 1.4426950408889634
MESH = pl.DeviceIdType.MESH
F32 = jnp.float32
BF16 = jnp.bfloat16


def dot(a, b, ca, cb):
    return lax.dot_general(a, b, (((ca,), (cb,)), ((), ())), preferred_element_type=F32)


def kernel(
    q_ref, k_ref, v_ref, w_ref, g_ref,
    mixed_o, dq_o, dk_o, dv_o, wg_o,
    k_all, v_all, q_all, w_all, g_all, kt, vt,
    o_st, o_core, o_chip, o_far, lse_own, lse_core, lse_chip, lse_far, lse_c, w_own, w_core, w_chip, w_far,
    attn_all, d_st, d_r1, d_sum, d_rc, d_up, d_yl, do_all, dp_all, delta,
    kacc, vacc, k_st, v_st, q_st, k_r1, v_r1, k_r2, v_r2, q_core, q_up, q_rc,
    m_st, m_core, m_up, m_rc, w_st, w_rc,
    sz, rz, sy, ry, sd, rx, sl, rd, sa, ra, rh, sb, rb, sk, rk, sq, rq, sw, rw, p_all,
):
    row, col = lax.axis_index("row"), lax.axis_index("col")
    z, q = row // 4, row % 4
    yh, co = q // 2, q % 2
    yl, x = col // 4, col % 4
    inner = x % 2 == yh
    outer = x % 2 != yh
    x_up, x_dn, other_yl = yl * 4 + (x + 1) % 4, yl * 4 + (x + 3) % 4, (1 - yl) * 4 + x
    z_up, z_dn, z_op = (z + 1) % 4, (z + 3) % 4, (z + 2) % 4
    up, dn = z_up * 4 + q, z_dn * 4 + q

    def ypeer(j):
        a = yh if j < 2 else 1 - yh
        b = co if j % 2 == 0 else 1 - co
        return a * 2 + b

    core = z * 4 + ypeer(1)
    far = z * 4 + ypeer(2)

    def copy(src, dst, ss, rs, r, c):
        return pltpu.make_async_remote_copy(
            src_ref=src, dst_ref=dst, send_sem=ss, recv_sem=rs, device_id=(r, c), device_id_type=MESH
        )

    def send(src, dst, ss, rs, r, c):
        d = copy(src, dst, ss, rs, r, c)
        d.start()
        return d

    def recv(dst, ss, rs):
        copy(dst, dst, ss, rs, row, col).wait_recv()

    def left(src, ss, rs):
        copy(src, src, ss, rs, row, col).wait_send()

    def rows(i, n):
        return pl.ds(pl.multiple_of(i * n, n), n)

    barrier = pltpu.get_barrier_semaphore()

    def greet(r, c):
        pl.semaphore_signal(barrier, inc=1, device_id=(r, c), device_id_type=MESH)

    for r in (up, dn, z_op * 4 + q, core, far):
        greet(r, col)
    for c in (x_up, x_dn, other_yl):
        greet(row, c)
    pl.semaphore_wait(barrier, 8)

    sends = []

    def lower(b):
        return rows(2 * b, PB)

    def upper(b):
        return rows(2 * b + 1, PB)

    def z_start(i, src, dst):
        to = dst.at[rows(z, TB), :]
        sends.append(send(src, to, sz.at[i, 0], rz.at[i, 0], up, col))
        sends.append(send(src, to, sz.at[i, 1], rz.at[i, 1], dn, col))

    def z_pass(i, dst):
        recv(dst.at[rows(z_dn, TB), :], sz.at[i, 0], rz.at[i, 0])
        a = dst.at[lower(z_dn), :]
        sends.append(send(a, a, sz.at[i, 2], rz.at[i, 2], up, col))
        recv(dst.at[rows(z_up, TB), :], sz.at[i, 1], rz.at[i, 1])
        b = dst.at[upper(z_up), :]
        sends.append(send(b, b, sz.at[i, 3], rz.at[i, 3], dn, col))

    def z_last(i, dst):
        recv(dst.at[lower(z_op), :], sz.at[i, 2], rz.at[i, 2])
        recv(dst.at[upper(z_op), :], sz.at[i, 3], rz.at[i, 3])

    def to_y(i, j, src, dst):
        sends.append(send(src, dst, sy.at[i, j - 1], ry.at[i, j - 1], far if j == 2 else core, col))

    def from_y(i, j, dst):
        recv(dst, sy.at[i, j - 1], ry.at[i, j - 1])

    z_start(0, k_ref, k_all)
    to_y(0, 2, q_ref, q_all.at[rows(q, TB), :])
    to_y(0, 1, q_ref, q_all.at[rows(q, TB), :])
    z_start(1, v_ref, v_all)
    to_y(1, 2, g_ref, g_all.at[rows(q, TB), :])
    to_y(1, 1, g_ref, g_all.at[rows(q, TB), :])
    k_all[rows(z, TB), :] = k_ref[...]
    v_all[rows(z, TB), :] = v_ref[...]
    q_all[rows(q, TB), :] = q_ref[...]
    g_all[rows(q, TB), :] = g_ref[...]
    w_all[rows(z, TB), :] = w_ref[...]
    lse_own[...] = jnp.zeros_like(lse_own)
    dp_all[co] = jnp.zeros((8, ZT), F32)

    part_far = rows(ypeer(2), TB)
    z_pass(0, k_all)
    from_y(0, 2, q_all.at[part_far, :])
    to_y(0, 3, q_all.at[part_far, :], q_all.at[part_far, :])
    z_pass(1, v_all)
    z_start(2, w_ref, w_all)
    for j in (1, 3):
        from_y(0, j, q_all.at[rows(ypeer(j), TB), :])
    z_last(0, k_all)
    kt[...] = k_all[...].T
    from_y(1, 2, g_all.at[part_far, :])
    to_y(1, 3, g_all.at[part_far, :], g_all.at[part_far, :])
    z_last(1, v_all)
    vt[...] = v_all[...].T

    def forward(h, carry):
        hs = rows(h, HD)
        kh, vh = k_all[:, hs], vt[hs, :]
        for t in range(3):
            ts = slice(t * QT, (t + 1) * QT)
            s = dot(kh, q_all[ts, hs], 1, 1)
            top = jnp.max(s, axis=0, keepdims=True)
            p = jnp.exp2((s - top) * (SCALE * LOG2E))
            total = jnp.sum(p, axis=0, keepdims=True)
            o = dot(vh, p.astype(BF16), 1, 0)
            o_st[hs, ts] = (o / total).astype(BF16)
            lse_own[pl.ds(h, 1), ts] = top * (SCALE * LOG2E) + jnp.log2(total)
        return carry

    def slot_of(c, other):
        return 2 * (1 - yl if other else yl) + c % 4 // 2

    slot_a, slot_b = slot_of(x, False), slot_of(x, True)

    def d_attn(n, zp):
        d_st[zp] = dot(w_all[rows(zp, TB), :], g_all[...], 1, 1).astype(BF16)
        tx = 2 * (zp % 2) + yh
        piece = jnp.where(zp // 2 == yl, 0, 1)

        @pl.when(inner & (tx != x))
        def _():
            send(d_st.at[zp, :PB], d_r1.at[piece], sd.at[n, 0], rx.at[piece], row, x_up)
            send(d_st.at[zp, PB:], d_r1.at[2 + piece], sd.at[n, 1], rx.at[2 + piece], row, x_dn)

        @pl.when(outer & (tx == (x + 1) % 4))
        def _():
            send(d_st.at[zp, PB:], d_rc.at[piece, PB:], sd.at[n, 0], rd.at[2 * piece + 1], row, x_up)

        @pl.when(outer & (tx == (x + 3) % 4))
        def _():
            send(d_st.at[zp, :PB], d_rc.at[2 + piece, :PB], sd.at[n, 0], rd.at[4 + 2 * piece], row, x_dn)

    lax.fori_loop(0, 2, forward, 0)
    for j in (1, 3):
        from_y(1, j, g_all.at[rows(ypeer(j), TB), :])
    z_pass(2, w_all)
    d_attn(0, z)
    lax.fori_loop(2, 3, forward, 0)

    to_y(3, 1, lse_own, lse_core)
    to_y(2, 1, o_st.at[rows(1 - co, TB), :], o_core)
    d_attn(1, z_dn)
    d_attn(2, z_up)

    def both(a, b):
        top = jnp.maximum(a, b)
        lse = top + jnp.log2(jnp.exp2(a - top) + jnp.exp2(b - top))
        return lse, jnp.exp2(a - lse), jnp.exp2(b - lse)

    def pieces():
        for i in range(3):
            yield (
                pl.ds((3 * co + i) // 2, 1),
                slice(i * 64, (i + 1) * 64),
                pl.ds(pl.multiple_of(co * TB + i * 64, 64), 64),
                pl.ds(pl.multiple_of(slot_a * TB + i * 64, 64), 64),
            )

    from_y(3, 1, lse_core)
    lse_chip[...], w_own[...], w_core[...] = both(lse_own[...], lse_core[...])
    to_y(3, 2, lse_chip, lse_far)
    from_y(2, 1, o_core)
    for head, part, src, to in pieces():
        o_chip[part, :] = (
            w_own[head, :] * o_st[src, :].astype(F32) + w_core[head, :] * o_core[part, :].astype(F32)
        ).astype(BF16)

    @pl.when(outer)
    def _():
        send(o_chip, o_far, sb.at[1], rb.at[1], far, col)

    z_last(2, w_all)
    d_attn(3, z_op)
    from_y(3, 2, lse_far)
    lse_c[...], w_chip[...], w_far[...] = both(lse_chip[...], lse_far[...])
    half = rows(co, TB)

    def again(h, carry):
        hs = rows(h, HD)
        kh = k_all[:, hs]
        for t in range(3):
            ts = slice(t * QT, (t + 1) * QT)
            s = dot(kh, q_all[ts, hs], 1, 1)
            p_all[rows(h, ZT), ts] = jnp.exp2(s * (SCALE * LOG2E) - lse_c[pl.ds(h, 1), ts]).astype(BF16)
        return carry

    def block(b, i):
        return attn_all.at[rows(2 * b + i, PB), :]

    def weight_part(b):
        w_st[rows(b, TB), :] = dot(attn_all[rows(b, TB), :], g_all[...], 1, 0).astype(BF16)

        @pl.when(b != z)
        def _():
            send(w_st.at[rows(b, TB), :], w_rc.at[z], sw.at[b], rw.at[z], b * 4 + q, col)

    @pl.when(inner)
    def _():
        lax.fori_loop(0, NH, again, 0)
        recv(o_far, sb.at[1], rb.at[1])
        for head, part, src, to in pieces():
            attn_all[to, :] = (
                w_chip[head, :] * o_chip[part, :].astype(F32) + w_far[head, :] * o_far[part, :].astype(F32)
            ).astype(BF16)
        def pass_on(b, i, n, to):
            send(block(b, i), block(b, i), sa.at[n], ra.at[2 * b + i], row, to)

        pass_on(slot_a, 0, 0, other_yl)
        pass_on(slot_a, 0, 2, x_up)
        pass_on(slot_a, 1, 4, x_dn)
        pass_on(slot_a, 1, 1, other_yl)
        pass_on(slot_a, 1, 3, x_up)
        pass_on(slot_a, 0, 5, x_dn)
        weight_part(slot_a)
        for i in (2, 3, 6, 7):
            recv(d_rc.at[i // 4 * 2 + 1, i % 2 * PB : (i % 2 + 1) * PB], sd.at[0, 0], rd.at[i])
        d_up[...] = (d_st[slot_b].astype(F32) + d_rc[1].astype(F32) + d_rc[3].astype(F32)).astype(BF16)
        send(d_up, d_yl, sb.at[0], rb.at[0], row, other_yl)
        recv(block(slot_b, 0), sa.at[0], ra.at[2 * slot_b])
        pass_on(slot_b, 0, 6, x_up)
        recv(block(slot_b, 1), sa.at[0], ra.at[2 * slot_b + 1])
        pass_on(slot_b, 1, 7, x_dn)
        pass_on(slot_b, 1, 8, x_up)
        pass_on(slot_b, 0, 9, x_dn)
        weight_part(slot_b)
        for i in (0, 1, 4, 5):
            recv(d_rc.at[i // 4 * 2, i % 2 * PB : (i % 2 + 1) * PB], sd.at[0, 0], rd.at[i])
        recv(d_yl, sb.at[0], rb.at[0])
        do_all[half, :] = (
            d_st[slot_a].astype(F32) + d_rc[0].astype(F32) + d_rc[2].astype(F32) + d_yl[...].astype(F32)
        ).astype(BF16)
        send(do_all.at[half, :], do_all.at[half, :], sb.at[2], rb.at[2], far, col)
        send(do_all.at[half, :], do_all.at[half, :], sb.at[3], rb.at[3], core, col)
        for head, part, src, to in pieces():
            dp_all[co, head, :] += jnp.sum(
                do_all[src, :].astype(F32) * attn_all[to, :].astype(F32), axis=0, keepdims=True
            )
        send(dp_all.at[co], dp_all.at[co], sb.at[4], rb.at[4], far, col)
        send(dp_all.at[co], dp_all.at[co], sb.at[5], rb.at[5], core, col)

    @pl.when(outer)
    def _():
        for p in (1, 0):
            s_up, s_dn = slot_of(x + 1, p == 1), slot_of(x + 3, p == 1)
            recv(d_r1.at[p], sd.at[0, 0], rx.at[p])
            d_sum[p] = (d_st[s_up, :PB].astype(F32) + d_r1[p].astype(F32)).astype(BF16)
            send(d_sum.at[p], d_rc.at[p, :PB], sl.at[p], rd.at[2 * p], row, x_up)
            recv(d_r1.at[2 + p], sd.at[0, 0], rx.at[2 + p])
            d_sum[2 + p] = (d_st[s_dn, PB:].astype(F32) + d_r1[2 + p].astype(F32)).astype(BF16)
            send(d_sum.at[2 + p], d_rc.at[2 + p, PB:], sl.at[2 + p], rd.at[4 + 2 * p + 1], row, x_dn)
        lax.fori_loop(0, NH, again, 0)
        for p in range(2):
            s_up, s_dn = slot_of(x + 1, p == 1), slot_of(x + 3, p == 1)
            recv(block(s_dn, 0), sa.at[0], ra.at[2 * s_dn])
            send(block(s_dn, 0), block(s_dn, 0), sa.at[p], rh.at[2 * s_dn], row, x_up)
            recv(block(s_up, 1), sa.at[0], ra.at[2 * s_up + 1])
            send(block(s_up, 1), block(s_up, 1), sa.at[2 + p], rh.at[2 * s_up + 1], row, x_dn)
            recv(block(s_dn, 1), sa.at[0], ra.at[2 * s_dn + 1])
            weight_part(s_dn)
            recv(block(s_up, 0), sa.at[0], ra.at[2 * s_up])
            weight_part(s_up)

    def z_add(st, r1, r2, hs, ss, rs):
        recv(r1.at[0, :, hs], ss(0), rs(0))
        a, b = lower(z_up), upper(z_dn)
        st[a, hs] = (st[a, hs].astype(F32) + r1[0, :, hs].astype(F32)).astype(BF16)
        send(st.at[rows(z_up, TB), hs], r2.at[0, :, hs], ss(2), rs(2), up, col)
        recv(r1.at[1, :, hs], ss(1), rs(1))
        st[b, hs] = (st[b, hs].astype(F32) + r1[1, :, hs].astype(F32)).astype(BF16)
        send(st.at[rows(z_dn, TB), hs], r2.at[1, :, hs], ss(3), rs(3), dn, col)

    def z_sum(st, r2, hs, ss, rs):
        recv(r2.at[0, :, hs], ss(2), rs(2))
        recv(r2.at[1, :, hs], ss(3), rs(3))
        return (
            st[rows(z, TB), hs].astype(F32) + r2[0, :, hs].astype(F32) + r2[1, :, hs].astype(F32)
        ).astype(BF16)

    def z_left(st, r1, r2, hs, ss, rs):
        for j in range(2):
            left(r1.at[0, :, hs], ss(j), rs(j))
            left(r2.at[0, :, hs], ss(2 + j), rs(2 + j))

    @pl.when(inner)
    def _():
        for p in range(2):
            b = slot_of(x + 2, p == 1)
            for i in range(2):
                recv(block(b, i), sa.at[0], rh.at[2 * b + i])
            weight_part(b)

    @pl.when(outer)
    def _():
        recv(do_all.at[half, :], sb.at[2], rb.at[2])
        send(do_all.at[half, :], do_all.at[half, :], sb.at[3], rb.at[3], core, col)
        recv(dp_all.at[co], sb.at[4], rb.at[4])
        send(dp_all.at[co], dp_all.at[co], sb.at[5], rb.at[5], core, col)

    def mixed_part(i, carry):
        m_st[rows(i, QT), :] = dot(attn_all[:, rows(i, QT)], w_all[...], 0, 0).astype(BF16)
        return carry

    lax.fori_loop(0, 3, mixed_part, 0)
    to_y(5, 3, m_st.at[rows(ypeer(3), TB), :], m_core.at[1])
    to_y(5, 1, m_st.at[rows(ypeer(1), TB), :], m_core.at[0])

    recv(do_all.at[rows(1 - co, TB), :], sb.at[3], rb.at[3])
    recv(dp_all.at[1 - co], sb.at[5], rb.at[5])
    delta[...] = dp_all[0] + dp_all[1]
    from_y(5, 3, m_core.at[1])
    m_up[...] = (m_st[part_far, :].astype(F32) + m_core[1].astype(F32)).astype(BF16)
    to_y(5, 2, m_up, m_rc)

    def k_sems(sem, i, h):
        return lambda j: sem.at[i, h, j]

    def head_next(h):
        hs = rows(h, HD)
        recv(q_core.at[1, :, hs], sq.at[h, 2], rq.at[h, 2])
        q_up[:, hs] = (q_st[part_far, hs].astype(F32) + q_core[1, :, hs].astype(F32)).astype(BF16)
        send(q_up.at[:, hs], q_rc.at[:, hs], sq.at[h, 1], rq.at[h, 1], far, col)
        z_add(v_st, v_r1, v_r2, hs, k_sems(sk, 0, h), k_sems(rk, 0, h))
        z_add(k_st, k_r1, k_r2, hs, k_sems(sk, 1, h), k_sems(rk, 1, h))

    def backward(h, carry):
        hs = rows(h, HD)
        kh = k_all[:, hs]
        vh = v_all[:, hs]
        for t in range(3):
            ts = slice(t * QT, (t + 1) * QT)
            qh = q_all[ts, hs]
            doh = do_all[hs, ts]
            p = p_all[rows(h, ZT), ts]
            dprob = dot(vh, doh, 1, 0)
            ds = (p.astype(F32) * (dprob - delta[pl.ds(h, 1), ts]) * SCALE).astype(BF16)
            dvt = dot(p, doh, 1, 1)
            dkt = dot(ds, qh, 1, 0)
            if t == 0:
                vacc[...] = dvt
                kacc[...] = dkt
            else:
                vacc[...] += dvt
                kacc[...] += dkt
            q_st[ts, hs] = dot(kt[hs, :], ds, 1, 0).T.astype(BF16)
        v_st[:, hs] = vacc[...].astype(BF16)
        k_st[:, hs] = kacc[...].astype(BF16)
        for i, (st, r1) in enumerate(((v_st, v_r1), (k_st, k_r1))):
            send(st.at[lower(z_op), hs], r1.at[0, :, hs], sk.at[i, h, 0], rk.at[i, h, 0], up, col)
            send(st.at[upper(z_op), hs], r1.at[1, :, hs], sk.at[i, h, 1], rk.at[i, h, 1], dn, col)
        send(q_st.at[rows(ypeer(3), TB), hs], q_core.at[1, :, hs], sq.at[h, 2], rq.at[h, 2], core, col)
        send(q_st.at[rows(ypeer(1), TB), hs], q_core.at[0, :, hs], sq.at[h, 0], rq.at[h, 0], core, col)

        @pl.when(h > 0)
        def _():
            head_next(h - 1)

        return carry

    lax.fori_loop(0, NH, backward, 0)
    head_next(NH - 1)

    from_y(5, 1, m_core.at[0])
    from_y(5, 2, m_rc)
    mixed_o[...] = (m_st[rows(q, TB), :].astype(F32) + m_core[0].astype(F32) + m_rc[...].astype(F32)).astype(BF16)
    total = w_st[rows(z, TB), :].astype(F32)
    for d in (1, 3, 2):
        src = (z + d) % 4
        recv(w_rc.at[src], sw.at[0], rw.at[src])
        total += w_rc[src].astype(F32)
    wg_o[...] = total.astype(BF16)
    for h in range(NH):
        hs = slice(h * HD, (h + 1) * HD)
        recv(q_core.at[0, :, hs], sq.at[h, 0], rq.at[h, 0])
        recv(q_rc.at[:, hs], sq.at[h, 1], rq.at[h, 1])
        dq_o[:, hs] = (
            q_st[rows(q, TB), hs].astype(F32) + q_core[0, :, hs].astype(F32) + q_rc[:, hs].astype(F32)
        ).astype(BF16)
        dv_o[:, hs] = z_sum(v_st, v_r2, hs, k_sems(sk, 0, h), k_sems(rk, 0, h))
        dk_o[:, hs] = z_sum(k_st, k_r2, hs, k_sems(sk, 1, h), k_sems(rk, 1, h))

    for d in sends:
        d.wait_send()
    left(do_all.at[half, :], sb.at[3], rb.at[3])
    left(dp_all.at[0], sb.at[5], rb.at[5])

    @pl.when(inner)
    def _():
        for n, zp in enumerate((z, z_dn, z_up, z_op)):
            @pl.when(2 * (zp % 2) + yh != x)
            def _():
                left(d_st.at[0, :PB], sd.at[n, 0], rx.at[0])
                left(d_st.at[0, :PB], sd.at[n, 1], rx.at[0])

        for i in range(10):
            left(block(0, 0), sa.at[i], ra.at[0])
        left(d_up, sb.at[0], rb.at[0])
        left(do_all.at[half, :], sb.at[2], rb.at[2])
        left(dp_all.at[0], sb.at[4], rb.at[4])

    @pl.when(outer)
    def _():
        for n in range(4):
            left(d_st.at[0, :PB], sd.at[n, 0], rx.at[0])
            left(d_sum.at[n], sl.at[n], rx.at[0])
            left(block(0, 0), sa.at[n], ra.at[0])
        left(o_chip, sb.at[1], rb.at[1])

    for b in range(4):
        @pl.when(z != b)
        def _():
            left(w_rc.at[0], sw.at[b], rw.at[0])

    for h in range(NH):
        hs = slice(h * HD, (h + 1) * HD)
        for j in range(3):
            left(q_rc.at[:, hs], sq.at[h, j], rq.at[h, j])
        z_left(v_st, v_r1, v_r2, hs, k_sems(sk, 0, h), k_sems(rk, 0, h))
        z_left(k_st, k_r1, k_r2, hs, k_sems(sk, 1, h), k_sems(rk, 1, h))


def results(*refs):
    for src, dst in zip(refs[:5], refs[5:]):
        dst[...] = src[...]


def per_device(queries, keys_tile, values_tile, out_weight, out_grad):
    def vm(shape, dtype=BF16):
        return pltpu.VMEM(shape, dtype)

    dma = pltpu.SemaphoreType.DMA
    spec = pl.BlockSpec(memory_space=pltpu.VMEM)
    shapes = (
        jax.ShapeDtypeStruct((TB, DC), BF16),
        jax.ShapeDtypeStruct((TB, HC), BF16),
        jax.ShapeDtypeStruct((TB, HC), BF16),
        jax.ShapeDtypeStruct((TB, HC), BF16),
        jax.ShapeDtypeStruct((TB, DC), BF16),
    )
    outs = pl.pallas_call(
        kernel,
        out_shape=shapes,
        in_specs=[spec] * 5,
        out_specs=(spec,) * 5,
        scratch_shapes=[
            vm((ZT, HC)), vm((ZT, HC)), vm((ZT, HC)), vm((ZT, DC)), vm((ZT, DC)), vm((HC, ZT)), vm((HC, ZT)),
            vm((HC, ZT)), vm((TB, ZT)), vm((TB, ZT)), vm((TB, ZT)),
            *[vm((8, ZT), F32) for _ in range(9)],
            vm((ZT, ZT)), vm((4, TB, ZT)), vm((4, PB, ZT)), vm((4, PB, ZT)), vm((4, TB, ZT)), vm((TB, ZT)),
            vm((TB, ZT)), vm((HC, ZT)), vm((2, 8, ZT), F32), vm((8, ZT), F32),
            vm((ZT, HD), F32), vm((ZT, HD), F32), vm((ZT, HC)), vm((ZT, HC)), vm((ZT, HC)),
            vm((2, PB, HC)), vm((2, PB, HC)), vm((2, TB, HC)), vm((2, TB, HC)),
            vm((2, TB, HC)), vm((TB, HC)), vm((TB, HC)),
            vm((ZT, DC)), vm((2, TB, DC)), vm((TB, DC)), vm((TB, DC)),
            vm((ZT, DC)), vm((4, TB, DC)),
            dma((6, 4)), dma((6, 4)), dma((6, 3)), dma((6, 3)), dma((4, 2)), dma((4,)), dma((4,)), dma((8,)),
            dma((10,)), dma((8,)), dma((8,)), dma((6,)), dma((6,)), dma((2, 3, 4)), dma((2, 3, 4)),
            dma((3, 3)), dma((3, 3)), dma((4,)), dma((4,)), vm((NH * ZT, ZT)),
        ],
        compiler_params=pltpu.CompilerParams(
            collective_id=0, has_side_effects=True, vmem_limit_bytes=60 * 1024 * 1024
        ),
    )(queries, keys_tile, values_tile, out_weight, out_grad)
    return pl.pallas_call(results, out_shape=shapes, in_specs=[spec] * 5, out_specs=(spec,) * 5)(*outs)


def solution(mesh):
    spec = P("row", "col")
    return jax.shard_map(
        per_device, mesh=mesh, in_specs=(spec,) * 5, out_specs=(spec,) * 5, check_vma=False
    )
```

```python
import jax
import jax.numpy as jnp
from jax import lax
from jax.experimental import pallas as pl
from jax.experimental.pallas import tpu as pltpu
from jax.sharding import PartitionSpec as P

HD = 128
NH = 3
TB = 192
ZT = 4 * TB
HC = NH * HD
DC = 768
PB = HC // 4
QT = 256
SCALE = HD ** (-0.5)
LOG2E = 1.4426950408889634
MESH = pl.DeviceIdType.MESH
F32 = jnp.float32
BF16 = jnp.bfloat16


def dot(a, b, ca, cb):
    return lax.dot_general(a, b, (((ca,), (cb,)), ((), ())), preferred_element_type=F32)


def kernel(
    q_ref, k_ref, v_ref, w_ref, g_ref,
    mixed_o, dq_o, dk_o, dv_o, wg_o,
    k_all, v_all, q_all, w_all, g_all, kt, vt,
    o_st, o_core, o_chip, o_far, lse_own, lse_core, lse_chip, lse_far, lse_c, w_own, w_core, w_chip, w_far,
    attn_all, d_st, d_r1, d_sum, d_rc, d_up, d_yl, do_all, dp_all, delta,
    kacc, vacc, k_st, v_st, q_st, k_r1, v_r1, k_r2, v_r2, q_core, q_up, q_rc,
    m_st, m_core, m_up, m_rc, w_st, w_rc,
    sz, rz, sy, ry, sd, rx, sl, rd, sa, ra, rh, sb, rb, sk, rk, sq, rq, sw, rw, si, p_all,
):
    row, col = lax.axis_index("row"), lax.axis_index("col")
    z, q = row // 4, row % 4
    yh, co = q // 2, q % 2
    yl, x = col // 4, col % 4
    inner = x % 2 == yh
    outer = x % 2 != yh
    x_up, x_dn, other_yl = yl * 4 + (x + 1) % 4, yl * 4 + (x + 3) % 4, (1 - yl) * 4 + x
    z_up, z_dn, z_op = (z + 1) % 4, (z + 3) % 4, (z + 2) % 4
    up, dn = z_up * 4 + q, z_dn * 4 + q

    def ypeer(j):
        a = yh if j < 2 else 1 - yh
        b = co if j % 2 == 0 else 1 - co
        return a * 2 + b

    core = z * 4 + ypeer(1)
    far = z * 4 + ypeer(2)

    def copy(src, dst, ss, rs, r, c):
        return pltpu.make_async_remote_copy(
            src_ref=src, dst_ref=dst, send_sem=ss, recv_sem=rs, device_id=(r, c), device_id_type=MESH
        )

    def send(src, dst, ss, rs, r, c):
        d = copy(src, dst, ss, rs, r, c)
        d.start()
        return d

    def recv(dst, ss, rs):
        copy(dst, dst, ss, rs, row, col).wait_recv()

    def left(src, ss, rs):
        copy(src, src, ss, rs, row, col).wait_send()

    def rows(i, n):
        return pl.ds(pl.multiple_of(i * n, n), n)

    own_copies = [
        pltpu.make_async_copy(src, dst.at[rows(i, TB), :], si.at[n])
        for n, (src, dst, i) in enumerate(
            ((k_ref, k_all, z), (q_ref, q_all, q), (v_ref, v_all, z), (g_ref, g_all, q), (w_ref, w_all, z))
        )
    ]
    for c in own_copies:
        c.start()

    barrier = pltpu.get_barrier_semaphore()

    def greet(r, c):
        pl.semaphore_signal(barrier, inc=1, device_id=(r, c), device_id_type=MESH)

    for r in (up, dn, z_op * 4 + q, core, far):
        greet(r, col)
    for c in (x_up, x_dn, other_yl):
        greet(row, c)
    pl.semaphore_wait(barrier, 8)

    sends = []

    def lower(b):
        return rows(2 * b, PB)

    def upper(b):
        return rows(2 * b + 1, PB)

    def z_start(i, src, dst):
        to = dst.at[rows(z, TB), :]
        sends.append(send(src, to, sz.at[i, 0], rz.at[i, 0], up, col))
        sends.append(send(src, to, sz.at[i, 1], rz.at[i, 1], dn, col))

    def z_pass(i, dst):
        recv(dst.at[rows(z_dn, TB), :], sz.at[i, 0], rz.at[i, 0])
        a = dst.at[lower(z_dn), :]
        sends.append(send(a, a, sz.at[i, 2], rz.at[i, 2], up, col))
        recv(dst.at[rows(z_up, TB), :], sz.at[i, 1], rz.at[i, 1])
        b = dst.at[upper(z_up), :]
        sends.append(send(b, b, sz.at[i, 3], rz.at[i, 3], dn, col))

    def z_last(i, dst):
        recv(dst.at[lower(z_op), :], sz.at[i, 2], rz.at[i, 2])
        recv(dst.at[upper(z_op), :], sz.at[i, 3], rz.at[i, 3])

    def to_y(i, j, src, dst):
        sends.append(send(src, dst, sy.at[i, j - 1], ry.at[i, j - 1], far if j == 2 else core, col))

    def from_y(i, j, dst):
        recv(dst, sy.at[i, j - 1], ry.at[i, j - 1])

    z_start(0, k_ref, k_all)
    to_y(0, 2, q_ref, q_all.at[rows(q, TB), :])
    to_y(0, 1, q_ref, q_all.at[rows(q, TB), :])
    z_start(1, v_ref, v_all)
    to_y(1, 2, g_ref, g_all.at[rows(q, TB), :])
    to_y(1, 1, g_ref, g_all.at[rows(q, TB), :])
    lse_own[...] = jnp.zeros_like(lse_own)
    dp_all[co] = jnp.zeros((8, ZT), F32)

    for c in own_copies:
        c.wait()

    part_far = rows(ypeer(2), TB)
    z_pass(0, k_all)
    from_y(0, 2, q_all.at[part_far, :])
    to_y(0, 3, q_all.at[part_far, :], q_all.at[part_far, :])
    z_pass(1, v_all)
    z_start(2, w_ref, w_all)
    for j in (1, 3):
        from_y(0, j, q_all.at[rows(ypeer(j), TB), :])
    z_last(0, k_all)
    kt[...] = k_all[...].T
    from_y(1, 2, g_all.at[part_far, :])
    to_y(1, 3, g_all.at[part_far, :], g_all.at[part_far, :])
    z_last(1, v_all)
    vt[...] = v_all[...].T

    def forward(h, carry):
        hs = rows(h, HD)
        kh, vh = k_all[:, hs], vt[hs, :]
        for t in range(3):
            ts = slice(t * QT, (t + 1) * QT)
            s = dot(kh, q_all[ts, hs], 1, 1)
            top = jnp.max(s, axis=0, keepdims=True)
            p = jnp.exp2((s - top) * (SCALE * LOG2E))
            total = jnp.sum(p, axis=0, keepdims=True)
            o = dot(vh, p.astype(BF16), 1, 0)
            o_st[hs, ts] = (o / total).astype(BF16)
            lse_own[pl.ds(h, 1), ts] = top * (SCALE * LOG2E) + jnp.log2(total)
        return carry

    def slot_of(c, other):
        return 2 * (1 - yl if other else yl) + c % 4 // 2

    slot_a, slot_b = slot_of(x, False), slot_of(x, True)

    def d_attn(n, zp):
        d_st[zp] = dot(w_all[rows(zp, TB), :], g_all[...], 1, 1).astype(BF16)
        tx = 2 * (zp % 2) + yh
        piece = jnp.where(zp // 2 == yl, 0, 1)

        @pl.when(inner & (tx != x))
        def _():
            send(d_st.at[zp, :PB], d_r1.at[piece], sd.at[n, 0], rx.at[piece], row, x_up)
            send(d_st.at[zp, PB:], d_r1.at[2 + piece], sd.at[n, 1], rx.at[2 + piece], row, x_dn)

        @pl.when(outer & (tx == (x + 1) % 4))
        def _():
            send(d_st.at[zp, PB:], d_rc.at[piece, PB:], sd.at[n, 0], rd.at[2 * piece + 1], row, x_up)

        @pl.when(outer & (tx == (x + 3) % 4))
        def _():
            send(d_st.at[zp, :PB], d_rc.at[2 + piece, :PB], sd.at[n, 0], rd.at[4 + 2 * piece], row, x_dn)

    lax.fori_loop(0, 2, forward, 0)
    for j in (1, 3):
        from_y(1, j, g_all.at[rows(ypeer(j), TB), :])
    z_pass(2, w_all)
    d_attn(0, z)
    lax.fori_loop(2, 3, forward, 0)

    to_y(3, 1, lse_own, lse_core)
    to_y(2, 1, o_st.at[rows(1 - co, TB), :], o_core)
    d_attn(1, z_dn)
    d_attn(2, z_up)

    def both(a, b):
        top = jnp.maximum(a, b)
        lse = top + jnp.log2(jnp.exp2(a - top) + jnp.exp2(b - top))
        return lse, jnp.exp2(a - lse), jnp.exp2(b - lse)

    def pieces():
        for i in range(3):
            yield (
                pl.ds((3 * co + i) // 2, 1),
                slice(i * 64, (i + 1) * 64),
                pl.ds(pl.multiple_of(co * TB + i * 64, 64), 64),
                pl.ds(pl.multiple_of(slot_a * TB + i * 64, 64), 64),
            )

    from_y(3, 1, lse_core)
    lse_chip[...], w_own[...], w_core[...] = both(lse_own[...], lse_core[...])
    to_y(3, 2, lse_chip, lse_far)
    from_y(2, 1, o_core)
    for head, part, src, to in pieces():
        o_chip[part, :] = (
            w_own[head, :] * o_st[src, :].astype(F32) + w_core[head, :] * o_core[part, :].astype(F32)
        ).astype(BF16)

    @pl.when(outer)
    def _():
        send(o_chip, o_far, sb.at[1], rb.at[1], far, col)

    z_last(2, w_all)
    d_attn(3, z_op)
    from_y(3, 2, lse_far)
    lse_c[...], w_chip[...], w_far[...] = both(lse_chip[...], lse_far[...])
    half = rows(co, TB)

    def again(h, carry):
        hs = rows(h, HD)
        kh = k_all[:, hs]
        for t in range(3):
            ts = slice(t * QT, (t + 1) * QT)
            s = dot(kh, q_all[ts, hs], 1, 1)
            p_all[rows(h, ZT), ts] = jnp.exp2(s * (SCALE * LOG2E) - lse_c[pl.ds(h, 1), ts]).astype(BF16)
        return carry

    def block(b, i):
        return attn_all.at[rows(2 * b + i, PB), :]

    def weight_part(b):
        w_st[rows(b, TB), :] = dot(attn_all[rows(b, TB), :], g_all[...], 1, 0).astype(BF16)

        @pl.when(b != z)
        def _():
            send(w_st.at[rows(b, TB), :], w_rc.at[z], sw.at[b], rw.at[z], b * 4 + q, col)

    @pl.when(inner)
    def _():
        lax.fori_loop(0, NH, again, 0)
        recv(o_far, sb.at[1], rb.at[1])
        for head, part, src, to in pieces():
            attn_all[to, :] = (
                w_chip[head, :] * o_chip[part, :].astype(F32) + w_far[head, :] * o_far[part, :].astype(F32)
            ).astype(BF16)
        def pass_on(b, i, n, to):
            send(block(b, i), block(b, i), sa.at[n], ra.at[2 * b + i], row, to)

        pass_on(slot_a, 0, 0, other_yl)
        pass_on(slot_a, 0, 2, x_up)
        pass_on(slot_a, 1, 4, x_dn)
        pass_on(slot_a, 1, 1, other_yl)
        pass_on(slot_a, 1, 3, x_up)
        pass_on(slot_a, 0, 5, x_dn)
        weight_part(slot_a)
        for i in (2, 3, 6, 7):
            recv(d_rc.at[i // 4 * 2 + 1, i % 2 * PB : (i % 2 + 1) * PB], sd.at[0, 0], rd.at[i])
        d_up[...] = (d_st[slot_b].astype(F32) + d_rc[1].astype(F32) + d_rc[3].astype(F32)).astype(BF16)
        send(d_up, d_yl, sb.at[0], rb.at[0], row, other_yl)
        recv(block(slot_b, 0), sa.at[0], ra.at[2 * slot_b])
        pass_on(slot_b, 0, 6, x_up)
        recv(block(slot_b, 1), sa.at[0], ra.at[2 * slot_b + 1])
        pass_on(slot_b, 1, 7, x_dn)
        pass_on(slot_b, 1, 8, x_up)
        pass_on(slot_b, 0, 9, x_dn)
        weight_part(slot_b)
        for i in (0, 1, 4, 5):
            recv(d_rc.at[i // 4 * 2, i % 2 * PB : (i % 2 + 1) * PB], sd.at[0, 0], rd.at[i])
        recv(d_yl, sb.at[0], rb.at[0])
        do_all[half, :] = (
            d_st[slot_a].astype(F32) + d_rc[0].astype(F32) + d_rc[2].astype(F32) + d_yl[...].astype(F32)
        ).astype(BF16)
        send(do_all.at[half, :], do_all.at[half, :], sb.at[2], rb.at[2], far, col)
        send(do_all.at[half, :], do_all.at[half, :], sb.at[3], rb.at[3], core, col)
        for head, part, src, to in pieces():
            dp_all[co, head, :] += jnp.sum(
                do_all[src, :].astype(F32) * attn_all[to, :].astype(F32), axis=0, keepdims=True
            )
        send(dp_all.at[co], dp_all.at[co], sb.at[4], rb.at[4], far, col)
        send(dp_all.at[co], dp_all.at[co], sb.at[5], rb.at[5], core, col)

    @pl.when(outer)
    def _():
        for p in (1, 0):
            s_up, s_dn = slot_of(x + 1, p == 1), slot_of(x + 3, p == 1)
            recv(d_r1.at[p], sd.at[0, 0], rx.at[p])
            d_sum[p] = (d_st[s_up, :PB].astype(F32) + d_r1[p].astype(F32)).astype(BF16)
            send(d_sum.at[p], d_rc.at[p, :PB], sl.at[p], rd.at[2 * p], row, x_up)
            recv(d_r1.at[2 + p], sd.at[0, 0], rx.at[2 + p])
            d_sum[2 + p] = (d_st[s_dn, PB:].astype(F32) + d_r1[2 + p].astype(F32)).astype(BF16)
            send(d_sum.at[2 + p], d_rc.at[2 + p, PB:], sl.at[2 + p], rd.at[4 + 2 * p + 1], row, x_dn)
        lax.fori_loop(0, NH, again, 0)
        for p in range(2):
            s_up, s_dn = slot_of(x + 1, p == 1), slot_of(x + 3, p == 1)
            recv(block(s_dn, 0), sa.at[0], ra.at[2 * s_dn])
            send(block(s_dn, 0), block(s_dn, 0), sa.at[p], rh.at[2 * s_dn], row, x_up)
            recv(block(s_up, 1), sa.at[0], ra.at[2 * s_up + 1])
            send(block(s_up, 1), block(s_up, 1), sa.at[2 + p], rh.at[2 * s_up + 1], row, x_dn)
            recv(block(s_dn, 1), sa.at[0], ra.at[2 * s_dn + 1])
            weight_part(s_dn)
            recv(block(s_up, 0), sa.at[0], ra.at[2 * s_up])
            weight_part(s_up)

    def z_add(st, r1, r2, hs, ss, rs):
        recv(r1.at[0, :, hs], ss(0), rs(0))
        a, b = lower(z_up), upper(z_dn)
        st[a, hs] = (st[a, hs].astype(F32) + r1[0, :, hs].astype(F32)).astype(BF16)
        send(st.at[rows(z_up, TB), hs], r2.at[0, :, hs], ss(2), rs(2), up, col)
        recv(r1.at[1, :, hs], ss(1), rs(1))
        st[b, hs] = (st[b, hs].astype(F32) + r1[1, :, hs].astype(F32)).astype(BF16)
        send(st.at[rows(z_dn, TB), hs], r2.at[1, :, hs], ss(3), rs(3), dn, col)

    def z_sum(st, r2, hs, ss, rs):
        recv(r2.at[0, :, hs], ss(2), rs(2))
        recv(r2.at[1, :, hs], ss(3), rs(3))
        return (
            st[rows(z, TB), hs].astype(F32) + r2[0, :, hs].astype(F32) + r2[1, :, hs].astype(F32)
        ).astype(BF16)

    def z_left(st, r1, r2, hs, ss, rs):
        for j in range(2):
            left(r1.at[0, :, hs], ss(j), rs(j))
            left(r2.at[0, :, hs], ss(2 + j), rs(2 + j))

    @pl.when(inner)
    def _():
        for p in range(2):
            b = slot_of(x + 2, p == 1)
            for i in range(2):
                recv(block(b, i), sa.at[0], rh.at[2 * b + i])
            weight_part(b)

    @pl.when(outer)
    def _():
        recv(do_all.at[half, :], sb.at[2], rb.at[2])
        send(do_all.at[half, :], do_all.at[half, :], sb.at[3], rb.at[3], core, col)
        recv(dp_all.at[co], sb.at[4], rb.at[4])
        send(dp_all.at[co], dp_all.at[co], sb.at[5], rb.at[5], core, col)

    def mixed_part(i, carry):
        m_st[rows(i, QT), :] = dot(attn_all[:, rows(i, QT)], w_all[...], 0, 0).astype(BF16)
        return carry

    lax.fori_loop(0, 3, mixed_part, 0)
    to_y(5, 3, m_st.at[rows(ypeer(3), TB), :], m_core.at[1])
    to_y(5, 1, m_st.at[rows(ypeer(1), TB), :], m_core.at[0])

    recv(do_all.at[rows(1 - co, TB), :], sb.at[3], rb.at[3])
    recv(dp_all.at[1 - co], sb.at[5], rb.at[5])
    delta[...] = dp_all[0] + dp_all[1]
    from_y(5, 3, m_core.at[1])
    m_up[...] = (m_st[part_far, :].astype(F32) + m_core[1].astype(F32)).astype(BF16)
    to_y(5, 2, m_up, m_rc)

    def k_sems(sem, i, h):
        return lambda j: sem.at[i, h, j]

    def head_next(h):
        hs = rows(h, HD)
        recv(q_core.at[1, :, hs], sq.at[h, 2], rq.at[h, 2])
        q_up[:, hs] = (q_st[part_far, hs].astype(F32) + q_core[1, :, hs].astype(F32)).astype(BF16)
        send(q_up.at[:, hs], q_rc.at[:, hs], sq.at[h, 1], rq.at[h, 1], far, col)
        z_add(v_st, v_r1, v_r2, hs, k_sems(sk, 0, h), k_sems(rk, 0, h))
        z_add(k_st, k_r1, k_r2, hs, k_sems(sk, 1, h), k_sems(rk, 1, h))

    def backward(h, carry):
        hs = rows(h, HD)
        kh = k_all[:, hs]
        vh = v_all[:, hs]
        for t in range(3):
            ts = slice(t * QT, (t + 1) * QT)
            qh = q_all[ts, hs]
            doh = do_all[hs, ts]
            p = p_all[rows(h, ZT), ts]
            dprob = dot(vh, doh, 1, 0)
            ds = (p.astype(F32) * (dprob - delta[pl.ds(h, 1), ts]) * SCALE).astype(BF16)
            dvt = dot(p, doh, 1, 1)
            dkt = dot(ds, qh, 1, 0)
            if t == 0:
                vacc[...] = dvt
                kacc[...] = dkt
            else:
                vacc[...] += dvt
                kacc[...] += dkt
            q_st[ts, hs] = dot(kt[hs, :], ds, 1, 0).T.astype(BF16)
        v_st[:, hs] = vacc[...].astype(BF16)
        k_st[:, hs] = kacc[...].astype(BF16)
        for i, (st, r1) in enumerate(((v_st, v_r1), (k_st, k_r1))):
            send(st.at[lower(z_op), hs], r1.at[0, :, hs], sk.at[i, h, 0], rk.at[i, h, 0], up, col)
            send(st.at[upper(z_op), hs], r1.at[1, :, hs], sk.at[i, h, 1], rk.at[i, h, 1], dn, col)
        send(q_st.at[rows(ypeer(3), TB), hs], q_core.at[1, :, hs], sq.at[h, 2], rq.at[h, 2], core, col)
        send(q_st.at[rows(ypeer(1), TB), hs], q_core.at[0, :, hs], sq.at[h, 0], rq.at[h, 0], core, col)

        @pl.when(h > 0)
        def _():
            head_next(h - 1)

        return carry

    lax.fori_loop(0, NH, backward, 0)
    head_next(NH - 1)

    from_y(5, 1, m_core.at[0])
    from_y(5, 2, m_rc)
    mixed_o[...] = (m_st[rows(q, TB), :].astype(F32) + m_core[0].astype(F32) + m_rc[...].astype(F32)).astype(BF16)
    total = w_st[rows(z, TB), :].astype(F32)
    for d in (1, 3, 2):
        src = (z + d) % 4
        recv(w_rc.at[src], sw.at[0], rw.at[src])
        total += w_rc[src].astype(F32)
    wg_o[...] = total.astype(BF16)
    for h in range(NH):
        hs = slice(h * HD, (h + 1) * HD)
        recv(q_core.at[0, :, hs], sq.at[h, 0], rq.at[h, 0])
        recv(q_rc.at[:, hs], sq.at[h, 1], rq.at[h, 1])
        dq_o[:, hs] = (
            q_st[rows(q, TB), hs].astype(F32) + q_core[0, :, hs].astype(F32) + q_rc[:, hs].astype(F32)
        ).astype(BF16)
        dv_o[:, hs] = z_sum(v_st, v_r2, hs, k_sems(sk, 0, h), k_sems(rk, 0, h))
        dk_o[:, hs] = z_sum(k_st, k_r2, hs, k_sems(sk, 1, h), k_sems(rk, 1, h))

    for d in sends:
        d.wait_send()
    left(do_all.at[half, :], sb.at[3], rb.at[3])
    left(dp_all.at[0], sb.at[5], rb.at[5])

    @pl.when(inner)
    def _():
        for n, zp in enumerate((z, z_dn, z_up, z_op)):
            @pl.when(2 * (zp % 2) + yh != x)
            def _():
                left(d_st.at[0, :PB], sd.at[n, 0], rx.at[0])
                left(d_st.at[0, :PB], sd.at[n, 1], rx.at[0])

        for i in range(10):
            left(block(0, 0), sa.at[i], ra.at[0])
        left(d_up, sb.at[0], rb.at[0])
        left(do_all.at[half, :], sb.at[2], rb.at[2])
        left(dp_all.at[0], sb.at[4], rb.at[4])

    @pl.when(outer)
    def _():
        for n in range(4):
            left(d_st.at[0, :PB], sd.at[n, 0], rx.at[0])
            left(d_sum.at[n], sl.at[n], rx.at[0])
            left(block(0, 0), sa.at[n], ra.at[0])
        left(o_chip, sb.at[1], rb.at[1])

    for b in range(4):
        @pl.when(z != b)
        def _():
            left(w_rc.at[0], sw.at[b], rw.at[0])

    for h in range(NH):
        hs = slice(h * HD, (h + 1) * HD)
        for j in range(3):
            left(q_rc.at[:, hs], sq.at[h, j], rq.at[h, j])
        z_left(v_st, v_r1, v_r2, hs, k_sems(sk, 0, h), k_sems(rk, 0, h))
        z_left(k_st, k_r1, k_r2, hs, k_sems(sk, 1, h), k_sems(rk, 1, h))


def results(*refs):
    for src, dst in zip(refs[:5], refs[5:]):
        dst[...] = src[...]


def per_device(queries, keys_tile, values_tile, out_weight, out_grad):
    def vm(shape, dtype=BF16):
        return pltpu.VMEM(shape, dtype)

    dma = pltpu.SemaphoreType.DMA
    spec = pl.BlockSpec(memory_space=pltpu.VMEM)
    shapes = (
        jax.ShapeDtypeStruct((TB, DC), BF16),
        jax.ShapeDtypeStruct((TB, HC), BF16),
        jax.ShapeDtypeStruct((TB, HC), BF16),
        jax.ShapeDtypeStruct((TB, HC), BF16),
        jax.ShapeDtypeStruct((TB, DC), BF16),
    )
    outs = pl.pallas_call(
        kernel,
        out_shape=shapes,
        in_specs=[pl.BlockSpec(memory_space=pl.ANY)] * 5,
        out_specs=(spec,) * 5,
        scratch_shapes=[
            vm((ZT, HC)), vm((ZT, HC)), vm((ZT, HC)), vm((ZT, DC)), vm((ZT, DC)), vm((HC, ZT)), vm((HC, ZT)),
            vm((HC, ZT)), vm((TB, ZT)), vm((TB, ZT)), vm((TB, ZT)),
            *[vm((8, ZT), F32) for _ in range(9)],
            vm((ZT, ZT)), vm((4, TB, ZT)), vm((4, PB, ZT)), vm((4, PB, ZT)), vm((4, TB, ZT)), vm((TB, ZT)),
            vm((TB, ZT)), vm((HC, ZT)), vm((2, 8, ZT), F32), vm((8, ZT), F32),
            vm((ZT, HD), F32), vm((ZT, HD), F32), vm((ZT, HC)), vm((ZT, HC)), vm((ZT, HC)),
            vm((2, PB, HC)), vm((2, PB, HC)), vm((2, TB, HC)), vm((2, TB, HC)),
            vm((2, TB, HC)), vm((TB, HC)), vm((TB, HC)),
            vm((ZT, DC)), vm((2, TB, DC)), vm((TB, DC)), vm((TB, DC)),
            vm((ZT, DC)), vm((4, TB, DC)),
            dma((6, 4)), dma((6, 4)), dma((6, 3)), dma((6, 3)), dma((4, 2)), dma((4,)), dma((4,)), dma((8,)),
            dma((10,)), dma((8,)), dma((8,)), dma((6,)), dma((6,)), dma((2, 3, 4)), dma((2, 3, 4)),
            dma((3, 3)), dma((3, 3)), dma((4,)), dma((4,)), dma((5,)), vm((NH * ZT, ZT)),
        ],
        compiler_params=pltpu.CompilerParams(
            collective_id=0, has_side_effects=True, vmem_limit_bytes=60 * 1024 * 1024
        ),
    )(queries, keys_tile, values_tile, out_weight, out_grad)
    return pl.pallas_call(results, out_shape=shapes, in_specs=[spec] * 5, out_specs=(spec,) * 5)(*outs)


def solution(mesh):
    spec = P("row", "col")
    return jax.shard_map(
        per_device, mesh=mesh, in_specs=(spec,) * 5, out_specs=(spec,) * 5, check_vma=False
    )
```

```python
import jax
import jax.numpy as jnp
from jax import lax
from jax.experimental import pallas as pl
from jax.experimental.pallas import tpu as pltpu
from jax.sharding import PartitionSpec as P

HD = 128
NH = 3
TB = 192
ZT = 4 * TB
HC = NH * HD
DC = 768
PB = HC // 4
NK = 3 * TB
QT = 256
SCALE = HD ** (-0.5)
LOG2E = 1.4426950408889634
MESH = pl.DeviceIdType.MESH
F32 = jnp.float32
BF16 = jnp.bfloat16


def dot(a, b, ca, cb):
    return lax.dot_general(a, b, (((ca,), (cb,)), ((), ())), preferred_element_type=F32)


def kernel(
    q_ref, k_ref, v_ref, w_ref, g_ref,
    mixed_o, dq_o, dk_o, dv_o, wg_o,
    k_all, v_all, q_all, w_all, g_all, kt, o_acc,
    o_st, o_core, o_chip, o_far, lse_own, lse_core, lse_chip, lse_far, lse_c, w_own, w_core, w_chip, w_far,
    attn_all, d_st, d_r1, d_sum, d_rc, d_up, d_yl, do_all, dp_all, delta,
    kacc, vacc, k_st, v_st, q_st, k_r1, v_r1, k_r2, v_r2, q_core, q_up, q_rc,
    m_st, m_core, m_up, m_rc, w_st, w_rc,
    sz, rz, sy, ry, sd, rx, sl, rd, sa, ra, rh, sb, rb, sk, rk, sq, rq, sw, rw, si, p_all,
):
    row, col = lax.axis_index("row"), lax.axis_index("col")
    z, q = row // 4, row % 4
    yh, co = q // 2, q % 2
    yl, x = col // 4, col % 4
    inner = x % 2 == yh
    outer = x % 2 != yh
    x_up, x_dn, other_yl = yl * 4 + (x + 1) % 4, yl * 4 + (x + 3) % 4, (1 - yl) * 4 + x
    z_up, z_dn, z_op = (z + 1) % 4, (z + 3) % 4, (z + 2) % 4
    up, dn = z_up * 4 + q, z_dn * 4 + q

    def ypeer(j):
        a = yh if j < 2 else 1 - yh
        b = co if j % 2 == 0 else 1 - co
        return a * 2 + b

    core = z * 4 + ypeer(1)
    far = z * 4 + ypeer(2)

    def copy(src, dst, ss, rs, r, c):
        return pltpu.make_async_remote_copy(
            src_ref=src, dst_ref=dst, send_sem=ss, recv_sem=rs, device_id=(r, c), device_id_type=MESH
        )

    def send(src, dst, ss, rs, r, c):
        d = copy(src, dst, ss, rs, r, c)
        d.start()
        return d

    def recv(dst, ss, rs):
        copy(dst, dst, ss, rs, row, col).wait_recv()

    def left(src, ss, rs):
        copy(src, src, ss, rs, row, col).wait_send()

    def rows(i, n):
        return pl.ds(i * n if isinstance(i, int) else pl.multiple_of(i * n, n), n)

    own_copies = [
        pltpu.make_async_copy(src, dst.at[rows(i, TB), :], si.at[n])
        for n, (src, dst, i) in enumerate(
            ((k_ref, k_all, 0), (q_ref, q_all, q), (v_ref, v_all, 0), (g_ref, g_all, q), (w_ref, w_all, z))
        )
    ]
    for c in own_copies:
        c.start()

    barrier = pltpu.get_barrier_semaphore()

    def greet(r, c):
        pl.semaphore_signal(barrier, inc=1, device_id=(r, c), device_id_type=MESH)

    for r in (up, dn, z_op * 4 + q, core, far):
        greet(r, col)
    for c in (x_up, x_dn, other_yl):
        greet(row, c)
    pl.semaphore_wait(barrier, 8)

    sends = []

    def lower(b):
        return rows(2 * b, PB)

    def upper(b):
        return rows(2 * b + 1, PB)

    def z_start(i, src, dst, at_up, at_dn):
        sends.append(send(src, dst.at[rows(at_up, TB), :], sz.at[i, 0], rz.at[i, 0], up, col))
        sends.append(send(src, dst.at[rows(at_dn, TB), :], sz.at[i, 1], rz.at[i, 1], dn, col))

    def z_pass(i, dst, b_dn, b_up, at_up, at_dn):
        recv(dst.at[rows(b_dn, TB), :], sz.at[i, 0], rz.at[i, 0])
        sends.append(send(dst.at[lower(b_dn), :], dst.at[lower(at_up), :], sz.at[i, 2], rz.at[i, 2], up, col))
        recv(dst.at[rows(b_up, TB), :], sz.at[i, 1], rz.at[i, 1])
        sends.append(send(dst.at[upper(b_up), :], dst.at[upper(at_dn), :], sz.at[i, 3], rz.at[i, 3], dn, col))

    def z_last(i, dst, b):
        recv(dst.at[lower(b), :], sz.at[i, 2], rz.at[i, 2])
        recv(dst.at[upper(b), :], sz.at[i, 3], rz.at[i, 3])

    def to_y(i, j, src, dst):
        sends.append(send(src, dst, sy.at[i, j - 1], ry.at[i, j - 1], far if j == 2 else core, col))

    def from_y(i, j, dst):
        recv(dst, sy.at[i, j - 1], ry.at[i, j - 1])

    z_start(0, k_ref, k_all, 1, 2)
    to_y(0, 2, q_ref, q_all.at[rows(q, TB), :])
    to_y(0, 1, q_ref, q_all.at[rows(q, TB), :])
    z_start(1, v_ref, v_all, 1, 2)
    to_y(1, 2, g_ref, g_all.at[rows(q, TB), :])
    to_y(1, 1, g_ref, g_all.at[rows(q, TB), :])
    lse_own[...] = jnp.zeros_like(lse_own)
    dp_all[co] = jnp.zeros((8, ZT), F32)

    for c in own_copies:
        c.wait()

    part_far = rows(ypeer(2), TB)
    z_pass(0, k_all, 1, 2, 3, 3)
    from_y(0, 2, q_all.at[part_far, :])
    to_y(0, 3, q_all.at[part_far, :], q_all.at[part_far, :])
    z_pass(1, v_all, 1, 2, 3, 3)
    z_start(2, w_ref, w_all, z, z)
    for j in (1, 3):
        from_y(0, j, q_all.at[rows(ypeer(j), TB), :])
    def forward(h, carry):
        hs = rows(h, HD)
        kh, vh = k_all[:NK, hs], v_all[:NK, hs]
        for t in range(3):
            ts = slice(t * QT, (t + 1) * QT)
            s = dot(kh, q_all[ts, hs], 1, 1)
            top = jnp.max(s, axis=0, keepdims=True)
            p = jnp.exp2((s - top) * (SCALE * LOG2E))
            o_acc[hs, ts] = dot(vh, p.astype(BF16), 0, 0)
            w_own[pl.ds(h, 1), ts] = top
            w_core[pl.ds(h, 1), ts] = jnp.sum(p, axis=0, keepdims=True)
        return carry

    def forward_last(h, carry):
        hs = rows(h, HD)
        kh, vh = k_all[NK:, hs], v_all[NK:, hs]
        for t in range(3):
            ts = slice(t * QT, (t + 1) * QT)
            s = dot(kh, q_all[ts, hs], 1, 1)
            old = w_own[pl.ds(h, 1), ts]
            top = jnp.maximum(jnp.max(s, axis=0, keepdims=True), old)
            p = jnp.exp2((s - top) * (SCALE * LOG2E))
            keep = jnp.exp2((old - top) * (SCALE * LOG2E))
            total = keep * w_core[pl.ds(h, 1), ts] + jnp.sum(p, axis=0, keepdims=True)
            o = keep * o_acc[hs, ts] + dot(vh, p.astype(BF16), 0, 0)
            o_st[hs, ts] = (o / total).astype(BF16)
            lse_own[pl.ds(h, 1), ts] = top * (SCALE * LOG2E) + jnp.log2(total)
        return carry

    def slot_of(c, other):
        return 2 * (1 - yl if other else yl) + c % 4 // 2

    slot_a, slot_b = slot_of(x, False), slot_of(x, True)

    def d_attn(n, zp):
        d_st[zp] = dot(w_all[rows(zp, TB), :], g_all[...], 1, 1).astype(BF16)
        tx = 2 * (zp % 2) + yh
        piece = jnp.where(zp // 2 == yl, 0, 1)

        @pl.when(inner & (tx != x))
        def _():
            send(d_st.at[zp, :PB], d_r1.at[piece], sd.at[n, 0], rx.at[piece], row, x_up)
            send(d_st.at[zp, PB:], d_r1.at[2 + piece], sd.at[n, 1], rx.at[2 + piece], row, x_dn)

        @pl.when(outer & (tx == (x + 1) % 4))
        def _():
            send(d_st.at[zp, PB:], d_rc.at[piece, PB:], sd.at[n, 0], rd.at[2 * piece + 1], row, x_up)

        @pl.when(outer & (tx == (x + 3) % 4))
        def _():
            send(d_st.at[zp, :PB], d_rc.at[2 + piece, :PB], sd.at[n, 0], rd.at[4 + 2 * piece], row, x_dn)

    lax.fori_loop(0, NH, forward, 0)
    from_y(1, 2, g_all.at[part_far, :])
    to_y(1, 3, g_all.at[part_far, :], g_all.at[part_far, :])
    z_last(0, k_all, 3)
    z_last(1, v_all, 3)
    lax.fori_loop(0, NH, forward_last, 0)

    to_y(3, 1, lse_own, lse_core)
    to_y(2, 1, o_st.at[rows(1 - co, TB), :], o_core)
    kt[...] = k_all[...].T
    for j in (1, 3):
        from_y(1, j, g_all.at[rows(ypeer(j), TB), :])
    z_pass(2, w_all, z_dn, z_up, z_dn, z_up)
    d_attn(0, z)
    d_attn(1, z_dn)
    d_attn(2, z_up)

    def both(a, b):
        top = jnp.maximum(a, b)
        lse = top + jnp.log2(jnp.exp2(a - top) + jnp.exp2(b - top))
        return lse, jnp.exp2(a - lse), jnp.exp2(b - lse)

    def pieces():
        for i in range(3):
            yield (
                pl.ds((3 * co + i) // 2, 1),
                slice(i * 64, (i + 1) * 64),
                pl.ds(pl.multiple_of(co * TB + i * 64, 64), 64),
                pl.ds(pl.multiple_of(slot_a * TB + i * 64, 64), 64),
            )

    from_y(3, 1, lse_core)
    lse_chip[...], w_own[...], w_core[...] = both(lse_own[...], lse_core[...])
    to_y(3, 2, lse_chip, lse_far)
    from_y(2, 1, o_core)
    for head, part, src, to in pieces():
        o_chip[part, :] = (
            w_own[head, :] * o_st[src, :].astype(F32) + w_core[head, :] * o_core[part, :].astype(F32)
        ).astype(BF16)

    @pl.when(outer)
    def _():
        send(o_chip, o_far, sb.at[1], rb.at[1], far, col)

    z_last(2, w_all, z_op)
    d_attn(3, z_op)
    from_y(3, 2, lse_far)
    lse_c[...], w_chip[...], w_far[...] = both(lse_chip[...], lse_far[...])
    half = rows(co, TB)

    def again(h, carry):
        hs = rows(h, HD)
        kh = k_all[:, hs]
        for t in range(3):
            ts = slice(t * QT, (t + 1) * QT)
            s = dot(kh, q_all[ts, hs], 1, 1)
            p_all[rows(h, ZT), ts] = jnp.exp2(s * (SCALE * LOG2E) - lse_c[pl.ds(h, 1), ts]).astype(BF16)
        return carry

    def block(b, i):
        return attn_all.at[rows(2 * b + i, PB), :]

    def weight_part(b):
        w_st[rows(b, TB), :] = dot(attn_all[rows(b, TB), :], g_all[...], 1, 0).astype(BF16)

        @pl.when(b != z)
        def _():
            send(w_st.at[rows(b, TB), :], w_rc.at[z], sw.at[b], rw.at[z], b * 4 + q, col)

    @pl.when(inner)
    def _():
        lax.fori_loop(0, NH, again, 0)
        recv(o_far, sb.at[1], rb.at[1])
        for head, part, src, to in pieces():
            attn_all[to, :] = (
                w_chip[head, :] * o_chip[part, :].astype(F32) + w_far[head, :] * o_far[part, :].astype(F32)
            ).astype(BF16)
        def pass_on(b, i, n, to):
            send(block(b, i), block(b, i), sa.at[n], ra.at[2 * b + i], row, to)

        pass_on(slot_a, 0, 0, other_yl)
        pass_on(slot_a, 0, 2, x_up)
        pass_on(slot_a, 1, 4, x_dn)
        pass_on(slot_a, 1, 1, other_yl)
        pass_on(slot_a, 1, 3, x_up)
        pass_on(slot_a, 0, 5, x_dn)
        weight_part(slot_a)
        for i in (2, 3, 6, 7):
            recv(d_rc.at[i // 4 * 2 + 1, i % 2 * PB : (i % 2 + 1) * PB], sd.at[0, 0], rd.at[i])
        d_up[...] = (d_st[slot_b].astype(F32) + d_rc[1].astype(F32) + d_rc[3].astype(F32)).astype(BF16)
        send(d_up, d_yl, sb.at[0], rb.at[0], row, other_yl)
        recv(block(slot_b, 0), sa.at[0], ra.at[2 * slot_b])
        pass_on(slot_b, 0, 6, x_up)
        recv(block(slot_b, 1), sa.at[0], ra.at[2 * slot_b + 1])
        pass_on(slot_b, 1, 7, x_dn)
        pass_on(slot_b, 1, 8, x_up)
        pass_on(slot_b, 0, 9, x_dn)
        weight_part(slot_b)
        for i in (0, 1, 4, 5):
            recv(d_rc.at[i // 4 * 2, i % 2 * PB : (i % 2 + 1) * PB], sd.at[0, 0], rd.at[i])
        recv(d_yl, sb.at[0], rb.at[0])
        do_all[half, :] = (
            d_st[slot_a].astype(F32) + d_rc[0].astype(F32) + d_rc[2].astype(F32) + d_yl[...].astype(F32)
        ).astype(BF16)
        send(do_all.at[half, :], do_all.at[half, :], sb.at[2], rb.at[2], far, col)
        send(do_all.at[half, :], do_all.at[half, :], sb.at[3], rb.at[3], core, col)
        for head, part, src, to in pieces():
            dp_all[co, head, :] += jnp.sum(
                do_all[src, :].astype(F32) * attn_all[to, :].astype(F32), axis=0, keepdims=True
            )
        send(dp_all.at[co], dp_all.at[co], sb.at[4], rb.at[4], far, col)
        send(dp_all.at[co], dp_all.at[co], sb.at[5], rb.at[5], core, col)

    @pl.when(outer)
    def _():
        for p in (1, 0):
            s_up, s_dn = slot_of(x + 1, p == 1), slot_of(x + 3, p == 1)
            recv(d_r1.at[p], sd.at[0, 0], rx.at[p])
            d_sum[p] = (d_st[s_up, :PB].astype(F32) + d_r1[p].astype(F32)).astype(BF16)
            send(d_sum.at[p], d_rc.at[p, :PB], sl.at[p], rd.at[2 * p], row, x_up)
            recv(d_r1.at[2 + p], sd.at[0, 0], rx.at[2 + p])
            d_sum[2 + p] = (d_st[s_dn, PB:].astype(F32) + d_r1[2 + p].astype(F32)).astype(BF16)
            send(d_sum.at[2 + p], d_rc.at[2 + p, PB:], sl.at[2 + p], rd.at[4 + 2 * p + 1], row, x_dn)
        lax.fori_loop(0, NH, again, 0)
        for p in range(2):
            s_up, s_dn = slot_of(x + 1, p == 1), slot_of(x + 3, p == 1)
            recv(block(s_dn, 0), sa.at[0], ra.at[2 * s_dn])
            send(block(s_dn, 0), block(s_dn, 0), sa.at[p], rh.at[2 * s_dn], row, x_up)
            recv(block(s_up, 1), sa.at[0], ra.at[2 * s_up + 1])
            send(block(s_up, 1), block(s_up, 1), sa.at[2 + p], rh.at[2 * s_up + 1], row, x_dn)
            recv(block(s_dn, 1), sa.at[0], ra.at[2 * s_dn + 1])
            weight_part(s_dn)
            recv(block(s_up, 0), sa.at[0], ra.at[2 * s_up])
            weight_part(s_up)

    def z_add(st, r1, r2, hs, ss, rs):
        recv(r1.at[0, :, hs], ss(0), rs(0))
        a, b = lower(2), upper(1)
        st[a, hs] = (st[a, hs].astype(F32) + r1[0, :, hs].astype(F32)).astype(BF16)
        send(st.at[rows(2, TB), hs], r2.at[0, :, hs], ss(2), rs(2), up, col)
        recv(r1.at[1, :, hs], ss(1), rs(1))
        st[b, hs] = (st[b, hs].astype(F32) + r1[1, :, hs].astype(F32)).astype(BF16)
        send(st.at[rows(1, TB), hs], r2.at[1, :, hs], ss(3), rs(3), dn, col)

    def z_sum(st, r2, hs, ss, rs):
        recv(r2.at[0, :, hs], ss(2), rs(2))
        recv(r2.at[1, :, hs], ss(3), rs(3))
        return (
            st[rows(0, TB), hs].astype(F32) + r2[0, :, hs].astype(F32) + r2[1, :, hs].astype(F32)
        ).astype(BF16)

    def z_left(st, r1, r2, hs, ss, rs):
        for j in range(2):
            left(r1.at[0, :, hs], ss(j), rs(j))
            left(r2.at[0, :, hs], ss(2 + j), rs(2 + j))

    @pl.when(inner)
    def _():
        for p in range(2):
            b = slot_of(x + 2, p == 1)
            for i in range(2):
                recv(block(b, i), sa.at[0], rh.at[2 * b + i])
            weight_part(b)

    @pl.when(outer)
    def _():
        recv(do_all.at[half, :], sb.at[2], rb.at[2])
        send(do_all.at[half, :], do_all.at[half, :], sb.at[3], rb.at[3], core, col)
        recv(dp_all.at[co], sb.at[4], rb.at[4])
        send(dp_all.at[co], dp_all.at[co], sb.at[5], rb.at[5], core, col)

    def mixed_part(i, carry):
        m_st[rows(i, QT), :] = dot(attn_all[:, rows(i, QT)], w_all[...], 0, 0).astype(BF16)
        return carry

    lax.fori_loop(0, 3, mixed_part, 0)
    to_y(5, 3, m_st.at[rows(ypeer(3), TB), :], m_core.at[1])
    to_y(5, 1, m_st.at[rows(ypeer(1), TB), :], m_core.at[0])

    recv(do_all.at[rows(1 - co, TB), :], sb.at[3], rb.at[3])
    recv(dp_all.at[1 - co], sb.at[5], rb.at[5])
    delta[...] = dp_all[0] + dp_all[1]
    from_y(5, 3, m_core.at[1])
    m_up[...] = (m_st[part_far, :].astype(F32) + m_core[1].astype(F32)).astype(BF16)
    to_y(5, 2, m_up, m_rc)

    def k_sems(sem, i, h):
        return lambda j: sem.at[i, h, j]

    def head_next(h):
        hs = rows(h, HD)
        recv(q_core.at[1, :, hs], sq.at[h, 2], rq.at[h, 2])
        q_up[:, hs] = (q_st[part_far, hs].astype(F32) + q_core[1, :, hs].astype(F32)).astype(BF16)
        send(q_up.at[:, hs], q_rc.at[:, hs], sq.at[h, 1], rq.at[h, 1], far, col)
        z_add(v_st, v_r1, v_r2, hs, k_sems(sk, 0, h), k_sems(rk, 0, h))
        z_add(k_st, k_r1, k_r2, hs, k_sems(sk, 1, h), k_sems(rk, 1, h))

    def backward(h, carry):
        hs = rows(h, HD)
        kh = k_all[:, hs]
        vh = v_all[:, hs]
        for t in range(3):
            ts = slice(t * QT, (t + 1) * QT)
            qh = q_all[ts, hs]
            doh = do_all[hs, ts]
            p = p_all[rows(h, ZT), ts]
            dprob = dot(vh, doh, 1, 0)
            ds = (p.astype(F32) * (dprob - delta[pl.ds(h, 1), ts]) * SCALE).astype(BF16)
            dvt = dot(p, doh, 1, 1)
            dkt = dot(ds, qh, 1, 0)
            if t == 0:
                vacc[...] = dvt
                kacc[...] = dkt
            else:
                vacc[...] += dvt
                kacc[...] += dkt
            q_st[ts, hs] = dot(kt[hs, :], ds, 1, 0).T.astype(BF16)
        v_st[:, hs] = vacc[...].astype(BF16)
        k_st[:, hs] = kacc[...].astype(BF16)
        for i, (st, r1) in enumerate(((v_st, v_r1), (k_st, k_r1))):
            send(st.at[lower(3), hs], r1.at[0, :, hs], sk.at[i, h, 0], rk.at[i, h, 0], up, col)
            send(st.at[upper(3), hs], r1.at[1, :, hs], sk.at[i, h, 1], rk.at[i, h, 1], dn, col)
        send(q_st.at[rows(ypeer(3), TB), hs], q_core.at[1, :, hs], sq.at[h, 2], rq.at[h, 2], core, col)
        send(q_st.at[rows(ypeer(1), TB), hs], q_core.at[0, :, hs], sq.at[h, 0], rq.at[h, 0], core, col)

        @pl.when(h > 0)
        def _():
            head_next(h - 1)

        return carry

    lax.fori_loop(0, NH, backward, 0)
    head_next(NH - 1)

    from_y(5, 1, m_core.at[0])
    from_y(5, 2, m_rc)
    mixed_o[...] = (m_st[rows(q, TB), :].astype(F32) + m_core[0].astype(F32) + m_rc[...].astype(F32)).astype(BF16)
    total = w_st[rows(z, TB), :].astype(F32)
    for d in (1, 3, 2):
        src = (z + d) % 4
        recv(w_rc.at[src], sw.at[0], rw.at[src])
        total += w_rc[src].astype(F32)
    wg_o[...] = total.astype(BF16)
    for h in range(NH):
        hs = slice(h * HD, (h + 1) * HD)
        recv(q_core.at[0, :, hs], sq.at[h, 0], rq.at[h, 0])
        recv(q_rc.at[:, hs], sq.at[h, 1], rq.at[h, 1])
        dq_o[:, hs] = (
            q_st[rows(q, TB), hs].astype(F32) + q_core[0, :, hs].astype(F32) + q_rc[:, hs].astype(F32)
        ).astype(BF16)
        dv_o[:, hs] = z_sum(v_st, v_r2, hs, k_sems(sk, 0, h), k_sems(rk, 0, h))
        dk_o[:, hs] = z_sum(k_st, k_r2, hs, k_sems(sk, 1, h), k_sems(rk, 1, h))

    for d in sends:
        d.wait_send()
    left(do_all.at[half, :], sb.at[3], rb.at[3])
    left(dp_all.at[0], sb.at[5], rb.at[5])

    @pl.when(inner)
    def _():
        for n, zp in enumerate((z, z_dn, z_up, z_op)):
            @pl.when(2 * (zp % 2) + yh != x)
            def _():
                left(d_st.at[0, :PB], sd.at[n, 0], rx.at[0])
                left(d_st.at[0, :PB], sd.at[n, 1], rx.at[0])

        for i in range(10):
            left(block(0, 0), sa.at[i], ra.at[0])
        left(d_up, sb.at[0], rb.at[0])
        left(do_all.at[half, :], sb.at[2], rb.at[2])
        left(dp_all.at[0], sb.at[4], rb.at[4])

    @pl.when(outer)
    def _():
        for n in range(4):
            left(d_st.at[0, :PB], sd.at[n, 0], rx.at[0])
            left(d_sum.at[n], sl.at[n], rx.at[0])
            left(block(0, 0), sa.at[n], ra.at[0])
        left(o_chip, sb.at[1], rb.at[1])

    for b in range(4):
        @pl.when(z != b)
        def _():
            left(w_rc.at[0], sw.at[b], rw.at[0])

    for h in range(NH):
        hs = slice(h * HD, (h + 1) * HD)
        for j in range(3):
            left(q_rc.at[:, hs], sq.at[h, j], rq.at[h, j])
        z_left(v_st, v_r1, v_r2, hs, k_sems(sk, 0, h), k_sems(rk, 0, h))
        z_left(k_st, k_r1, k_r2, hs, k_sems(sk, 1, h), k_sems(rk, 1, h))


def results(*refs):
    for src, dst in zip(refs[:5], refs[5:]):
        dst[...] = src[...]


def per_device(queries, keys_tile, values_tile, out_weight, out_grad):
    def vm(shape, dtype=BF16):
        return pltpu.VMEM(shape, dtype)

    dma = pltpu.SemaphoreType.DMA
    spec = pl.BlockSpec(memory_space=pltpu.VMEM)
    shapes = (
        jax.ShapeDtypeStruct((TB, DC), BF16),
        jax.ShapeDtypeStruct((TB, HC), BF16),
        jax.ShapeDtypeStruct((TB, HC), BF16),
        jax.ShapeDtypeStruct((TB, HC), BF16),
        jax.ShapeDtypeStruct((TB, DC), BF16),
    )
    outs = pl.pallas_call(
        kernel,
        out_shape=shapes,
        in_specs=[pl.BlockSpec(memory_space=pl.ANY)] * 5,
        out_specs=(spec,) * 5,
        scratch_shapes=[
            vm((ZT, HC)), vm((ZT, HC)), vm((ZT, HC)), vm((ZT, DC)), vm((ZT, DC)), vm((HC, ZT)), vm((HC, ZT), F32),
            vm((HC, ZT)), vm((TB, ZT)), vm((TB, ZT)), vm((TB, ZT)),
            *[vm((8, ZT), F32) for _ in range(9)],
            vm((ZT, ZT)), vm((4, TB, ZT)), vm((4, PB, ZT)), vm((4, PB, ZT)), vm((4, TB, ZT)), vm((TB, ZT)),
            vm((TB, ZT)), vm((HC, ZT)), vm((2, 8, ZT), F32), vm((8, ZT), F32),
            vm((ZT, HD), F32), vm((ZT, HD), F32), vm((ZT, HC)), vm((ZT, HC)), vm((ZT, HC)),
            vm((2, PB, HC)), vm((2, PB, HC)), vm((2, TB, HC)), vm((2, TB, HC)),
            vm((2, TB, HC)), vm((TB, HC)), vm((TB, HC)),
            vm((ZT, DC)), vm((2, TB, DC)), vm((TB, DC)), vm((TB, DC)),
            vm((ZT, DC)), vm((4, TB, DC)),
            dma((6, 4)), dma((6, 4)), dma((6, 3)), dma((6, 3)), dma((4, 2)), dma((4,)), dma((4,)), dma((8,)),
            dma((10,)), dma((8,)), dma((8,)), dma((6,)), dma((6,)), dma((2, 3, 4)), dma((2, 3, 4)),
            dma((3, 3)), dma((3, 3)), dma((4,)), dma((4,)), dma((5,)), vm((NH * ZT, ZT)),
        ],
        compiler_params=pltpu.CompilerParams(
            collective_id=0, has_side_effects=True, vmem_limit_bytes=60 * 1024 * 1024
        ),
    )(queries, keys_tile, values_tile, out_weight, out_grad)
    return pl.pallas_call(results, out_shape=shapes, in_specs=[spec] * 5, out_specs=(spec,) * 5)(*outs)


def solution(mesh):
    spec = P("row", "col")
    return jax.shard_map(
        per_device, mesh=mesh, in_specs=(spec,) * 5, out_specs=(spec,) * 5, check_vma=False
    )
```

```python
import jax
import jax.numpy as jnp
from jax import lax
from jax.experimental import pallas as pl
from jax.experimental.pallas import tpu as pltpu
from jax.sharding import PartitionSpec as P

HD = 128
NH = 3
TB = 192
ZT = 4 * TB
HC = NH * HD
DC = 768
PB = HC // 4
NK = 3 * TB
QT = 256
SCALE = HD ** (-0.5)
LOG2E = 1.4426950408889634
MESH = pl.DeviceIdType.MESH
F32 = jnp.float32
BF16 = jnp.bfloat16


def dot(a, b, ca, cb):
    return lax.dot_general(a, b, (((ca,), (cb,)), ((), ())), preferred_element_type=F32)


def kernel(
    q_ref, k_ref, v_ref, w_ref, g_ref,
    mixed_o, dq_o, dk_o, dv_o, wg_o,
    k_all, v_all, q_all, w_all, g_all, kt, o_acc,
    o_st, o_core, o_chip, o_far, lse_own, lse_core, lse_chip, lse_far, lse_c, w_own, w_core, w_chip, w_far,
    attn_all, d_st, d_r1, d_sum, d_rc, d_up, d_yl, do_all, dp_all, delta,
    kacc, vacc, k_st, v_st, q_st, k_r1, v_r1, k_r2, v_r2, q_core, q_up, q_rc,
    m_st, m_core, m_up, m_rc, w_st, w_rc,
    sz, rz, sy, ry, sd, rx, sl, rd, sa, ra, rh, sb, rb, sk, rk, sq, rq, sw, rw, si, p_all,
):
    row, col = lax.axis_index("row"), lax.axis_index("col")
    z, q = row // 4, row % 4
    yh, co = q // 2, q % 2
    yl, x = col // 4, col % 4
    inner = x % 2 == yh
    outer = x % 2 != yh
    x_up, x_dn, other_yl = yl * 4 + (x + 1) % 4, yl * 4 + (x + 3) % 4, (1 - yl) * 4 + x
    z_up, z_dn, z_op = (z + 1) % 4, (z + 3) % 4, (z + 2) % 4
    up, dn = z_up * 4 + q, z_dn * 4 + q

    def ypeer(j):
        a = yh if j < 2 else 1 - yh
        b = co if j % 2 == 0 else 1 - co
        return a * 2 + b

    core = z * 4 + ypeer(1)
    far = z * 4 + ypeer(2)

    def copy(src, dst, ss, rs, r, c):
        return pltpu.make_async_remote_copy(
            src_ref=src, dst_ref=dst, send_sem=ss, recv_sem=rs, device_id=(r, c), device_id_type=MESH
        )

    def send(src, dst, ss, rs, r, c):
        d = copy(src, dst, ss, rs, r, c)
        d.start()
        return d

    def recv(dst, ss, rs):
        copy(dst, dst, ss, rs, row, col).wait_recv()

    def left(src, ss, rs):
        copy(src, src, ss, rs, row, col).wait_send()

    def rows(i, n):
        return pl.ds(i * n if isinstance(i, int) else pl.multiple_of(i * n, n), n)

    own_copies = [
        pltpu.make_async_copy(src, dst.at[rows(i, TB), :], si.at[n])
        for n, (src, dst, i) in enumerate(
            ((k_ref, k_all, 0), (q_ref, q_all, q), (v_ref, v_all, 0), (g_ref, g_all, q), (w_ref, w_all, z))
        )
    ]
    for c in own_copies:
        c.start()

    barrier = pltpu.get_barrier_semaphore()

    def greet(r, c):
        pl.semaphore_signal(barrier, inc=1, device_id=(r, c), device_id_type=MESH)

    for r in (up, dn, z_op * 4 + q, core, far):
        greet(r, col)
    for c in (x_up, x_dn, other_yl):
        greet(row, c)
    pl.semaphore_wait(barrier, 8)

    sends = []

    def lower(b):
        return rows(2 * b, PB)

    def upper(b):
        return rows(2 * b + 1, PB)

    def z_start(i, src, dst, at_up, at_dn):
        sends.append(send(src, dst.at[rows(at_up, TB), :], sz.at[i, 0], rz.at[i, 0], up, col))
        sends.append(send(src, dst.at[rows(at_dn, TB), :], sz.at[i, 1], rz.at[i, 1], dn, col))

    def z_pass(i, dst, b_dn, b_up, at_up, at_dn):
        recv(dst.at[rows(b_dn, TB), :], sz.at[i, 0], rz.at[i, 0])
        sends.append(send(dst.at[lower(b_dn), :], dst.at[lower(at_up), :], sz.at[i, 2], rz.at[i, 2], up, col))
        recv(dst.at[rows(b_up, TB), :], sz.at[i, 1], rz.at[i, 1])
        sends.append(send(dst.at[upper(b_up), :], dst.at[upper(at_dn), :], sz.at[i, 3], rz.at[i, 3], dn, col))

    def z_last(i, dst, b):
        recv(dst.at[lower(b), :], sz.at[i, 2], rz.at[i, 2])
        recv(dst.at[upper(b), :], sz.at[i, 3], rz.at[i, 3])

    def to_y(i, j, src, dst):
        sends.append(send(src, dst, sy.at[i, j - 1], ry.at[i, j - 1], far if j == 2 else core, col))

    def from_y(i, j, dst):
        recv(dst, sy.at[i, j - 1], ry.at[i, j - 1])

    z_start(0, k_ref, k_all, 1, 2)
    to_y(0, 2, q_ref, q_all.at[rows(q, TB), :])
    to_y(0, 1, q_ref, q_all.at[rows(q, TB), :])
    z_start(1, v_ref, v_all, 1, 2)
    to_y(1, 2, g_ref, g_all.at[rows(q, TB), :])
    to_y(1, 1, g_ref, g_all.at[rows(q, TB), :])
    lse_own[...] = jnp.zeros_like(lse_own)
    dp_all[co] = jnp.zeros((8, ZT), F32)

    for c in own_copies:
        c.wait()

    part_far = rows(ypeer(2), TB)
    z_pass(0, k_all, 1, 2, 3, 3)
    from_y(0, 2, q_all.at[part_far, :])
    to_y(0, 3, q_all.at[part_far, :], q_all.at[part_far, :])
    z_pass(1, v_all, 1, 2, 3, 3)
    z_start(2, w_ref, w_all, z, z)
    for j in (1, 3):
        from_y(0, j, q_all.at[rows(ypeer(j), TB), :])
    def forward(h, carry):
        hs = rows(h, HD)
        kh, vh = k_all[:NK, hs], v_all[:NK, hs]
        for t in range(3):
            ts = slice(t * QT, (t + 1) * QT)
            s = dot(kh, q_all[ts, hs], 1, 1)
            top = jnp.max(s, axis=0, keepdims=True)
            p = jnp.exp2((s - top) * (SCALE * LOG2E))
            o_acc[hs, ts] = dot(vh, p.astype(BF16), 0, 0)
            w_own[pl.ds(h, 1), ts] = top
            w_core[pl.ds(h, 1), ts] = jnp.sum(p, axis=0, keepdims=True)
        return carry

    def forward_last(h, carry):
        hs = rows(h, HD)
        kh, vh = k_all[NK:, hs], v_all[NK:, hs]
        for t in range(3):
            ts = slice(t * QT, (t + 1) * QT)
            s = dot(kh, q_all[ts, hs], 1, 1)
            old = w_own[pl.ds(h, 1), ts]
            top = jnp.maximum(jnp.max(s, axis=0, keepdims=True), old)
            p = jnp.exp2((s - top) * (SCALE * LOG2E))
            keep = jnp.exp2((old - top) * (SCALE * LOG2E))
            total = keep * w_core[pl.ds(h, 1), ts] + jnp.sum(p, axis=0, keepdims=True)
            o = keep * o_acc[hs, ts] + dot(vh, p.astype(BF16), 0, 0)
            o_st[hs, ts] = (o / total).astype(BF16)
            lse_own[pl.ds(h, 1), ts] = top * (SCALE * LOG2E) + jnp.log2(total)
        return carry

    def slot_of(c, other):
        return 2 * (1 - yl if other else yl) + c % 4 // 2

    slot_a, slot_b = slot_of(x, False), slot_of(x, True)

    def d_attn(n, zp):
        d_st[zp] = dot(w_all[rows(zp, TB), :], g_all[...], 1, 1).astype(BF16)
        tx = 2 * (zp % 2) + yh
        piece = jnp.where(zp // 2 == yl, 0, 1)

        @pl.when(inner & (tx != x))
        def _():
            send(d_st.at[zp, :PB], d_r1.at[piece], sd.at[n, 0], rx.at[piece], row, x_up)
            send(d_st.at[zp, PB:], d_r1.at[2 + piece], sd.at[n, 1], rx.at[2 + piece], row, x_dn)

        @pl.when(outer & (tx == (x + 1) % 4))
        def _():
            send(d_st.at[zp, PB:], d_rc.at[piece, PB:], sd.at[n, 0], rd.at[2 * piece + 1], row, x_up)

        @pl.when(outer & (tx == (x + 3) % 4))
        def _():
            send(d_st.at[zp, :PB], d_rc.at[2 + piece, :PB], sd.at[n, 0], rd.at[4 + 2 * piece], row, x_dn)

    lax.fori_loop(0, NH, forward, 0)
    from_y(1, 2, g_all.at[part_far, :])
    to_y(1, 3, g_all.at[part_far, :], g_all.at[part_far, :])
    z_last(0, k_all, 3)
    z_last(1, v_all, 3)
    lax.fori_loop(0, NH, forward_last, 0)

    to_y(3, 1, lse_own, lse_core)
    to_y(2, 1, o_st.at[rows(1 - co, TB), :], o_core)
    for j in (1, 3):
        from_y(1, j, g_all.at[rows(ypeer(j), TB), :])
    z_pass(2, w_all, z_dn, z_up, z_dn, z_up)
    d_attn(0, z)
    d_attn(1, z_dn)
    d_attn(2, z_up)

    def both(a, b):
        top = jnp.maximum(a, b)
        lse = top + jnp.log2(jnp.exp2(a - top) + jnp.exp2(b - top))
        return lse, jnp.exp2(a - lse), jnp.exp2(b - lse)

    def pieces():
        for i in range(3):
            yield (
                pl.ds((3 * co + i) // 2, 1),
                slice(i * 64, (i + 1) * 64),
                pl.ds(pl.multiple_of(co * TB + i * 64, 64), 64),
                pl.ds(pl.multiple_of(slot_a * TB + i * 64, 64), 64),
            )

    from_y(3, 1, lse_core)
    lse_chip[...], w_own[...], w_core[...] = both(lse_own[...], lse_core[...])
    to_y(3, 2, lse_chip, lse_far)
    from_y(2, 1, o_core)
    for head, part, src, to in pieces():
        o_chip[part, :] = (
            w_own[head, :] * o_st[src, :].astype(F32) + w_core[head, :] * o_core[part, :].astype(F32)
        ).astype(BF16)

    @pl.when(outer)
    def _():
        send(o_chip, o_far, sb.at[1], rb.at[1], far, col)

    z_last(2, w_all, z_op)
    d_attn(3, z_op)
    from_y(3, 2, lse_far)
    lse_c[...], w_chip[...], w_far[...] = both(lse_chip[...], lse_far[...])
    half = rows(co, TB)

    def again(h, carry):
        hs = rows(h, HD)
        kh = k_all[:, hs]
        for t in range(3):
            ts = slice(t * QT, (t + 1) * QT)
            s = dot(kh, q_all[ts, hs], 1, 1)
            p_all[rows(h, ZT), ts] = jnp.exp2(s * (SCALE * LOG2E) - lse_c[pl.ds(h, 1), ts]).astype(BF16)
        return carry

    def block(b, i):
        return attn_all.at[rows(2 * b + i, PB), :]

    def weight_part(b):
        w_st[rows(b, TB), :] = dot(attn_all[rows(b, TB), :], g_all[...], 1, 0).astype(BF16)

        @pl.when(b != z)
        def _():
            send(w_st.at[rows(b, TB), :], w_rc.at[z], sw.at[b], rw.at[z], b * 4 + q, col)

    @pl.when(inner)
    def _():
        lax.fori_loop(0, NH, again, 0)
        recv(o_far, sb.at[1], rb.at[1])
        for head, part, src, to in pieces():
            attn_all[to, :] = (
                w_chip[head, :] * o_chip[part, :].astype(F32) + w_far[head, :] * o_far[part, :].astype(F32)
            ).astype(BF16)
        def pass_on(b, i, n, to):
            send(block(b, i), block(b, i), sa.at[n], ra.at[2 * b + i], row, to)

        pass_on(slot_a, 0, 0, other_yl)
        pass_on(slot_a, 0, 2, x_up)
        pass_on(slot_a, 1, 4, x_dn)
        pass_on(slot_a, 1, 1, other_yl)
        pass_on(slot_a, 1, 3, x_up)
        pass_on(slot_a, 0, 5, x_dn)
        weight_part(slot_a)
        for i in (2, 3, 6, 7):
            recv(d_rc.at[i // 4 * 2 + 1, i % 2 * PB : (i % 2 + 1) * PB], sd.at[0, 0], rd.at[i])
        d_up[...] = (d_st[slot_b].astype(F32) + d_rc[1].astype(F32) + d_rc[3].astype(F32)).astype(BF16)
        send(d_up, d_yl, sb.at[0], rb.at[0], row, other_yl)
        recv(block(slot_b, 0), sa.at[0], ra.at[2 * slot_b])
        pass_on(slot_b, 0, 6, x_up)
        recv(block(slot_b, 1), sa.at[0], ra.at[2 * slot_b + 1])
        pass_on(slot_b, 1, 7, x_dn)
        pass_on(slot_b, 1, 8, x_up)
        pass_on(slot_b, 0, 9, x_dn)
        weight_part(slot_b)
        for i in (0, 1, 4, 5):
            recv(d_rc.at[i // 4 * 2, i % 2 * PB : (i % 2 + 1) * PB], sd.at[0, 0], rd.at[i])
        recv(d_yl, sb.at[0], rb.at[0])
        do_all[half, :] = (
            d_st[slot_a].astype(F32) + d_rc[0].astype(F32) + d_rc[2].astype(F32) + d_yl[...].astype(F32)
        ).astype(BF16)
        send(do_all.at[half, :], do_all.at[half, :], sb.at[2], rb.at[2], far, col)
        send(do_all.at[half, :], do_all.at[half, :], sb.at[3], rb.at[3], core, col)
        for head, part, src, to in pieces():
            dp_all[co, head, :] += jnp.sum(
                do_all[src, :].astype(F32) * attn_all[to, :].astype(F32), axis=0, keepdims=True
            )
        send(dp_all.at[co], dp_all.at[co], sb.at[4], rb.at[4], far, col)
        send(dp_all.at[co], dp_all.at[co], sb.at[5], rb.at[5], core, col)

    @pl.when(outer)
    def _():
        for p in (1, 0):
            s_up, s_dn = slot_of(x + 1, p == 1), slot_of(x + 3, p == 1)
            recv(d_r1.at[p], sd.at[0, 0], rx.at[p])
            d_sum[p] = (d_st[s_up, :PB].astype(F32) + d_r1[p].astype(F32)).astype(BF16)
            send(d_sum.at[p], d_rc.at[p, :PB], sl.at[p], rd.at[2 * p], row, x_up)
            recv(d_r1.at[2 + p], sd.at[0, 0], rx.at[2 + p])
            d_sum[2 + p] = (d_st[s_dn, PB:].astype(F32) + d_r1[2 + p].astype(F32)).astype(BF16)
            send(d_sum.at[2 + p], d_rc.at[2 + p, PB:], sl.at[2 + p], rd.at[4 + 2 * p + 1], row, x_dn)
        lax.fori_loop(0, NH, again, 0)
        for p in range(2):
            s_up, s_dn = slot_of(x + 1, p == 1), slot_of(x + 3, p == 1)
            recv(block(s_dn, 0), sa.at[0], ra.at[2 * s_dn])
            send(block(s_dn, 0), block(s_dn, 0), sa.at[p], rh.at[2 * s_dn], row, x_up)
            recv(block(s_up, 1), sa.at[0], ra.at[2 * s_up + 1])
            send(block(s_up, 1), block(s_up, 1), sa.at[2 + p], rh.at[2 * s_up + 1], row, x_dn)
            recv(block(s_dn, 1), sa.at[0], ra.at[2 * s_dn + 1])
            weight_part(s_dn)
            recv(block(s_up, 0), sa.at[0], ra.at[2 * s_up])
            weight_part(s_up)

    def z_add(st, r1, r2, hs, ss, rs):
        recv(r1.at[0, :, hs], ss(0), rs(0))
        a, b = lower(2), upper(1)
        st[a, hs] = (st[a, hs].astype(F32) + r1[0, :, hs].astype(F32)).astype(BF16)
        send(st.at[rows(2, TB), hs], r2.at[0, :, hs], ss(2), rs(2), up, col)
        recv(r1.at[1, :, hs], ss(1), rs(1))
        st[b, hs] = (st[b, hs].astype(F32) + r1[1, :, hs].astype(F32)).astype(BF16)
        send(st.at[rows(1, TB), hs], r2.at[1, :, hs], ss(3), rs(3), dn, col)

    def z_sum(st, r2, hs, ss, rs):
        recv(r2.at[0, :, hs], ss(2), rs(2))
        recv(r2.at[1, :, hs], ss(3), rs(3))
        return (
            st[rows(0, TB), hs].astype(F32) + r2[0, :, hs].astype(F32) + r2[1, :, hs].astype(F32)
        ).astype(BF16)

    def z_left(st, r1, r2, hs, ss, rs):
        for j in range(2):
            left(r1.at[0, :, hs], ss(j), rs(j))
            left(r2.at[0, :, hs], ss(2 + j), rs(2 + j))

    @pl.when(inner)
    def _():
        for p in range(2):
            b = slot_of(x + 2, p == 1)
            for i in range(2):
                recv(block(b, i), sa.at[0], rh.at[2 * b + i])
            weight_part(b)

    @pl.when(outer)
    def _():
        recv(do_all.at[half, :], sb.at[2], rb.at[2])
        send(do_all.at[half, :], do_all.at[half, :], sb.at[3], rb.at[3], core, col)
        recv(dp_all.at[co], sb.at[4], rb.at[4])
        send(dp_all.at[co], dp_all.at[co], sb.at[5], rb.at[5], core, col)

    def mixed_part(i, carry):
        m_st[rows(i, QT), :] = dot(attn_all[:, rows(i, QT)], w_all[...], 0, 0).astype(BF16)
        return carry

    lax.fori_loop(0, 3, mixed_part, 0)
    to_y(5, 3, m_st.at[rows(ypeer(3), TB), :], m_core.at[1])
    to_y(5, 1, m_st.at[rows(ypeer(1), TB), :], m_core.at[0])

    kt[...] = k_all[...].T
    recv(do_all.at[rows(1 - co, TB), :], sb.at[3], rb.at[3])
    recv(dp_all.at[1 - co], sb.at[5], rb.at[5])
    delta[...] = dp_all[0] + dp_all[1]
    from_y(5, 3, m_core.at[1])
    m_up[...] = (m_st[part_far, :].astype(F32) + m_core[1].astype(F32)).astype(BF16)
    to_y(5, 2, m_up, m_rc)

    def k_sems(sem, i, h):
        return lambda j: sem.at[i, h, j]

    def head_next(h):
        hs = rows(h, HD)
        recv(q_core.at[1, :, hs], sq.at[h, 2], rq.at[h, 2])
        q_up[:, hs] = (q_st[part_far, hs].astype(F32) + q_core[1, :, hs].astype(F32)).astype(BF16)
        send(q_up.at[:, hs], q_rc.at[:, hs], sq.at[h, 1], rq.at[h, 1], far, col)
        z_add(v_st, v_r1, v_r2, hs, k_sems(sk, 0, h), k_sems(rk, 0, h))
        z_add(k_st, k_r1, k_r2, hs, k_sems(sk, 1, h), k_sems(rk, 1, h))

    def backward(h, carry):
        hs = rows(h, HD)
        kh = k_all[:, hs]
        vh = v_all[:, hs]
        for t in range(3):
            ts = slice(t * QT, (t + 1) * QT)
            qh = q_all[ts, hs]
            doh = do_all[hs, ts]
            p = p_all[rows(h, ZT), ts]
            dprob = dot(vh, doh, 1, 0)
            ds = (p.astype(F32) * (dprob - delta[pl.ds(h, 1), ts]) * SCALE).astype(BF16)
            dvt = dot(p, doh, 1, 1)
            dkt = dot(ds, qh, 1, 0)
            if t == 0:
                vacc[...] = dvt
                kacc[...] = dkt
            else:
                vacc[...] += dvt
                kacc[...] += dkt
            q_st[ts, hs] = dot(kt[hs, :], ds, 1, 0).T.astype(BF16)
        v_st[:, hs] = vacc[...].astype(BF16)
        k_st[:, hs] = kacc[...].astype(BF16)
        for i, (st, r1) in enumerate(((v_st, v_r1), (k_st, k_r1))):
            send(st.at[lower(3), hs], r1.at[0, :, hs], sk.at[i, h, 0], rk.at[i, h, 0], up, col)
            send(st.at[upper(3), hs], r1.at[1, :, hs], sk.at[i, h, 1], rk.at[i, h, 1], dn, col)
        send(q_st.at[rows(ypeer(3), TB), hs], q_core.at[1, :, hs], sq.at[h, 2], rq.at[h, 2], core, col)
        send(q_st.at[rows(ypeer(1), TB), hs], q_core.at[0, :, hs], sq.at[h, 0], rq.at[h, 0], core, col)

        @pl.when(h > 0)
        def _():
            head_next(h - 1)

        return carry

    lax.fori_loop(0, NH, backward, 0)
    head_next(NH - 1)

    from_y(5, 1, m_core.at[0])
    from_y(5, 2, m_rc)
    mixed_o[...] = (m_st[rows(q, TB), :].astype(F32) + m_core[0].astype(F32) + m_rc[...].astype(F32)).astype(BF16)
    total = w_st[rows(z, TB), :].astype(F32)
    for d in (1, 3, 2):
        src = (z + d) % 4
        recv(w_rc.at[src], sw.at[0], rw.at[src])
        total += w_rc[src].astype(F32)
    wg_o[...] = total.astype(BF16)
    for h in range(NH):
        hs = slice(h * HD, (h + 1) * HD)
        recv(q_core.at[0, :, hs], sq.at[h, 0], rq.at[h, 0])
        recv(q_rc.at[:, hs], sq.at[h, 1], rq.at[h, 1])
        dq_o[:, hs] = (
            q_st[rows(q, TB), hs].astype(F32) + q_core[0, :, hs].astype(F32) + q_rc[:, hs].astype(F32)
        ).astype(BF16)
        dv_o[:, hs] = z_sum(v_st, v_r2, hs, k_sems(sk, 0, h), k_sems(rk, 0, h))
        dk_o[:, hs] = z_sum(k_st, k_r2, hs, k_sems(sk, 1, h), k_sems(rk, 1, h))

    for d in sends:
        d.wait_send()
    left(do_all.at[half, :], sb.at[3], rb.at[3])
    left(dp_all.at[0], sb.at[5], rb.at[5])

    @pl.when(inner)
    def _():
        for n, zp in enumerate((z, z_dn, z_up, z_op)):
            @pl.when(2 * (zp % 2) + yh != x)
            def _():
                left(d_st.at[0, :PB], sd.at[n, 0], rx.at[0])
                left(d_st.at[0, :PB], sd.at[n, 1], rx.at[0])

        for i in range(10):
            left(block(0, 0), sa.at[i], ra.at[0])
        left(d_up, sb.at[0], rb.at[0])
        left(do_all.at[half, :], sb.at[2], rb.at[2])
        left(dp_all.at[0], sb.at[4], rb.at[4])

    @pl.when(outer)
    def _():
        for n in range(4):
            left(d_st.at[0, :PB], sd.at[n, 0], rx.at[0])
            left(d_sum.at[n], sl.at[n], rx.at[0])
            left(block(0, 0), sa.at[n], ra.at[0])
        left(o_chip, sb.at[1], rb.at[1])

    for b in range(4):
        @pl.when(z != b)
        def _():
            left(w_rc.at[0], sw.at[b], rw.at[0])

    for h in range(NH):
        hs = slice(h * HD, (h + 1) * HD)
        for j in range(3):
            left(q_rc.at[:, hs], sq.at[h, j], rq.at[h, j])
        z_left(v_st, v_r1, v_r2, hs, k_sems(sk, 0, h), k_sems(rk, 0, h))
        z_left(k_st, k_r1, k_r2, hs, k_sems(sk, 1, h), k_sems(rk, 1, h))


def results(*refs):
    for src, dst in zip(refs[:5], refs[5:]):
        dst[...] = src[...]


def per_device(queries, keys_tile, values_tile, out_weight, out_grad):
    def vm(shape, dtype=BF16):
        return pltpu.VMEM(shape, dtype)

    dma = pltpu.SemaphoreType.DMA
    spec = pl.BlockSpec(memory_space=pltpu.VMEM)
    shapes = (
        jax.ShapeDtypeStruct((TB, DC), BF16),
        jax.ShapeDtypeStruct((TB, HC), BF16),
        jax.ShapeDtypeStruct((TB, HC), BF16),
        jax.ShapeDtypeStruct((TB, HC), BF16),
        jax.ShapeDtypeStruct((TB, DC), BF16),
    )
    outs = pl.pallas_call(
        kernel,
        out_shape=shapes,
        in_specs=[pl.BlockSpec(memory_space=pl.ANY)] * 5,
        out_specs=(spec,) * 5,
        scratch_shapes=[
            vm((ZT, HC)), vm((ZT, HC)), vm((ZT, HC)), vm((ZT, DC)), vm((ZT, DC)), vm((HC, ZT)), vm((HC, ZT), F32),
            vm((HC, ZT)), vm((TB, ZT)), vm((TB, ZT)), vm((TB, ZT)),
            *[vm((8, ZT), F32) for _ in range(9)],
            vm((ZT, ZT)), vm((4, TB, ZT)), vm((4, PB, ZT)), vm((4, PB, ZT)), vm((4, TB, ZT)), vm((TB, ZT)),
            vm((TB, ZT)), vm((HC, ZT)), vm((2, 8, ZT), F32), vm((8, ZT), F32),
            vm((ZT, HD), F32), vm((ZT, HD), F32), vm((ZT, HC)), vm((ZT, HC)), vm((ZT, HC)),
            vm((2, PB, HC)), vm((2, PB, HC)), vm((2, TB, HC)), vm((2, TB, HC)),
            vm((2, TB, HC)), vm((TB, HC)), vm((TB, HC)),
            vm((ZT, DC)), vm((2, TB, DC)), vm((TB, DC)), vm((TB, DC)),
            vm((ZT, DC)), vm((4, TB, DC)),
            dma((6, 4)), dma((6, 4)), dma((6, 3)), dma((6, 3)), dma((4, 2)), dma((4,)), dma((4,)), dma((8,)),
            dma((10,)), dma((8,)), dma((8,)), dma((6,)), dma((6,)), dma((2, 3, 4)), dma((2, 3, 4)),
            dma((3, 3)), dma((3, 3)), dma((4,)), dma((4,)), dma((5,)), vm((NH * ZT, ZT)),
        ],
        compiler_params=pltpu.CompilerParams(
            collective_id=0, has_side_effects=True, vmem_limit_bytes=60 * 1024 * 1024
        ),
    )(queries, keys_tile, values_tile, out_weight, out_grad)
    return pl.pallas_call(results, out_shape=shapes, in_specs=[spec] * 5, out_specs=(spec,) * 5)(*outs)


def solution(mesh):
    spec = P("row", "col")
    return jax.shard_map(
        per_device, mesh=mesh, in_specs=(spec,) * 5, out_specs=(spec,) * 5, check_vma=False
    )
```

```python
import jax
import jax.numpy as jnp
from jax import lax
from jax.experimental import pallas as pl
from jax.experimental.pallas import tpu as pltpu
from jax.sharding import PartitionSpec as P

HD = 128
NH = 3
TB = 192
ZT = 4 * TB
HC = NH * HD
DC = 768
PB = HC // 4
NK = 3 * TB
QT = 256
SCALE = HD ** (-0.5)
LOG2E = 1.4426950408889634
MESH = pl.DeviceIdType.MESH
F32 = jnp.float32
BF16 = jnp.bfloat16


def dot(a, b, ca, cb):
    return lax.dot_general(a, b, (((ca,), (cb,)), ((), ())), preferred_element_type=F32)


def kernel(
    q_ref, k_ref, v_ref, w_ref, g_ref,
    mixed_o, dq_o, dk_o, dv_o, wg_o,
    k_all, v_all, q_all, w_all, g_all, kt, o_acc,
    o_st, o_core, o_chip, o_far, lse_own, lse_core, lse_chip, lse_far, lse_c, w_own, w_core, w_chip, w_far,
    attn_all, d_st, d_r1, d_sum, d_rc, d_up, d_yl, do_all, dp_all, delta,
    kacc, vacc, k_st, v_st, q_st, k_r1, v_r1, k_r2, v_r2, q_core, q_up, q_rc,
    m_st, m_core, m_up, m_rc, w_st, w_rc,
    sz, rz, sy, ry, sd, rx, sl, rd, sa, ra, rh, sb, rb, sk, rk, sq, rq, sw, rw, si, p_all,
):
    row, col = lax.axis_index("row"), lax.axis_index("col")
    z, q = row // 4, row % 4
    yh, co = q // 2, q % 2
    yl, x = col // 4, col % 4
    inner = x % 2 == yh
    outer = x % 2 != yh
    x_up, x_dn, other_yl = yl * 4 + (x + 1) % 4, yl * 4 + (x + 3) % 4, (1 - yl) * 4 + x
    z_up, z_dn, z_op = (z + 1) % 4, (z + 3) % 4, (z + 2) % 4
    up, dn = z_up * 4 + q, z_dn * 4 + q

    def ypeer(j):
        a = yh if j < 2 else 1 - yh
        b = co if j % 2 == 0 else 1 - co
        return a * 2 + b

    core = z * 4 + ypeer(1)
    far = z * 4 + ypeer(2)

    def copy(src, dst, ss, rs, r, c):
        return pltpu.make_async_remote_copy(
            src_ref=src, dst_ref=dst, send_sem=ss, recv_sem=rs, device_id=(r, c), device_id_type=MESH
        )

    def send(src, dst, ss, rs, r, c):
        d = copy(src, dst, ss, rs, r, c)
        d.start()
        return d

    def recv(dst, ss, rs):
        copy(dst, dst, ss, rs, row, col).wait_recv()

    def left(src, ss, rs):
        copy(src, src, ss, rs, row, col).wait_send()

    def rows(i, n):
        return pl.ds(i * n if isinstance(i, int) else pl.multiple_of(i * n, n), n)

    own_copies = [
        pltpu.make_async_copy(src, dst.at[rows(i, TB), :], si.at[n])
        for n, (src, dst, i) in enumerate(
            ((k_ref, k_all, 0), (q_ref, q_all, q), (v_ref, v_all, 0), (g_ref, g_all, q), (w_ref, w_all, z))
        )
    ]
    for c in own_copies:
        c.start()

    barrier = pltpu.get_barrier_semaphore()

    def greet(r, c):
        pl.semaphore_signal(barrier, inc=1, device_id=(r, c), device_id_type=MESH)

    for r in (up, dn, z_op * 4 + q, core, far):
        greet(r, col)
    for c in (x_up, x_dn, other_yl):
        greet(row, c)
    pl.semaphore_wait(barrier, 8)

    sends = []

    def lower(b):
        return rows(2 * b, PB)

    def upper(b):
        return rows(2 * b + 1, PB)

    def z_start(i, src, dst, at_up, at_dn):
        sends.append(send(src, dst.at[rows(at_up, TB), :], sz.at[i, 0], rz.at[i, 0], up, col))
        sends.append(send(src, dst.at[rows(at_dn, TB), :], sz.at[i, 1], rz.at[i, 1], dn, col))

    def z_pass(i, dst, b_dn, b_up, at_up, at_dn):
        recv(dst.at[rows(b_dn, TB), :], sz.at[i, 0], rz.at[i, 0])
        sends.append(send(dst.at[lower(b_dn), :], dst.at[lower(at_up), :], sz.at[i, 2], rz.at[i, 2], up, col))
        recv(dst.at[rows(b_up, TB), :], sz.at[i, 1], rz.at[i, 1])
        sends.append(send(dst.at[upper(b_up), :], dst.at[upper(at_dn), :], sz.at[i, 3], rz.at[i, 3], dn, col))

    def z_last(i, dst, b):
        recv(dst.at[lower(b), :], sz.at[i, 2], rz.at[i, 2])
        recv(dst.at[upper(b), :], sz.at[i, 3], rz.at[i, 3])

    def to_y(i, j, src, dst):
        sends.append(send(src, dst, sy.at[i, j - 1], ry.at[i, j - 1], far if j == 2 else core, col))

    def from_y(i, j, dst):
        recv(dst, sy.at[i, j - 1], ry.at[i, j - 1])

    z_start(0, k_ref, k_all, 1, 2)
    to_y(0, 2, q_ref, q_all.at[rows(q, TB), :])
    to_y(0, 1, q_ref, q_all.at[rows(q, TB), :])
    z_start(1, v_ref, v_all, 1, 2)
    to_y(1, 2, g_ref, g_all.at[rows(q, TB), :])
    to_y(1, 1, g_ref, g_all.at[rows(q, TB), :])
    lse_own[...] = jnp.zeros_like(lse_own)
    dp_all[co] = jnp.zeros((8, ZT), F32)

    for c in own_copies:
        c.wait()

    part_far = rows(ypeer(2), TB)
    z_pass(0, k_all, 1, 2, 3, 3)
    from_y(0, 2, q_all.at[part_far, :])
    to_y(0, 3, q_all.at[part_far, :], q_all.at[part_far, :])
    z_pass(1, v_all, 1, 2, 3, 3)
    z_start(2, w_ref, w_all, z, z)
    for j in (1, 3):
        from_y(0, j, q_all.at[rows(ypeer(j), TB), :])
    def forward(h, carry):
        hs = rows(h, HD)
        kh, vh = k_all[:NK, hs], v_all[:NK, hs]
        for t in range(3):
            ts = slice(t * QT, (t + 1) * QT)
            s = dot(kh, q_all[ts, hs], 1, 1)
            top = jnp.max(s, axis=0, keepdims=True)
            p = jnp.exp2((s - top) * (SCALE * LOG2E))
            o_acc[hs, ts] = dot(vh, p.astype(BF16), 0, 0)
            w_own[pl.ds(h, 1), ts] = top
            w_core[pl.ds(h, 1), ts] = jnp.sum(p, axis=0, keepdims=True)
        return carry

    def forward_last(h, carry):
        hs = rows(h, HD)
        kh, vh = k_all[NK:, hs], v_all[NK:, hs]
        for t in range(3):
            ts = slice(t * QT, (t + 1) * QT)
            s = dot(kh, q_all[ts, hs], 1, 1)
            old = w_own[pl.ds(h, 1), ts]
            top = jnp.maximum(jnp.max(s, axis=0, keepdims=True), old)
            p = jnp.exp2((s - top) * (SCALE * LOG2E))
            keep = jnp.exp2((old - top) * (SCALE * LOG2E))
            total = keep * w_core[pl.ds(h, 1), ts] + jnp.sum(p, axis=0, keepdims=True)
            o = keep * o_acc[hs, ts] + dot(vh, p.astype(BF16), 0, 0)
            o_st[hs, ts] = (o / total).astype(BF16)
            lse_own[pl.ds(h, 1), ts] = top * (SCALE * LOG2E) + jnp.log2(total)
        return carry

    def slot_of(c, other):
        return 2 * (1 - yl if other else yl) + c % 4 // 2

    slot_a, slot_b = slot_of(x, False), slot_of(x, True)

    def d_attn(n, zp):
        d_st[zp] = dot(w_all[rows(zp, TB), :], g_all[...], 1, 1).astype(BF16)
        tx = 2 * (zp % 2) + yh
        piece = jnp.where(zp // 2 == yl, 0, 1)

        @pl.when(inner & (tx != x))
        def _():
            send(d_st.at[zp, :PB], d_r1.at[piece], sd.at[n, 0], rx.at[piece], row, x_up)
            send(d_st.at[zp, PB:], d_r1.at[2 + piece], sd.at[n, 1], rx.at[2 + piece], row, x_dn)

        @pl.when(outer & (tx == (x + 1) % 4))
        def _():
            send(d_st.at[zp, PB:], d_rc.at[piece, PB:], sd.at[n, 0], rd.at[2 * piece + 1], row, x_up)

        @pl.when(outer & (tx == (x + 3) % 4))
        def _():
            send(d_st.at[zp, :PB], d_rc.at[2 + piece, :PB], sd.at[n, 0], rd.at[4 + 2 * piece], row, x_dn)

    lax.fori_loop(0, NH, forward, 0)
    from_y(1, 2, g_all.at[part_far, :])
    to_y(1, 3, g_all.at[part_far, :], g_all.at[part_far, :])
    z_last(0, k_all, 3)
    z_last(1, v_all, 3)
    lax.fori_loop(0, NH, forward_last, 0)

    to_y(3, 1, lse_own, lse_core)
    to_y(2, 1, o_st.at[rows(1 - co, TB), :], o_core)
    kt[...] = k_all[...].T
    for j in (1, 3):
        from_y(1, j, g_all.at[rows(ypeer(j), TB), :])
    z_pass(2, w_all, z_dn, z_up, z_dn, z_up)
    d_attn(0, z)
    d_attn(1, z_dn)
    d_attn(2, z_up)

    def both(a, b):
        top = jnp.maximum(a, b)
        lse = top + jnp.log2(jnp.exp2(a - top) + jnp.exp2(b - top))
        return lse, jnp.exp2(a - lse), jnp.exp2(b - lse)

    def pieces():
        for i in range(3):
            yield (
                pl.ds((3 * co + i) // 2, 1),
                slice(i * 64, (i + 1) * 64),
                pl.ds(pl.multiple_of(co * TB + i * 64, 64), 64),
                pl.ds(pl.multiple_of(slot_a * TB + i * 64, 64), 64),
            )

    from_y(3, 1, lse_core)
    lse_chip[...], w_own[...], w_core[...] = both(lse_own[...], lse_core[...])
    to_y(3, 2, lse_chip, lse_far)
    from_y(2, 1, o_core)
    for head, part, src, to in pieces():
        o_chip[part, :] = (
            w_own[head, :] * o_st[src, :].astype(F32) + w_core[head, :] * o_core[part, :].astype(F32)
        ).astype(BF16)

    @pl.when(outer)
    def _():
        send(o_chip, o_far, sb.at[1], rb.at[1], far, col)

    z_last(2, w_all, z_op)
    d_attn(3, z_op)
    from_y(3, 2, lse_far)
    lse_c[...], w_chip[...], w_far[...] = both(lse_chip[...], lse_far[...])
    half = rows(co, TB)

    def again(h, carry):
        hs = rows(h, HD)
        kh = k_all[:, hs]
        for t in range(3):
            ts = slice(t * QT, (t + 1) * QT)
            s = dot(kh, q_all[ts, hs], 1, 1)
            p_all[rows(h, ZT), ts] = jnp.exp2(s * (SCALE * LOG2E) - lse_c[pl.ds(h, 1), ts]).astype(BF16)
        return carry

    def block(b, i):
        return attn_all.at[rows(2 * b + i, PB), :]

    def weight_part(b):
        w_st[rows(b, TB), :] = dot(attn_all[rows(b, TB), :], g_all[...], 1, 0).astype(BF16)

        @pl.when(b != z)
        def _():
            send(w_st.at[rows(b, TB), :], w_rc.at[z], sw.at[b], rw.at[z], b * 4 + q, col)

    @pl.when(inner)
    def _():
        lax.fori_loop(0, NH, again, 0)
        recv(o_far, sb.at[1], rb.at[1])
        for head, part, src, to in pieces():
            attn_all[to, :] = (
                w_chip[head, :] * o_chip[part, :].astype(F32) + w_far[head, :] * o_far[part, :].astype(F32)
            ).astype(BF16)
        def pass_on(b, i, n, to):
            send(block(b, i), block(b, i), sa.at[n], ra.at[2 * b + i], row, to)

        pass_on(slot_a, 0, 0, other_yl)
        pass_on(slot_a, 0, 2, x_up)
        pass_on(slot_a, 1, 4, x_dn)
        pass_on(slot_a, 1, 1, other_yl)
        pass_on(slot_a, 1, 3, x_up)
        pass_on(slot_a, 0, 5, x_dn)
        weight_part(slot_a)
        for i in (2, 3, 6, 7):
            recv(d_rc.at[i // 4 * 2 + 1, i % 2 * PB : (i % 2 + 1) * PB], sd.at[0, 0], rd.at[i])
        d_up[...] = (d_st[slot_b].astype(F32) + d_rc[1].astype(F32) + d_rc[3].astype(F32)).astype(BF16)
        send(d_up, d_yl, sb.at[0], rb.at[0], row, other_yl)
        recv(block(slot_b, 0), sa.at[0], ra.at[2 * slot_b])
        pass_on(slot_b, 0, 6, x_up)
        recv(block(slot_b, 1), sa.at[0], ra.at[2 * slot_b + 1])
        pass_on(slot_b, 1, 7, x_dn)
        pass_on(slot_b, 1, 8, x_up)
        pass_on(slot_b, 0, 9, x_dn)
        weight_part(slot_b)
        for i in (0, 1, 4, 5):
            recv(d_rc.at[i // 4 * 2, i % 2 * PB : (i % 2 + 1) * PB], sd.at[0, 0], rd.at[i])
        recv(d_yl, sb.at[0], rb.at[0])
        do_all[half, :] = (
            d_st[slot_a].astype(F32) + d_rc[0].astype(F32) + d_rc[2].astype(F32) + d_yl[...].astype(F32)
        ).astype(BF16)
        send(do_all.at[half, :], do_all.at[half, :], sb.at[2], rb.at[2], far, col)
        send(do_all.at[half, :], do_all.at[half, :], sb.at[3], rb.at[3], core, col)
        for head, part, src, to in pieces():
            dp_all[co, head, :] += jnp.sum(
                do_all[src, :].astype(F32) * attn_all[to, :].astype(F32), axis=0, keepdims=True
            )
        send(dp_all.at[co], dp_all.at[co], sb.at[4], rb.at[4], far, col)
        send(dp_all.at[co], dp_all.at[co], sb.at[5], rb.at[5], core, col)

    @pl.when(outer)
    def _():
        lax.fori_loop(0, NH, again, 0)
        for p in (1, 0):
            s_up, s_dn = slot_of(x + 1, p == 1), slot_of(x + 3, p == 1)
            recv(d_r1.at[p], sd.at[0, 0], rx.at[p])
            d_sum[p] = (d_st[s_up, :PB].astype(F32) + d_r1[p].astype(F32)).astype(BF16)
            send(d_sum.at[p], d_rc.at[p, :PB], sl.at[p], rd.at[2 * p], row, x_up)
            recv(d_r1.at[2 + p], sd.at[0, 0], rx.at[2 + p])
            d_sum[2 + p] = (d_st[s_dn, PB:].astype(F32) + d_r1[2 + p].astype(F32)).astype(BF16)
            send(d_sum.at[2 + p], d_rc.at[2 + p, PB:], sl.at[2 + p], rd.at[4 + 2 * p + 1], row, x_dn)
        for p in range(2):
            s_up, s_dn = slot_of(x + 1, p == 1), slot_of(x + 3, p == 1)
            recv(block(s_dn, 0), sa.at[0], ra.at[2 * s_dn])
            send(block(s_dn, 0), block(s_dn, 0), sa.at[p], rh.at[2 * s_dn], row, x_up)
            recv(block(s_up, 1), sa.at[0], ra.at[2 * s_up + 1])
            send(block(s_up, 1), block(s_up, 1), sa.at[2 + p], rh.at[2 * s_up + 1], row, x_dn)
            recv(block(s_dn, 1), sa.at[0], ra.at[2 * s_dn + 1])
            weight_part(s_dn)
            recv(block(s_up, 0), sa.at[0], ra.at[2 * s_up])
            weight_part(s_up)

    def z_add(st, r1, r2, hs, ss, rs):
        recv(r1.at[0, :, hs], ss(0), rs(0))
        a, b = lower(2), upper(1)
        st[a, hs] = (st[a, hs].astype(F32) + r1[0, :, hs].astype(F32)).astype(BF16)
        send(st.at[rows(2, TB), hs], r2.at[0, :, hs], ss(2), rs(2), up, col)
        recv(r1.at[1, :, hs], ss(1), rs(1))
        st[b, hs] = (st[b, hs].astype(F32) + r1[1, :, hs].astype(F32)).astype(BF16)
        send(st.at[rows(1, TB), hs], r2.at[1, :, hs], ss(3), rs(3), dn, col)

    def z_sum(st, r2, hs, ss, rs):
        recv(r2.at[0, :, hs], ss(2), rs(2))
        recv(r2.at[1, :, hs], ss(3), rs(3))
        return (
            st[rows(0, TB), hs].astype(F32) + r2[0, :, hs].astype(F32) + r2[1, :, hs].astype(F32)
        ).astype(BF16)

    def z_left(st, r1, r2, hs, ss, rs):
        for j in range(2):
            left(r1.at[0, :, hs], ss(j), rs(j))
            left(r2.at[0, :, hs], ss(2 + j), rs(2 + j))

    @pl.when(inner)
    def _():
        for p in range(2):
            b = slot_of(x + 2, p == 1)
            for i in range(2):
                recv(block(b, i), sa.at[0], rh.at[2 * b + i])
            weight_part(b)

    @pl.when(outer)
    def _():
        recv(do_all.at[half, :], sb.at[2], rb.at[2])
        send(do_all.at[half, :], do_all.at[half, :], sb.at[3], rb.at[3], core, col)
        recv(dp_all.at[co], sb.at[4], rb.at[4])
        send(dp_all.at[co], dp_all.at[co], sb.at[5], rb.at[5], core, col)

    def mixed_part(i, carry):
        m_st[rows(i, QT), :] = dot(attn_all[:, rows(i, QT)], w_all[...], 0, 0).astype(BF16)
        return carry

    lax.fori_loop(0, 3, mixed_part, 0)
    to_y(5, 3, m_st.at[rows(ypeer(3), TB), :], m_core.at[1])
    to_y(5, 1, m_st.at[rows(ypeer(1), TB), :], m_core.at[0])

    recv(do_all.at[rows(1 - co, TB), :], sb.at[3], rb.at[3])
    recv(dp_all.at[1 - co], sb.at[5], rb.at[5])
    delta[...] = dp_all[0] + dp_all[1]
    from_y(5, 3, m_core.at[1])
    m_up[...] = (m_st[part_far, :].astype(F32) + m_core[1].astype(F32)).astype(BF16)
    to_y(5, 2, m_up, m_rc)

    def k_sems(sem, i, h):
        return lambda j: sem.at[i, h, j]

    def head_next(h):
        hs = rows(h, HD)
        recv(q_core.at[1, :, hs], sq.at[h, 2], rq.at[h, 2])
        q_up[:, hs] = (q_st[part_far, hs].astype(F32) + q_core[1, :, hs].astype(F32)).astype(BF16)
        send(q_up.at[:, hs], q_rc.at[:, hs], sq.at[h, 1], rq.at[h, 1], far, col)
        z_add(v_st, v_r1, v_r2, hs, k_sems(sk, 0, h), k_sems(rk, 0, h))
        z_add(k_st, k_r1, k_r2, hs, k_sems(sk, 1, h), k_sems(rk, 1, h))

    def backward(h, carry):
        hs = rows(h, HD)
        kh = k_all[:, hs]
        vh = v_all[:, hs]
        for t in range(3):
            ts = slice(t * QT, (t + 1) * QT)
            qh = q_all[ts, hs]
            doh = do_all[hs, ts]
            p = p_all[rows(h, ZT), ts]
            dprob = dot(vh, doh, 1, 0)
            ds = (p.astype(F32) * (dprob - delta[pl.ds(h, 1), ts]) * SCALE).astype(BF16)
            dvt = dot(p, doh, 1, 1)
            dkt = dot(ds, qh, 1, 0)
            if t == 0:
                vacc[...] = dvt
                kacc[...] = dkt
            else:
                vacc[...] += dvt
                kacc[...] += dkt
            q_st[ts, hs] = dot(kt[hs, :], ds, 1, 0).T.astype(BF16)
        v_st[:, hs] = vacc[...].astype(BF16)
        k_st[:, hs] = kacc[...].astype(BF16)
        for i, (st, r1) in enumerate(((v_st, v_r1), (k_st, k_r1))):
            send(st.at[lower(3), hs], r1.at[0, :, hs], sk.at[i, h, 0], rk.at[i, h, 0], up, col)
            send(st.at[upper(3), hs], r1.at[1, :, hs], sk.at[i, h, 1], rk.at[i, h, 1], dn, col)
        send(q_st.at[rows(ypeer(3), TB), hs], q_core.at[1, :, hs], sq.at[h, 2], rq.at[h, 2], core, col)
        send(q_st.at[rows(ypeer(1), TB), hs], q_core.at[0, :, hs], sq.at[h, 0], rq.at[h, 0], core, col)

        @pl.when(h > 0)
        def _():
            head_next(h - 1)

        return carry

    lax.fori_loop(0, NH, backward, 0)
    head_next(NH - 1)

    from_y(5, 1, m_core.at[0])
    from_y(5, 2, m_rc)
    mixed_o[...] = (m_st[rows(q, TB), :].astype(F32) + m_core[0].astype(F32) + m_rc[...].astype(F32)).astype(BF16)
    total = w_st[rows(z, TB), :].astype(F32)
    for d in (1, 3, 2):
        src = (z + d) % 4
        recv(w_rc.at[src], sw.at[0], rw.at[src])
        total += w_rc[src].astype(F32)
    wg_o[...] = total.astype(BF16)
    for h in range(NH):
        hs = slice(h * HD, (h + 1) * HD)
        recv(q_core.at[0, :, hs], sq.at[h, 0], rq.at[h, 0])
        recv(q_rc.at[:, hs], sq.at[h, 1], rq.at[h, 1])
        dq_o[:, hs] = (
            q_st[rows(q, TB), hs].astype(F32) + q_core[0, :, hs].astype(F32) + q_rc[:, hs].astype(F32)
        ).astype(BF16)
        dv_o[:, hs] = z_sum(v_st, v_r2, hs, k_sems(sk, 0, h), k_sems(rk, 0, h))
        dk_o[:, hs] = z_sum(k_st, k_r2, hs, k_sems(sk, 1, h), k_sems(rk, 1, h))

    for d in sends:
        d.wait_send()
    left(do_all.at[half, :], sb.at[3], rb.at[3])
    left(dp_all.at[0], sb.at[5], rb.at[5])

    @pl.when(inner)
    def _():
        for n, zp in enumerate((z, z_dn, z_up, z_op)):
            @pl.when(2 * (zp % 2) + yh != x)
            def _():
                left(d_st.at[0, :PB], sd.at[n, 0], rx.at[0])
                left(d_st.at[0, :PB], sd.at[n, 1], rx.at[0])

        for i in range(10):
            left(block(0, 0), sa.at[i], ra.at[0])
        left(d_up, sb.at[0], rb.at[0])
        left(do_all.at[half, :], sb.at[2], rb.at[2])
        left(dp_all.at[0], sb.at[4], rb.at[4])

    @pl.when(outer)
    def _():
        for n in range(4):
            left(d_st.at[0, :PB], sd.at[n, 0], rx.at[0])
            left(d_sum.at[n], sl.at[n], rx.at[0])
            left(block(0, 0), sa.at[n], ra.at[0])
        left(o_chip, sb.at[1], rb.at[1])

    for b in range(4):
        @pl.when(z != b)
        def _():
            left(w_rc.at[0], sw.at[b], rw.at[0])

    for h in range(NH):
        hs = slice(h * HD, (h + 1) * HD)
        for j in range(3):
            left(q_rc.at[:, hs], sq.at[h, j], rq.at[h, j])
        z_left(v_st, v_r1, v_r2, hs, k_sems(sk, 0, h), k_sems(rk, 0, h))
        z_left(k_st, k_r1, k_r2, hs, k_sems(sk, 1, h), k_sems(rk, 1, h))


def results(*refs):
    for src, dst in zip(refs[:5], refs[5:]):
        dst[...] = src[...]


def per_device(queries, keys_tile, values_tile, out_weight, out_grad):
    def vm(shape, dtype=BF16):
        return pltpu.VMEM(shape, dtype)

    dma = pltpu.SemaphoreType.DMA
    spec = pl.BlockSpec(memory_space=pltpu.VMEM)
    shapes = (
        jax.ShapeDtypeStruct((TB, DC), BF16),
        jax.ShapeDtypeStruct((TB, HC), BF16),
        jax.ShapeDtypeStruct((TB, HC), BF16),
        jax.ShapeDtypeStruct((TB, HC), BF16),
        jax.ShapeDtypeStruct((TB, DC), BF16),
    )
    outs = pl.pallas_call(
        kernel,
        out_shape=shapes,
        in_specs=[pl.BlockSpec(memory_space=pl.ANY)] * 5,
        out_specs=(spec,) * 5,
        scratch_shapes=[
            vm((ZT, HC)), vm((ZT, HC)), vm((ZT, HC)), vm((ZT, DC)), vm((ZT, DC)), vm((HC, ZT)), vm((HC, ZT), F32),
            vm((HC, ZT)), vm((TB, ZT)), vm((TB, ZT)), vm((TB, ZT)),
            *[vm((8, ZT), F32) for _ in range(9)],
            vm((ZT, ZT)), vm((4, TB, ZT)), vm((4, PB, ZT)), vm((4, PB, ZT)), vm((4, TB, ZT)), vm((TB, ZT)),
            vm((TB, ZT)), vm((HC, ZT)), vm((2, 8, ZT), F32), vm((8, ZT), F32),
            vm((ZT, HD), F32), vm((ZT, HD), F32), vm((ZT, HC)), vm((ZT, HC)), vm((ZT, HC)),
            vm((2, PB, HC)), vm((2, PB, HC)), vm((2, TB, HC)), vm((2, TB, HC)),
            vm((2, TB, HC)), vm((TB, HC)), vm((TB, HC)),
            vm((ZT, DC)), vm((2, TB, DC)), vm((TB, DC)), vm((TB, DC)),
            vm((ZT, DC)), vm((4, TB, DC)),
            dma((6, 4)), dma((6, 4)), dma((6, 3)), dma((6, 3)), dma((4, 2)), dma((4,)), dma((4,)), dma((8,)),
            dma((10,)), dma((8,)), dma((8,)), dma((6,)), dma((6,)), dma((2, 3, 4)), dma((2, 3, 4)),
            dma((3, 3)), dma((3, 3)), dma((4,)), dma((4,)), dma((5,)), vm((NH * ZT, ZT)),
        ],
        compiler_params=pltpu.CompilerParams(
            collective_id=0, has_side_effects=True, vmem_limit_bytes=60 * 1024 * 1024
        ),
    )(queries, keys_tile, values_tile, out_weight, out_grad)
    return pl.pallas_call(results, out_shape=shapes, in_specs=[spec] * 5, out_specs=(spec,) * 5)(*outs)


def solution(mesh):
    spec = P("row", "col")
    return jax.shard_map(
        per_device, mesh=mesh, in_specs=(spec,) * 5, out_specs=(spec,) * 5, check_vma=False
    )
```
